128 devices in a mesh: grp: 8 (over x, y_hi), blk: 16 (over y_lo, z, core).
Axes of the slice: x: 4, y: 4 (y_hi: 2, y_lo: 2; y = y_hi * 2 + y_lo), z: 4, core: 2. Of those that a mesh axis runs over, the one named last changes fastest.
Arguments:
- integrals: float32 [96, 1024, 1536], P('grp', 'blk'), may hold values from -0.9 to 0.9
- pair_lists: int32 [8, 2], P('grp'), may hold values from 0 to 96, as said below
- row_orbital: int32 [96], P('grp'), may hold values from 0 to 95, each once
- occ_energy: float32 [96], replicated, may hold values from -2 to -0.5
- vir_energy: float32 [1024], P('blk'), may hold values from 0.5 to 4
Outputs:
- three_index_density: float32 [96, 1024, 1536], P('grp', 'blk')
The draws below stay inside these ranges and needn't reach their ends.
Inputs may be any that keep to these rules, and one draw needn't show every extreme that they name: `pair_lists`: entries are rows of the integrals, or 96 in unused slots; used slots come first; every group lists one to 2 rows, some group exactly one and some exactly 2; no two rows listed by one group are held by the same group (a group may list one of its own rows). `row_orbital`: each orbital stands in exactly one row.
All inputs are finite; a program needn't handle non-finite values.
Results may differ from the reference program's by a relative error of at most 0.0001.
Values sent between devices are 32-bit elements; how exact they have to be, the bound alone decides.
A program may use at most 128 MiB of HBM per device.

```python
import jax
import jax.numpy as jnp
from jax import lax

V = 1024
X = 1536
OCC_GRP = 12
MAXJ = 2
GROUPS = 8
O = 96


def draw_pair_lists(key, part):
    key_count, key_busy, key_owner, key_offset = jax.random.split(key, 4)
    counts = jax.random.randint(key_count, (GROUPS,), 1, MAXJ + 1)
    busiest = jax.random.randint(key_busy, (), 0, GROUPS)
    lightest = (busiest + 1) % GROUPS
    group_ids = jnp.arange(GROUPS)
    counts = jnp.where(group_ids == busiest, MAXJ, counts)
    counts = jnp.where(group_ids == lightest, 1, counts)
    owner_keys = jax.random.split(key_owner, GROUPS)
    owners = jax.vmap(lambda owner_key: jax.random.permutation(owner_key, GROUPS))(owner_keys)[:, :MAXJ]
    offsets = jax.random.randint(key_offset, (GROUPS, MAXJ), 0, OCC_GRP)
    listed = owners * OCC_GRP + offsets
    slot_grid = jnp.arange(MAXJ)[None, :]
    return jnp.where(slot_grid < counts[:, None], listed, O).astype(jnp.int32)


def level_of(key, dims, shards, smallest, high):
    def one(position, parts):
        draws = jax.random.uniform(jax.random.fold_in(jax.random.fold_in(key, 6), position), (parts,), jnp.float32, smallest / len(shards), high / len(shards))
        return jnp.repeat(jnp.exp(draws), dims[position] // parts).reshape((-1,) + (1,) * (len(dims) - position - 1))

    loudness = one(*shards[0])
    for cut in shards[1:]:
        loudness = loudness * one(*cut)
    return loudness


def normal_values(stream_key, dims, deviation, limit, shards=(), held_as=jnp.bfloat16):
    array = deviation * jax.random.normal(stream_key, dims, jnp.float32)
    if shards:
        array = array * level_of(stream_key, dims, shards, -0.22, 0.18)
    return jnp.clip(array, -limit, limit).astype(held_as)


def setup_inputs(seed: int = 0) -> dict:
    key_list = jax.random.split(jax.random.key(seed), 6)
    return {
        "integrals": normal_values(key_list[0], (O, V, X), 0.15, 0.9, ((0, 8), (1, 16)), jnp.float32),
        "pair_lists": draw_pair_lists(jax.random.fold_in(key_list[5], 71), 0),
        "row_orbital": jax.random.permutation(key_list[2], O).astype(jnp.int32),
        "occ_energy": jnp.clip(jax.random.uniform(key_list[3], (O,), jnp.float32, -2.0, -0.5), -2.0, -0.5),
        "vir_energy": jnp.clip(0.5 + 3.5 * jax.random.uniform(key_list[4], (V,), jnp.float32) ** level_of(key_list[4], (V,), ((0, 16),), -0.2, 0.2), 0.5, 4.0),
    }


def reference(integrals, pair_lists, row_orbital, occ_energy, vir_energy):
    highest = lax.Precision.HIGHEST
    density = jnp.zeros(integrals.shape, jnp.float32)
    row_energy = occ_energy[row_orbital]
    for group_index in range(GROUPS):
        first_row = group_index * OCC_GRP
        own_rows = integrals[first_row:first_row + OCC_GRP]
        own_energy = row_energy[first_row:first_row + OCC_GRP]
        for slot_index in range(MAXJ):
            target = pair_lists[group_index, slot_index]
            is_valid = (target < O).astype(jnp.float32)
            row_index = jnp.minimum(target, O - 1).astype(jnp.int32)
            partner = lax.dynamic_index_in_dim(integrals, row_index, 0, keepdims=False) * is_valid
            pair_block = jnp.einsum('iap,bp->iab', own_rows, partner, precision=highest)
            denominator = (own_energy[:, None, None] + row_energy[row_index]
                           - vir_energy[None, :, None] - vir_energy[None, None, :])
            amplitude = pair_block / denominator
            forward = jnp.einsum('iab,bp->iap', amplitude, partner, precision=highest)
            density = density.at[first_row:first_row + OCC_GRP].add(forward)
            returned = jnp.einsum('iab,iap->bp', amplitude, own_rows, precision=highest)
            current = lax.dynamic_index_in_dim(density, row_index, 0, keepdims=False)
            density = lax.dynamic_update_index_in_dim(density, current + returned * is_valid, row_index, 0)
    return density
```

```python
import jax
import jax.numpy as jnp
from jax import lax
from jax.experimental import pallas as pl
from jax.experimental.pallas import tpu as pltpu
from jax.sharding import PartitionSpec as P

MESH = pl.DeviceIdType.MESH
F32 = jnp.float32
BF16 = jnp.bfloat16
GROUPS = 8
BLOCKS = 16
OWN = 12
SLOTS = 2
WIDTH = 64
AUX = 1536
HELD = OWN * WIDTH
ALL = 2 * HELD
STACK = 2 * SLOTS * WIDTH
TILE = 256
CHUNKS = 2
PART = WIDTH // CHUNKS


def note_kernel(ints_ref, vir_ref, ints_out, vir_out, send_a, recv_a, send_b, recv_b, local):
    group = lax.axis_index("grp")
    block = lax.axis_index("blk")
    barrier = pltpu.get_barrier_semaphore()
    for step in range(1, GROUPS):
        pl.semaphore_signal(barrier, 1, device_id={"grp": lax.rem(group + step, GROUPS)}, device_id_type=MESH)
    for step in range(1, BLOCKS):
        pl.semaphore_signal(barrier, 1, device_id={"blk": lax.rem(block + step, BLOCKS)}, device_id_type=MESH)
    keep_a = pltpu.make_async_copy(ints_ref, ints_out.at[group], local.at[0])
    keep_b = pltpu.make_async_copy(vir_ref, vir_out.at[block], local.at[1])
    keep_a.start()
    keep_b.start()
    pl.semaphore_wait(barrier, GROUPS + BLOCKS - 2)

    def to_group(step, slot):
        return pltpu.make_async_remote_copy(
            ints_ref, ints_out.at[slot], send_a.at[step], recv_a.at[slot],
            device_id={"grp": lax.rem(group + step, GROUPS)}, device_id_type=MESH)

    def to_block(step, slot):
        return pltpu.make_async_remote_copy(
            vir_ref, vir_out.at[slot], send_b.at[step], recv_b.at[slot],
            device_id={"blk": lax.rem(block + step, BLOCKS)}, device_id_type=MESH)

    for step in range(1, GROUPS):
        to_group(step, group).start()
    for step in range(1, BLOCKS):
        to_block(step, block).start()
    keep_a.wait()
    keep_b.wait()
    for step in range(1, GROUPS):
        to_group(step, group).wait_send()
        to_group(step, lax.rem(group + step, GROUPS)).wait_recv()
    for step in range(1, BLOCKS):
        to_block(step, block).wait_send()
        to_block(step, lax.rem(block + step, BLOCKS)).wait_recv()


def exchange_notes(ints, vir):
    return pl.pallas_call(
        note_kernel,
        out_shape=(
            jax.ShapeDtypeStruct((GROUPS, 1, 128), jnp.int32),
            jax.ShapeDtypeStruct((BLOCKS, 1, 128), F32),
        ),
        in_specs=[pl.BlockSpec(memory_space=pltpu.VMEM)] * 2,
        out_specs=(pl.BlockSpec(memory_space=pltpu.VMEM),) * 2,
        scratch_shapes=[
            pltpu.SemaphoreType.DMA((GROUPS,)),
            pltpu.SemaphoreType.DMA((GROUPS,)),
            pltpu.SemaphoreType.DMA((BLOCKS,)),
            pltpu.SemaphoreType.DMA((BLOCKS,)),
            pltpu.SemaphoreType.DMA((2,)),
        ],
        compiler_params=pltpu.CompilerParams(collective_id=0, has_side_effects=True),
        name="notes",
    )(ints, vir)


def pick_kernel(_, rows_ref, out_ref):
    out_ref[...] = rows_ref[...]


def pick_rows(wanted, integrals):
    return pl.pallas_call(
        pick_kernel,
        out_shape=jax.ShapeDtypeStruct((GROUPS, WIDTH, AUX), F32),
        grid_spec=pltpu.PrefetchScalarGridSpec(
            num_scalar_prefetch=1,
            grid=(GROUPS,),
            in_specs=[pl.BlockSpec((1, WIDTH, AUX), lambda i, wanted: (wanted[i], 0, 0))],
            out_specs=pl.BlockSpec((1, WIDTH, AUX), lambda i, wanted: (i, 0, 0)),
        ),
        name="pick",
    )(wanted, integrals)


def split(values):
    high = values.astype(BF16)
    return high, (values - high.astype(F32)).astype(BF16)


def rows_of(slot, side, chunk=None):
    start = (slot * 2 + side) * WIDTH
    if chunk is None:
        return pl.ds(start, WIDTH)
    return pl.ds(start + chunk * PART, PART)


def main_kernel(
    sources, valid, picks, held_ref, outgoing, row_part, column_part,
    own_out, arrived,
    high, low, total, stack, travel, sums, landed, parts,
    side_send, side_land, home, other, got_a, got_b,
    swap_sem, fetch_send, fetch_recv, local_sem, side_a, side_b,
    hop_send, hop_recv, sum_send, sum_recv, back_a, back_b,
    out_send, out_recv, own_sem,
):
    group = lax.axis_index("grp")
    block = lax.axis_index("blk")
    core = lax.rem(block, 2)
    level = lax.rem(block // 2, 4)
    side = block // 8
    twin = {"blk": block + 1 - 2 * core}
    across = {"blk": lax.rem(block + 8, 16)}
    ring = (
        {"blk": side * 8 + lax.rem(level + 1, 4) * 2 + core},
        {"blk": side * 8 + lax.rem(level + 3, 4) * 2 + core},
    )
    got = (got_a, got_b)

    barrier = pltpu.get_barrier_semaphore()
    for peer in (twin, across, ring[0], ring[1]):
        pl.semaphore_signal(barrier, 1, device_id=peer, device_id_type=MESH)
    for step in range(1, GROUPS):
        pl.semaphore_signal(barrier, 1, device_id={"grp": lax.rem(group + step, GROUPS)}, device_id_type=MESH)

    keep = pltpu.make_async_copy(held_ref, total.at[pl.ds(0, HELD)], local_sem.at[CHUNKS])
    keep.start()
    keep_own = [
        pltpu.make_async_copy(outgoing.at[group, pl.ds(c * PART, PART)], got[c].at[group], local_sem.at[c])
        for c in range(CHUNKS)
    ]
    for copy in keep_own:
        copy.start()
    pl.semaphore_wait(barrier, GROUPS + 3)

    def remote(src, dst, send, recv, peer):
        return pltpu.make_async_remote_copy(src, dst, send, recv, device_id=peer, device_id_type=MESH)

    def fetch(step, c, slot):
        peer = lax.rem(group + step, GROUPS)
        return remote(outgoing.at[peer, pl.ds(c * PART, PART)], got[c].at[slot],
                      fetch_send.at[c, step], fetch_recv.at[c, slot], {"grp": peer})

    swap = remote(held_ref, total.at[pl.ds(HELD, HELD)], swap_sem.at[0], swap_sem.at[1], twin)
    for c in range(CHUNKS):
        for step in range(1, GROUPS):
            fetch(step, c, group).start()
        if c == 0:
            swap.start()

    def prepare(first):
        def tile(index, carry):
            rows = pl.ds(pl.multiple_of(first + index * 64, 64), 64)
            upper, lower = split(total[rows, :])
            high[rows, :] = upper
            low[rows, :] = lower
            total[rows, :] = jnp.zeros((64, AUX), F32)
            return carry
        lax.fori_loop(0, HELD // 64, tile, 0)

    keep.wait()
    prepare(0)

    def beside(slot, c):
        return remote(stack.at[0, rows_of(slot, 0, c)], stack.at[0, rows_of(slot, 1, c)],
                      side_a.at[slot, c], side_b.at[slot, c], across)

    def hop(step, slot, part, c):
        return remote(stack.at[step, rows_of(slot, part, c)], stack.at[step + 1, rows_of(slot, part, c)],
                      hop_send.at[step, slot, part, c], hop_recv.at[step, slot, part, c], ring[slot])

    for c in range(CHUNKS):
        keep_own[c].wait()
        for step in range(1, GROUPS):
            fetch(step, c, lax.rem(group + step, GROUPS)).wait_recv()
        for slot in range(SLOTS):
            stack[0, rows_of(slot, 0, c), :] = got[c][sources[slot]] * valid[slot]
        for slot in range(SLOTS):
            beside(slot, c).start()
            hop(0, slot, 0, c).start()
        if c == 0:
            swap.wait()
            prepare(HELD)
    for c in range(CHUNKS):
        for slot in range(SLOTS):
            beside(slot, c).wait_recv()
            hop(0, slot, 1, c).start()

    def sum_hop(step, slot, part, c):
        return remote(sums.at[step, rows_of(slot, part, c)], landed.at[step - 1, rows_of(slot, part, c)],
                      sum_send.at[step, slot, part, c], sum_recv.at[step, slot, part, c], ring[slot])

    pieces = [(slot, part, c) for part in (0, 1) for c in range(CHUNKS) for slot in range(SLOTS)]
    sum_pieces = [(slot, part, c) for part in (1, 0) for c in range(CHUNKS) for slot in range(SLOTS)]

    def stage(step, carry):
        @pl.when(step > 0)
        def _():
            for slot, part, c in pieces:
                hop(step - 1, slot, part, c).wait_recv()

                @pl.when(step < 3)
                def _():
                    hop(step, slot, part, c).start()

        def cut(index, carry):
            rows = pl.ds(pl.multiple_of(index * 64, 64), 64)
            upper, lower = split(stack[step, rows, :])
            travel[rows, :] = upper
            travel[pl.ds(pl.multiple_of(STACK + index * 64, 64), 64), :] = lower
            travel[pl.ds(pl.multiple_of(2 * STACK + index * 64, 64), 64), :] = upper
            sums[step, rows, :] = jnp.zeros((64, AUX), F32)
            return carry

        lax.fori_loop(0, STACK // 64, cut, 0)

        def tile(index, carry):
            rows = pl.ds(pl.multiple_of(index * TILE, TILE), TILE)
            nt = (((1,), (1,)), ((), ()))
            tn = (((0,), (0,)), ((), ()))
            upper = high[rows, :]
            lower = low[rows, :]
            near = travel[pl.ds(0, STACK), :]
            far = travel[pl.ds(STACK, STACK), :]
            pair = lax.dot_general(upper, near, nt, preferred_element_type=F32)
            pair += lax.dot_general(upper, far, nt, preferred_element_type=F32)
            pair += lax.dot_general(lower, near, nt, preferred_element_type=F32)
            amplitude = pair / (row_part[rows, :] + column_part[step])
            big, small = split(amplitude)
            total[rows, :] += jnp.dot(jnp.concatenate([big, big, small], axis=1), travel[...], preferred_element_type=F32)
            back = lax.dot_general(big, upper, tn, preferred_element_type=F32)
            back += lax.dot_general(big, lower, tn, preferred_element_type=F32)
            back += lax.dot_general(small, upper, tn, preferred_element_type=F32)
            sums[step] += back
            return carry

        lax.fori_loop(0, ALL // TILE, tile, 0)

        @pl.when(step > 0)
        def _():
            for slot, part, c in sum_pieces:
                @pl.when(step > 1)
                def _():
                    sum_hop(step - 1, slot, part, c).wait_recv()
                    rows = rows_of(slot, part, c)
                    sums[step, rows, :] += landed[step - 2, rows, :]
                sum_hop(step, slot, part, c).start()
        return carry

    lax.fori_loop(0, 4, stage, 0)

    give = remote(total.at[pl.ds(HELD, HELD)], other, own_sem.at[0], own_sem.at[1], twin)
    give.start()

    def cross(slot, c):
        rows = pl.ds(slot * WIDTH + c * PART, PART)
        return remote(side_send.at[rows], side_land.at[rows], back_a.at[slot, c], back_b.at[slot, c], across)

    for slot, part, c in sum_pieces:
        sum_hop(3, slot, part, c).wait_recv()
        rows = rows_of(slot, part, c)
        value = sums[0, rows, :] + landed[2, rows, :]
        if part == 1:
            side_send[pl.ds(slot * WIDTH + c * PART, PART), :] = value
            cross(slot, c).start()
        else:
            home[pl.ds(slot * WIDTH + c * PART, PART), :] = value

    def ship(step, c, slot):
        peer = lax.rem(group + step, GROUPS)
        return remote(got[c].at[peer], arrived.at[slot, pl.ds(c * PART, PART)],
                      out_send.at[c, step], out_recv.at[c, slot], {"grp": peer})

    stay = [
        pltpu.make_async_copy(got[c].at[group], arrived.at[group, pl.ds(c * PART, PART)], local_sem.at[c])
        for c in range(CHUNKS)
    ]
    for c in range(CHUNKS):
        ready = []
        for slot in range(SLOTS):
            cross(slot, c).wait_recv()
            rows = pl.ds(slot * WIDTH + c * PART, PART)
            home[rows, :] += side_land[rows, :]
        for step in range(1, GROUPS + 1):
            peer = lax.rem(group + step, GROUPS)
            got[c][peer] = (picks[0, peer] * home[pl.ds(c * PART, PART), :]
                            + picks[1, peer] * home[pl.ds(WIDTH + c * PART, PART), :])
            if step < GROUPS:
                ship(step, c, group).start()
        stay[c].start()

    give.wait()

    def merge(index, carry):
        rows = pl.ds(pl.multiple_of(index * 64, 64), 64)
        total[rows, :] += other[rows, :]
        return carry

    lax.fori_loop(0, HELD // 64, merge, 0)
    store = pltpu.make_async_copy(total.at[pl.ds(0, HELD)], own_out, local_sem.at[CHUNKS])
    store.start()
    for c in range(CHUNKS):
        for step in range(1, GROUPS):
            fetch(step, c, group).wait_send()
        for slot in range(SLOTS):
            beside(slot, c).wait_send()
            cross(slot, c).wait_send()
            for part in range(2):
                for step in range(3):
                    hop(step, slot, part, c).wait_send()
                    sum_hop(step + 1, slot, part, c).wait_send()
    for c in range(CHUNKS):
        stay[c].wait()
        for step in range(1, GROUPS):
            ship(step, c, group).wait_send()
            ship(step, c, lax.rem(group + step, GROUPS)).wait_recv()
    store.wait()


def run_main(sources, valid, picks, held, outgoing, row_part, column_part):
    smem = pl.BlockSpec(memory_space=pltpu.SMEM)
    vmem = pl.BlockSpec(memory_space=pltpu.VMEM)
    hbm = pl.BlockSpec(memory_space=pl.ANY)
    dma = pltpu.SemaphoreType.DMA
    return pl.pallas_call(
        main_kernel,
        out_shape=(
            jax.ShapeDtypeStruct((HELD, AUX), F32),
            jax.ShapeDtypeStruct((GROUPS, WIDTH, AUX), F32),
        ),
        in_specs=[smem, smem, smem, hbm, hbm, vmem, vmem],
        out_specs=(hbm, hbm),
        scratch_shapes=[
            pltpu.VMEM((ALL, AUX), BF16),
            pltpu.VMEM((ALL, AUX), BF16),
            pltpu.VMEM((ALL, AUX), F32),
            pltpu.VMEM((4, STACK, AUX), F32),
            pltpu.VMEM((3 * STACK, AUX), BF16),
            pltpu.VMEM((4, STACK, AUX), F32),
            pltpu.VMEM((3, STACK, AUX), F32),
            pltpu.VMEM((8, 128), F32),
            pltpu.VMEM((SLOTS * WIDTH, AUX), F32),
            pltpu.VMEM((SLOTS * WIDTH, AUX), F32),
            pltpu.VMEM((SLOTS * WIDTH, AUX), F32),
            pltpu.VMEM((HELD, AUX), F32),
            pltpu.VMEM((GROUPS, PART, AUX), F32),
            pltpu.VMEM((GROUPS, PART, AUX), F32),
            dma((2,)),
            dma((CHUNKS, GROUPS)),
            dma((CHUNKS, GROUPS)),
            dma((CHUNKS + 1,)),
            dma((SLOTS, CHUNKS)),
            dma((SLOTS, CHUNKS)),
            dma((4, SLOTS, 2, CHUNKS)),
            dma((4, SLOTS, 2, CHUNKS)),
            dma((4, SLOTS, 2, CHUNKS)),
            dma((4, SLOTS, 2, CHUNKS)),
            dma((SLOTS, CHUNKS)),
            dma((SLOTS, CHUNKS)),
            dma((CHUNKS, GROUPS)),
            dma((CHUNKS, GROUPS)),
            dma((2,)),
        ],
        compiler_params=pltpu.CompilerParams(
            collective_id=1, has_side_effects=True, vmem_limit_bytes=64_000_000),
        name="main",
    )(sources, valid, picks, held, outgoing, row_part, column_part)


def join_kernel(wanted, present, own_ref, arrived_ref, out_ref):
    out_ref[...] = own_ref[...]
    for peer in range(GROUPS):
        @pl.when(present[peer] > 0)
        def _():
            out_ref[wanted[peer]] += arrived_ref[peer]


def join(wanted, present, own, arrived):
    height = 16
    return pl.pallas_call(
        join_kernel,
        out_shape=jax.ShapeDtypeStruct((OWN, WIDTH, AUX), F32),
        grid_spec=pltpu.PrefetchScalarGridSpec(
            num_scalar_prefetch=2,
            grid=(WIDTH // height,),
            in_specs=[
                pl.BlockSpec((OWN, height, AUX), lambda i, *_: (0, i, 0)),
                pl.BlockSpec((GROUPS, height, AUX), lambda i, *_: (0, i, 0)),
            ],
            out_specs=pl.BlockSpec((OWN, height, AUX), lambda i, *_: (0, i, 0)),
        ),
        name="join",
    )(wanted, present, own, arrived)


def body(integrals, pair_lists, row_orbital, occ_energy, vir_energy):
    group = lax.axis_index("grp")
    block = lax.axis_index("blk")
    core = block % 2
    level = (block // 2) % 4
    side = block // 8
    ints = jnp.concatenate([pair_lists[0], row_orbital, jnp.zeros((128 - SLOTS - OWN,), jnp.int32)])[None]
    vir = jnp.concatenate([vir_energy, jnp.zeros((128 - WIDTH,), F32)])[None]
    ints_all, vir_all = exchange_notes(ints, vir)
    lists = ints_all[:, 0, :SLOTS]
    orbitals = ints_all[:, 0, SLOTS:SLOTS + OWN]
    vir_all = vir_all[:, 0, :WIDTH]
    owners = lists // OWN
    offsets = lists % OWN
    match = owners == group
    wanted = jnp.sum(jnp.where(match, offsets, 0), axis=1).astype(jnp.int32)
    present = jnp.any(match, axis=1).astype(jnp.int32)
    outgoing = pick_rows(wanted, integrals)

    mine = lax.dynamic_index_in_dim(lists, group, 0, keepdims=False)
    sources = jnp.minimum(mine // OWN, GROUPS - 1).astype(jnp.int32)
    valid = (mine < GROUPS * OWN).astype(F32)
    picks = (mine[:, None] // OWN == jnp.arange(GROUPS)[None, :]).astype(F32)
    ids = jnp.arange(occ_energy.shape[0])
    row_energy = jnp.sum(jnp.where(orbitals.reshape(-1)[:, None] == ids, occ_energy, 0.0), axis=1)
    own_energy = lax.dynamic_slice_in_dim(row_energy, group * OWN, OWN, 0)
    partner_energy = jnp.sum(jnp.where(mine[:, None] == ids, row_energy, 0.0), axis=1)
    pair_vir = lax.dynamic_slice_in_dim(vir_all, block - core, 2, 0)
    twin_vir = jnp.where(core == 0, pair_vir[1], pair_vir[0])
    row_part = jnp.concatenate([
        own_energy[:, None] - vir_energy[None, :],
        own_energy[:, None] - twin_vir[None, :],
    ]).reshape(ALL, 1)
    grid = jnp.where(core == 0, vir_all.reshape(2, 4, 2, WIDTH)[:, :, 0], vir_all.reshape(2, 4, 2, WIDTH)[:, :, 1])
    grid = jnp.where(side == 0, grid, grid[::-1])
    up = jnp.stack([lax.dynamic_index_in_dim(grid, (level + 4 - k) % 4, 1, keepdims=False) for k in range(4)])
    down = jnp.stack([lax.dynamic_index_in_dim(grid, (level + k) % 4, 1, keepdims=False) for k in range(4)])
    column_part = jnp.stack([partner_energy[0] - up, partner_energy[1] - down], axis=1).reshape(4, 1, STACK)

    own, arrived = run_main(
        sources, valid, picks, integrals.reshape(HELD, AUX), outgoing, row_part, column_part)
    return join(wanted, present, own.reshape(OWN, WIDTH, AUX), arrived)


def solution(mesh):
    in_specs = (P("grp", "blk", None), P("grp", None), P("grp"), P(), P("blk"))
    out_specs = P("grp", "blk", None)
    return jax.shard_map(body, mesh=mesh, in_specs=in_specs, out_specs=out_specs, check_vma=False)
```

```python
import jax
import jax.numpy as jnp
from jax import lax
from jax.experimental import pallas as pl
from jax.experimental.pallas import tpu as pltpu
from jax.sharding import PartitionSpec as P

MESH = pl.DeviceIdType.MESH
F32 = jnp.float32
BF16 = jnp.bfloat16
GROUPS = 8
BLOCKS = 16
OWN = 12
SLOTS = 2
WIDTH = 64
AUX = 1536
HELD = OWN * WIDTH
ALL = 2 * HELD
CHUNKS = 4
PART = WIDTH // CHUNKS
HALF = WIDTH // 2
STEP_ROWS = 2 * SLOTS * HALF
STACK = 2 * STEP_ROWS
TILE = 512
TILES = ALL // TILE
LANES = 128
NT = (((1,), (1,)), ((), ()))
TN = (((0,), (0,)), ((), ()))
CALL_OF = {(0, 0): (0, 0), (0, 1): (0, 1), (0, 2): (1, 0), (0, 3): (1, 1),
           (1, 1): (2, 0), (1, 2): (2, 1), (1, 3): (3, 0), (1, 0): (3, 1)}


def split(values):
    high = values.astype(BF16)
    return high, (values - high.astype(F32)).astype(BF16)


def step_rows(slot, part, c):
    return pl.ds((slot * 2 + part) * HALF + (c % 2) * PART, PART)


def sum_place(step, slot, part, c):
    call, half = CALL_OF[(c // 2, step)]
    return call, pl.ds(half * STEP_ROWS + (slot * 2 + part) * HALF + (c % 2) * PART, PART)


def main_kernel(
    lists_ref, orbitals_ref, occ_ref, vir_ref, held_ref,
    own_out, arrived, flags,
    ints_mine, ints_all, vir_mine, vir_all, ints,
    high, low, total, stack, travel, amp, sums, landed,
    side_send, side_land, home, other, row_part, column_part,
    got_0, got_1, got_2, got_3, box_0, box_1, box_2, box_3,
    note_a, note_b, note_c, note_d, local_sem, swap_sem,
    fetch_send, fetch_recv, side_a, side_b,
    hop_send, hop_recv, sum_send, sum_recv, back_a, back_b,
    out_send, out_recv, own_sem,
):
    group = lax.axis_index("grp")
    block = lax.axis_index("blk")
    core = lax.rem(block, 2)
    level = lax.rem(block // 2, 4)
    side = block // 8
    twin_block = block + 1 - 2 * core
    twin = {"blk": twin_block}
    across = {"blk": lax.rem(block + 8, 16)}
    ring = (
        {"blk": side * 8 + lax.rem(level + 1, 4) * 2 + core},
        {"blk": side * 8 + lax.rem(level + 3, 4) * 2 + core},
    )
    got = (got_0, got_1, got_2, got_3)
    box = (box_0, box_1, box_2, box_3)

    barrier = pltpu.get_barrier_semaphore()
    for step in range(1, GROUPS):
        pl.semaphore_signal(barrier, 1, device_id={"grp": lax.rem(group + step, GROUPS)}, device_id_type=MESH)
    for step in range(1, BLOCKS):
        pl.semaphore_signal(barrier, 1, device_id={"blk": lax.rem(block + step, BLOCKS)}, device_id_type=MESH)

    keep = pltpu.make_async_copy(held_ref, other, local_sem.at[0])
    keep.start()
    lane = lax.broadcasted_iota(jnp.int32, (1, LANES), 1)
    row = jnp.zeros((1, LANES), jnp.int32)
    for j in range(SLOTS):
        row = jnp.where(lane == j, lists_ref[0, j], row)
    for j in range(OWN):
        row = jnp.where(lane == SLOTS + j, orbitals_ref[j], row)
    ints_mine[...] = row
    ints_all[group] = row
    vir = vir_ref[...]
    vir_row = jnp.concatenate([vir[:, :HALF]] * 8 + [vir[:, HALF:]] * 8, axis=1)
    vir_mine[...] = vir_row
    vir_all[block] = vir_row
    pl.semaphore_wait(barrier, GROUPS + BLOCKS - 2)

    def remote(src, dst, send, recv, peer):
        return pltpu.make_async_remote_copy(src, dst, send, recv, device_id=peer, device_id_type=MESH)

    def to_group(step, slot):
        return remote(ints_mine, ints_all.at[slot], note_a.at[step], note_b.at[slot],
                      {"grp": lax.rem(group + step, GROUPS)})

    def to_block(step, slot):
        return remote(vir_mine, vir_all.at[slot], note_c.at[step], note_d.at[slot],
                      {"blk": lax.rem(block + step, BLOCKS)})

    for step in range(1, GROUPS):
        to_group(step, group).start()
    for step in range(1, BLOCKS):
        to_block(step, block).start()
    keep.wait()
    for step in range(1, GROUPS):
        to_group(step, lax.rem(group + step, GROUPS)).wait_recv()
    to_scalar = pltpu.make_async_copy(ints_all, ints, local_sem.at[1])
    to_scalar.start()
    to_scalar.wait()

    wanted = []
    for peer in range(GROUPS):
        place = jnp.int32(0)
        found = jnp.int32(0)
        for slot in range(SLOTS):
            listed = ints[peer, 0, slot]
            match = listed // OWN == group
            place = jnp.where(match, listed % OWN, place)
            found = jnp.where(match, 1, found)
        flags[0, peer] = place
        flags[1, peer] = found

    def fetch(step, c, slot):
        peer = lax.rem(group + step, GROUPS)
        return remote(box[c].at[step], got[c].at[slot],
                      fetch_send.at[c, step], fetch_recv.at[c, slot], {"grp": peer})

    def fill(c):
        for step in range(GROUPS):
            peer = lax.rem(group + step, GROUPS)
            values = other[flags[0, peer], pl.ds(c * PART, PART), :]
            if step == 0:
                got[c][group] = values
            else:
                box[c][step] = values

    fill(0)
    for c in range(CHUNKS):
        if c + 1 < CHUNKS:
            fill(c + 1)
        for step in range(1, GROUPS):
            fetch(step, c, group).start()

    swap = remote(held_ref, total.at[pl.ds(OWN, OWN)], swap_sem.at[0], swap_sem.at[1], twin)

    def prepare(source, first):
        def tile(index, carry):
            rows = pl.ds(pl.multiple_of((first + index) * WIDTH, WIDTH), WIDTH)
            upper, lower = split(source[index + (first if source is total else 0)])
            high[rows, :] = upper
            low[rows, :] = lower
            total[first + index] = jnp.zeros((WIDTH, AUX), F32)
            return carry
        lax.fori_loop(0, OWN, tile, 0)

    prepare(other, 0)
    swap.start()

    mine = [ints[group, 0, slot] for slot in range(SLOTS)]
    sources = [jnp.minimum(row // OWN, GROUPS - 1) for row in mine]
    valid = [jnp.where(row < GROUPS * OWN, jnp.float32(1), jnp.float32(0)) for row in mine]
    partner_energy = [
        occ_ref[ints[sources[slot], 0, SLOTS + mine[slot] % OWN]] for slot in range(SLOTS)
    ]
    for step in range(1, BLOCKS):
        to_block(step, lax.rem(block + step, BLOCKS)).wait_recv()
    square = (lax.broadcasted_iota(jnp.int32, (HALF, HALF), 0)
              == lax.broadcasted_iota(jnp.int32, (HALF, HALF), 1))
    for owner, place in ((block, 0), (twin_block, 1)):
        for h in range(2):
            line = vir_all[owner, :, pl.ds(h * STACK, LANES)][:, :HALF]
            column = jnp.sum(jnp.where(square, line, 0.0), axis=1, keepdims=True)
            for i in range(OWN):
                energy = occ_ref[ints[group, 0, SLOTS + i]]
                row_part[pl.ds((place * OWN + i) * WIDTH + h * HALF, HALF), :] = energy - column
    piece = lax.broadcasted_iota(jnp.int32, (1, STACK), 1) // HALF
    for at_call in range(4):
        terms = jnp.zeros((1, STACK), F32)
        for (h, step), (call, half) in CALL_OF.items():
            if call != at_call:
                continue
            for slot in range(SLOTS):
                for part in range(2):
                    from_level = lax.rem(level + (4 - step if slot == 0 else step), 4)
                    from_side = side + part - 2 * part * side
                    line = vir_all[from_side * 8 + from_level * 2 + core, :, pl.ds(h * STACK, STACK)]
                    here = piece == half * 4 + slot * 2 + part
                    terms = jnp.where(here, partner_energy[slot] - line, terms)
        column_part[at_call] = terms

    def beside(slot, c):
        return remote(stack.at[c // 2, 0, step_rows(slot, 0, c)], stack.at[c // 2, 0, step_rows(slot, 1, c)],
                      side_a.at[slot, c], side_b.at[slot, c], across)

    def hop(step, slot, part, c):
        rows = step_rows(slot, part, c)
        return remote(stack.at[c // 2, step, rows], stack.at[c // 2, step + 1, rows],
                      hop_send.at[step, slot, part, c], hop_recv.at[step, slot, part, c], ring[slot])

    def sum_hop(step, slot, part, c):
        call, rows = sum_place(step, slot, part, c)
        return remote(sums.at[call, rows], landed.at[c // 2, step - 1, step_rows(slot, part, c)],
                      sum_send.at[step - 1, slot, part, c], sum_recv.at[step - 1, slot, part, c], ring[slot])

    def home_rows(slot, c):
        return pl.ds(slot * WIDTH + c * PART, PART)

    def cross(slot, c):
        rows = home_rows(slot, c)
        return remote(side_send.at[rows], side_land.at[rows], back_a.at[slot, c], back_b.at[slot, c], across)

    def ship(step, c, slot):
        return remote(box[c].at[step], arrived.at[slot, pl.ds(c * PART, PART)],
                      out_send.at[c, step], out_recv.at[c, slot], {"grp": lax.rem(group + step, GROUPS)})

    def stay(c):
        return pltpu.make_async_copy(box[c].at[0], arrived.at[group, pl.ds(c * PART, PART)], local_sem.at[2 + c])

    def on_fetch(c):
        for step in range(1, GROUPS):
            fetch(step, c, lax.rem(group + step, GROUPS)).wait_recv()
        for slot in range(SLOTS):
            stack[c // 2, 0, step_rows(slot, 0, c), :] = got[c][sources[slot]] * valid[slot]
        for slot in range(SLOTS):
            beside(slot, c).start()
            hop(0, slot, 0, c).start()

    def on_side(c):
        for slot in range(SLOTS):
            beside(slot, c).wait_recv()
            hop(0, slot, 1, c).start()

    def on_hop(step, part, c):
        for slot in range(SLOTS):
            hop(step - 1, slot, part, c).wait_recv()
            if step < 3:
                hop(step, slot, part, c).start()

    def on_sum(step, c):
        for part in (1, 0):
            for slot in range(SLOTS):
                if step > 1:
                    sum_hop(step - 1, slot, part, c).wait_recv()
                    call, rows = sum_place(step, slot, part, c)
                    sums[call, rows, :] += landed[c // 2, step - 2, step_rows(slot, part, c), :]
        for part in (1, 0):
            for slot in range(SLOTS):
                sum_hop(step, slot, part, c).start()

    def on_home(c):
        for part in (1, 0):
            for slot in range(SLOTS):
                sum_hop(3, slot, part, c).wait_recv()
                call, rows = sum_place(0, slot, part, c)
                value = sums[call, rows, :] + landed[c // 2, 2, step_rows(slot, part, c), :]
                (side_send if part else home)[home_rows(slot, c), :] = value
            if part:
                for slot in range(SLOTS):
                    cross(slot, c).start()

    def on_cross(c):
        for step in range(1, GROUPS):
            fetch(step, c, group).wait_send()
        for slot in range(SLOTS):
            cross(slot, c).wait_recv()
            home[home_rows(slot, c), :] += side_land[home_rows(slot, c), :]
        for step in range(GROUPS):
            peer = lax.rem(group + step, GROUPS)
            picks = [jnp.where(row // OWN == peer, jnp.float32(1), jnp.float32(0)) for row in mine]
            box[c][step] = picks[0] * home[home_rows(0, c), :] + picks[1] * home[home_rows(1, c), :]
        for step in range(1, GROUPS):
            ship(step, c, group).start()
        stay(c).start()

    on_fetch(0)
    swap.wait()
    prepare(total, OWN)
    on_side(0)
    on_hop(1, 0, 0)
    on_hop(1, 1, 0)
    on_hop(2, 0, 0)
    on_fetch(1)
    on_side(1)
    on_hop(2, 1, 0)
    on_hop(1, 0, 1)
    on_hop(1, 1, 1)

    open_events = {
        1: [lambda: on_sum(1, 0), lambda: on_sum(1, 1), lambda: on_hop(2, 0, 2),
            lambda: on_hop(3, 0, 0), lambda: on_hop(3, 1, 0), lambda: on_hop(3, 0, 1), lambda: on_hop(3, 1, 1)],
        2: [lambda: on_hop(2, 1, 3), lambda: on_sum(2, 0), lambda: on_sum(2, 1)],
        3: [lambda: on_sum(1, 2), lambda: on_sum(1, 3),
            lambda: on_hop(3, 0, 2), lambda: on_hop(3, 1, 2), lambda: on_hop(3, 0, 3), lambda: on_hop(3, 1, 3),
            lambda: on_home(0)],
    }
    pair_events = {
        (0, 2): [lambda: on_fetch(2), lambda: on_hop(2, 0, 1)],
        (1, 2): [lambda: on_fetch(3), lambda: on_hop(2, 1, 2)],
        (3, 2): [lambda: on_home(1), lambda: on_sum(2, 2)],
    }
    back_events = {
        (0, 0): [lambda: on_side(2), lambda: on_hop(2, 1, 1), lambda: on_hop(1, 0, 2)],
        (0, 1): [lambda: on_hop(1, 1, 2)],
        (1, 0): [lambda: on_side(3), lambda: on_hop(1, 0, 3)],
        (1, 1): [lambda: on_hop(1, 1, 3), lambda: on_hop(2, 0, 3)],
        (2, 0): [lambda: on_sum(3, 0)],
        (2, 1): [lambda: on_sum(3, 1)],
        (3, 0): [lambda: on_cross(0)],
        (3, 1): [lambda: on_cross(1), lambda: on_sum(2, 3)],
    }

    def run(events, call, index):
        for (at_call, at_index), actions in events.items():
            @pl.when((call == at_call) & (index == at_index))
            def _():
                for action in actions:
                    action()

    def one_call(call, carry):
        for at_call, actions in open_events.items():
            @pl.when(call == at_call)
            def _():
                for action in actions:
                    action()

        h = call // 2
        first = (call % 2) * 2 + h
        second = (first + 1) % 4

        def cut(index, carry):
            for half, step in ((0, first), (1, second)):
                upper, lower = split(stack[h, step, pl.ds(pl.multiple_of(index * 64, 64), 64), :])
                start = half * STEP_ROWS + index * 64
                travel[pl.ds(pl.multiple_of(start, 64), 64), :] = upper
                travel[pl.ds(pl.multiple_of(STACK + start, 64), 64), :] = lower
                travel[pl.ds(pl.multiple_of(2 * STACK + start, 64), 64), :] = upper
                sums[call, pl.ds(pl.multiple_of(start, 64), 64), :] = jnp.zeros((64, AUX), F32)
            return carry

        lax.fori_loop(0, STEP_ROWS // 64, cut, 0)

        def pair_tile(index, carry):
            rows = pl.ds(pl.multiple_of(index * TILE, TILE), TILE)
            upper = high[rows, :]
            near = travel[pl.ds(0, STACK), :]
            pair = lax.dot_general(upper, near, NT, preferred_element_type=F32)
            pair += lax.dot_general(upper, travel[pl.ds(STACK, STACK), :], NT, preferred_element_type=F32)
            pair += lax.dot_general(low[rows, :], near, NT, preferred_element_type=F32)
            big, small = split(pair / (row_part[rows, :] + column_part[call]))
            amp[rows, pl.ds(0, STACK)] = big
            amp[rows, pl.ds(STACK, STACK)] = big
            amp[rows, pl.ds(2 * STACK, STACK)] = small
            run(pair_events, call, index)
            return carry

        lax.fori_loop(0, TILES, pair_tile, 0)

        def back_tile(index, carry):
            rows = pl.ds(pl.multiple_of(index * TILE, TILE), TILE)
            held = pl.ds(index * (TILE // WIDTH), TILE // WIDTH)
            forward = jnp.dot(amp[rows, :], travel[...], preferred_element_type=F32)
            total[held] += forward.reshape(TILE // WIDTH, WIDTH, AUX)
            upper = high[rows, :]
            big = amp[rows, pl.ds(0, STACK)]
            back = lax.dot_general(big, upper, TN, preferred_element_type=F32)
            back += lax.dot_general(big, low[rows, :], TN, preferred_element_type=F32)
            back += lax.dot_general(amp[rows, pl.ds(2 * STACK, STACK)], upper, TN, preferred_element_type=F32)
            sums[call] += back
            run(back_events, call, index)
            return carry

        lax.fori_loop(0, TILES, back_tile, 0)
        return carry

    lax.fori_loop(0, 4, one_call, 0)

    give = remote(total.at[pl.ds(OWN, OWN)], other, own_sem.at[0], own_sem.at[1], twin)
    on_sum(3, 2)
    give.start()
    on_home(2)
    on_sum(3, 3)
    on_cross(2)
    on_home(3)
    on_cross(3)
    give.wait()

    def merge(index, carry):
        total[index] += other[index]
        return carry

    lax.fori_loop(0, OWN, merge, 0)
    store = pltpu.make_async_copy(total.at[pl.ds(0, OWN)], own_out, local_sem.at[0])
    store.start()
    for step in range(1, GROUPS):
        to_group(step, group).wait_send()
    for step in range(1, BLOCKS):
        to_block(step, block).wait_send()
    for c in range(CHUNKS):
        for slot in range(SLOTS):
            beside(slot, c).wait_send()
            cross(slot, c).wait_send()
            for part in range(2):
                for step in range(3):
                    hop(step, slot, part, c).wait_send()
                    sum_hop(step + 1, slot, part, c).wait_send()
    for c in range(CHUNKS):
        stay(c).wait()
        for step in range(1, GROUPS):
            ship(step, c, group).wait_send()
            ship(step, c, lax.rem(group + step, GROUPS)).wait_recv()
    store.wait()


def run_main(lists, orbitals, occ, vir, held):
    smem = pl.BlockSpec(memory_space=pltpu.SMEM)
    vmem = pl.BlockSpec(memory_space=pltpu.VMEM)
    hbm = pl.BlockSpec(memory_space=pl.ANY)
    dma = pltpu.SemaphoreType.DMA
    chunk = pltpu.VMEM((GROUPS, PART, AUX), F32)
    return pl.pallas_call(
        main_kernel,
        out_shape=(
            jax.ShapeDtypeStruct((OWN, WIDTH, AUX), F32),
            jax.ShapeDtypeStruct((GROUPS, WIDTH, AUX), F32),
            jax.ShapeDtypeStruct((2, GROUPS), jnp.int32),
        ),
        in_specs=[smem, smem, smem, vmem, hbm],
        out_specs=(hbm, hbm, smem),
        scratch_shapes=[
            pltpu.VMEM((1, LANES), jnp.int32),
            pltpu.VMEM((GROUPS, 1, LANES), jnp.int32),
            pltpu.VMEM((1, 2 * STACK), F32),
            pltpu.VMEM((BLOCKS, 1, 2 * STACK), F32),
            pltpu.SMEM((GROUPS, 1, LANES), jnp.int32),
            pltpu.VMEM((ALL, AUX), BF16),
            pltpu.VMEM((ALL, AUX), BF16),
            pltpu.VMEM((2 * OWN, WIDTH, AUX), F32),
            pltpu.VMEM((2, 4, STEP_ROWS, AUX), F32),
            pltpu.VMEM((3 * STACK, AUX), BF16),
            pltpu.VMEM((ALL, 3 * STACK), BF16),
            pltpu.VMEM((4, STACK, AUX), F32),
            pltpu.VMEM((2, 3, STEP_ROWS, AUX), F32),
            pltpu.VMEM((SLOTS * WIDTH, AUX), F32),
            pltpu.VMEM((SLOTS * WIDTH, AUX), F32),
            pltpu.VMEM((SLOTS * WIDTH, AUX), F32),
            pltpu.VMEM((OWN, WIDTH, AUX), F32),
            pltpu.VMEM((ALL, 1), F32),
            pltpu.VMEM((4, 1, STACK), F32),
            chunk, chunk, chunk, chunk, chunk, chunk, chunk, chunk,
            dma((GROUPS,)),
            dma((GROUPS,)),
            dma((BLOCKS,)),
            dma((BLOCKS,)),
            dma((2 + CHUNKS,)),
            dma((2,)),
            dma((CHUNKS, GROUPS)),
            dma((CHUNKS, GROUPS)),
            dma((SLOTS, CHUNKS)),
            dma((SLOTS, CHUNKS)),
            dma((3, SLOTS, 2, CHUNKS)),
            dma((3, SLOTS, 2, CHUNKS)),
            dma((3, SLOTS, 2, CHUNKS)),
            dma((3, SLOTS, 2, CHUNKS)),
            dma((SLOTS, CHUNKS)),
            dma((SLOTS, CHUNKS)),
            dma((CHUNKS, GROUPS)),
            dma((CHUNKS, GROUPS)),
            dma((2,)),
        ],
        compiler_params=pltpu.CompilerParams(
            collective_id=0, has_side_effects=True, vmem_limit_bytes=66_000_000),
        name="main",
    )(lists, orbitals, occ, vir, held)


def join_kernel(flags, own_ref, arrived_ref, out_ref):
    out_ref[...] = own_ref[...]
    for peer in range(GROUPS):
        @pl.when(flags[1, peer] > 0)
        def _():
            out_ref[flags[0, peer]] += arrived_ref[peer]


def join(flags, own, arrived):
    height = 16
    return pl.pallas_call(
        join_kernel,
        out_shape=jax.ShapeDtypeStruct((OWN, WIDTH, AUX), F32),
        grid_spec=pltpu.PrefetchScalarGridSpec(
            num_scalar_prefetch=1,
            grid=(WIDTH // height,),
            in_specs=[
                pl.BlockSpec((OWN, height, AUX), lambda i, *_: (0, i, 0)),
                pl.BlockSpec((GROUPS, height, AUX), lambda i, *_: (0, i, 0)),
            ],
            out_specs=pl.BlockSpec((OWN, height, AUX), lambda i, *_: (0, i, 0)),
        ),
        name="join",
    )(flags, own, arrived)


def body(integrals, pair_lists, row_orbital, occ_energy, vir_energy):
    own, arrived, flags = run_main(
        pair_lists, row_orbital, occ_energy, vir_energy.reshape(1, WIDTH), integrals)
    return join(flags, own, arrived)


def solution(mesh):
    in_specs = (P("grp", "blk", None), P("grp", None), P("grp"), P(), P("blk"))
    out_specs = P("grp", "blk", None)
    return jax.shard_map(body, mesh=mesh, in_specs=in_specs, out_specs=out_specs, check_vma=False)
```

```python
import jax
import jax.numpy as jnp
from jax import lax
from jax.experimental import pallas as pl
from jax.experimental.pallas import tpu as pltpu
from jax.sharding import PartitionSpec as P

MESH = pl.DeviceIdType.MESH
F32 = jnp.float32
BF16 = jnp.bfloat16
GROUPS = 8
BLOCKS = 16
OWN = 12
SLOTS = 2
WIDTH = 64
AUX = 1536
HELD = OWN * WIDTH
ALL = 2 * HELD
CHUNKS = 4
PART = WIDTH // CHUNKS
HALF = WIDTH // 2
STEP_ROWS = 2 * SLOTS * HALF
STACK = 2 * STEP_ROWS
TILE = 512
TILES = ALL // TILE
LANES = 128
NT = (((1,), (1,)), ((), ()))
TN = (((0,), (0,)), ((), ()))
CALL_OF = {(0, 0): (0, 0), (0, 1): (0, 1), (0, 2): (1, 0), (0, 3): (1, 1),
           (1, 1): (2, 0), (1, 2): (2, 1), (1, 3): (3, 0), (1, 0): (3, 1)}


def split(values):
    high = values.astype(BF16)
    return high, (values - high.astype(F32)).astype(BF16)


def step_rows(slot, part, c):
    return pl.ds((slot * 2 + part) * HALF + (c % 2) * PART, PART)


def sum_place(step, slot, part, c):
    call, half = CALL_OF[(c // 2, step)]
    return call, pl.ds(half * STEP_ROWS + (slot * 2 + part) * HALF + (c % 2) * PART, PART)


def main_kernel(
    lists_ref, orbitals_ref, occ_ref, vir_ref, held_ref,
    own_out, arrived, flags,
    ints_mine, ints_all, vir_mine, vir_all, ints,
    high, low, total, stack, travel, amp, sums, landed,
    side_send, side_land, home, other, row_part, column_part,
    near_land, near_back,
    got_0, got_1, got_2, got_3, box_0, box_1, box_2, box_3,
    note_a, note_b, note_c, note_d, local_sem, swap_sem,
    fetch_send, fetch_recv, side_a, side_b,
    hop_send, hop_recv, sum_send, sum_recv, back_a, back_b,
    out_send, out_recv, own_sem, near_a, near_b, far_a, far_b,
):
    group = lax.axis_index("grp")
    block = lax.axis_index("blk")
    column = group // 2
    upper_side = lax.rem(group, 2)
    opposite = group + 1 - 2 * upper_side
    facing = {"grp": opposite}
    core = lax.rem(block, 2)
    level = lax.rem(block // 2, 4)
    side = block // 8
    twin_block = block + 1 - 2 * core
    twin = {"blk": twin_block}
    across = {"blk": lax.rem(block + 8, 16)}
    ring = (
        {"blk": side * 8 + lax.rem(level + 1, 4) * 2 + core},
        {"blk": side * 8 + lax.rem(level + 3, 4) * 2 + core},
    )
    got = (got_0, got_1, got_2, got_3)
    box = (box_0, box_1, box_2, box_3)

    barrier = pltpu.get_barrier_semaphore()
    for step in range(1, GROUPS):
        pl.semaphore_signal(barrier, 1, device_id={"grp": lax.rem(group + step, GROUPS)}, device_id_type=MESH)
    for step in range(1, BLOCKS):
        pl.semaphore_signal(barrier, 1, device_id={"blk": lax.rem(block + step, BLOCKS)}, device_id_type=MESH)

    keep = pltpu.make_async_copy(held_ref, other, local_sem.at[0])
    keep.start()
    lane = lax.broadcasted_iota(jnp.int32, (1, LANES), 1)
    row = jnp.zeros((1, LANES), jnp.int32)
    for j in range(SLOTS):
        row = jnp.where(lane == j, lists_ref[0, j], row)
    for j in range(OWN):
        row = jnp.where(lane == SLOTS + j, orbitals_ref[j], row)
    ints_mine[...] = row
    ints_all[group] = row
    vir = vir_ref[...]
    vir_row = jnp.concatenate([vir[:, :HALF]] * 8 + [vir[:, HALF:]] * 8, axis=1)
    vir_mine[...] = vir_row
    vir_all[block] = vir_row
    pl.semaphore_wait(barrier, GROUPS + BLOCKS - 2)

    def remote(src, dst, send, recv, peer):
        return pltpu.make_async_remote_copy(src, dst, send, recv, device_id=peer, device_id_type=MESH)

    def to_group(step, slot):
        return remote(ints_mine, ints_all.at[slot], note_a.at[step], note_b.at[slot],
                      {"grp": lax.rem(group + step, GROUPS)})

    def to_block(step, slot):
        return remote(vir_mine, vir_all.at[slot], note_c.at[step], note_d.at[slot],
                      {"blk": lax.rem(block + step, BLOCKS)})

    for step in range(1, GROUPS):
        to_group(step, group).start()
    for step in range(1, BLOCKS):
        to_block(step, block).start()
    keep.wait()
    for step in range(1, GROUPS):
        to_group(step, lax.rem(group + step, GROUPS)).wait_recv()
    to_scalar = pltpu.make_async_copy(ints_all, ints, local_sem.at[1])
    to_scalar.start()
    to_scalar.wait()

    def held_by(step, turn):
        return lax.rem(column + step, 4) * 2 + lax.rem(upper_side + turn, 2)

    for x in range(4):
        for turn in range(2):
            peer = x * 2 + lax.rem(upper_side + turn, 2)
            place = jnp.int32(0)
            found = jnp.int32(0)
            for slot in range(SLOTS):
                listed = ints[peer, 0, slot]
                match = listed // OWN == group
                place = jnp.where(match, listed % OWN, place)
                found = jnp.where(match, 1, found)
            flags[0, x * 2 + turn] = place
            flags[1, x * 2 + turn] = found

    def fetch(step, c, x):
        return remote(box[c].at[pl.ds(step * 2, 2)], got[c].at[pl.ds(x * 2, 2)],
                      fetch_send.at[c, step], fetch_recv.at[c, x], {"grp": held_by(step, 0)})

    def fill(c):
        for step in range(4):
            for turn in range(2):
                values = other[flags[0, lax.rem(column + step, 4) * 2 + turn], pl.ds(c * PART, PART), :]
                if step == 0:
                    got[c][column * 2 + turn] = values
                else:
                    box[c][step * 2 + turn] = values

    fill(0)
    for c in range(CHUNKS):
        if c + 1 < CHUNKS:
            fill(c + 1)
        for step in range(1, 4):
            fetch(step, c, column).start()

    swap = remote(held_ref, total.at[pl.ds(OWN, OWN)], swap_sem.at[0], swap_sem.at[1], twin)

    def prepare(source, first):
        def tile(index, carry):
            rows = pl.ds(pl.multiple_of((first + index) * WIDTH, WIDTH), WIDTH)
            upper, lower = split(source[index + (first if source is total else 0)])
            high[rows, :] = upper
            low[rows, :] = lower
            total[first + index] = jnp.zeros((WIDTH, AUX), F32)
            return carry
        lax.fori_loop(0, OWN, tile, 0)

    prepare(other, 0)
    swap.start()

    mine = [ints[group, 0, slot] for slot in range(SLOTS)]
    theirs = [ints[opposite, 0, slot] for slot in range(SLOTS)]
    one, none = jnp.float32(1), jnp.float32(0)
    sources = [jnp.minimum(row // OWN, GROUPS - 1) for row in mine]
    columns = [source // 2 for source in sources]
    their_columns = [jnp.minimum(row // OWN, GROUPS - 1) // 2 for row in theirs]
    level_with = [jnp.where((row < GROUPS * OWN) & (lax.rem(row // OWN, 2) == upper_side), one, none) for row in mine]
    opposed = [jnp.where((row < GROUPS * OWN) & (lax.rem(row // OWN, 2) != upper_side), one, none) for row in mine]
    partner_energy = [
        occ_ref[ints[sources[slot], 0, SLOTS + mine[slot] % OWN]] for slot in range(SLOTS)
    ]
    for step in range(1, BLOCKS):
        to_block(step, lax.rem(block + step, BLOCKS)).wait_recv()
    square = (lax.broadcasted_iota(jnp.int32, (HALF, HALF), 0)
              == lax.broadcasted_iota(jnp.int32, (HALF, HALF), 1))
    for owner, place in ((block, 0), (twin_block, 1)):
        for h in range(2):
            line = vir_all[owner, :, pl.ds(h * STACK, LANES)][:, :HALF]
            upright = jnp.sum(jnp.where(square, line, 0.0), axis=1, keepdims=True)
            for i in range(OWN):
                energy = occ_ref[ints[group, 0, SLOTS + i]]
                row_part[pl.ds((place * OWN + i) * WIDTH + h * HALF, HALF), :] = energy - upright
    piece = lax.broadcasted_iota(jnp.int32, (1, STACK), 1) // HALF
    for at_call in range(4):
        terms = jnp.zeros((1, STACK), F32)
        for (h, step), (call, half) in CALL_OF.items():
            if call != at_call:
                continue
            for slot in range(SLOTS):
                for part in range(2):
                    from_level = lax.rem(level + (4 - step if slot == 0 else step), 4)
                    from_side = side + part - 2 * part * side
                    line = vir_all[from_side * 8 + from_level * 2 + core, :, pl.ds(h * STACK, STACK)]
                    here = piece == half * 4 + slot * 2 + part
                    terms = jnp.where(here, partner_energy[slot] - line, terms)
        column_part[at_call] = terms

    def beside(slot, c):
        return remote(stack.at[c // 2, 0, step_rows(slot, 0, c)], stack.at[c // 2, 0, step_rows(slot, 1, c)],
                      side_a.at[slot, c], side_b.at[slot, c], across)

    def hop(step, slot, part, c):
        rows = step_rows(slot, part, c)
        return remote(stack.at[c // 2, step, rows], stack.at[c // 2, step + 1, rows],
                      hop_send.at[step, slot, part, c], hop_recv.at[step, slot, part, c], ring[slot])

    def sum_hop(step, slot, part, c):
        call, rows = sum_place(step, slot, part, c)
        return remote(sums.at[call, rows], landed.at[c // 2, step - 1, step_rows(slot, part, c)],
                      sum_send.at[step - 1, slot, part, c], sum_recv.at[step - 1, slot, part, c], ring[slot])

    def side_rows(slot, c):
        return pl.ds(slot * WIDTH + c * PART, PART)

    def cross(slot, c):
        rows = side_rows(slot, c)
        return remote(side_send.at[rows], side_land.at[rows], back_a.at[slot, c], back_b.at[slot, c], across)

    def pass_on(c):
        return remote(box[c].at[pl.ds(0, 2)], near_land.at[c], near_a.at[c], near_b.at[c], facing)

    def pass_back(c):
        return remote(home.at[c], near_back.at[c], far_a.at[c], far_b.at[c], facing)

    def ship(step, c, x):
        return remote(box[c].at[pl.ds(step * 2, 2)], arrived.at[pl.ds(x * 2, 2), pl.ds(c * PART, PART)],
                      out_send.at[c, step], out_recv.at[c, x], {"grp": held_by(step, 0)})

    def stay(c):
        return pltpu.make_async_copy(
            box[c].at[pl.ds(0, 2)], arrived.at[pl.ds(column * 2, 2), pl.ds(c * PART, PART)], local_sem.at[2 + c])

    def on_fetch(c):
        for step in range(1, 4):
            fetch(step, c, lax.rem(column + step, 4)).wait_recv()
        for slot in range(SLOTS):
            box[c][slot] = got[c][their_columns[slot] * 2 + 1]
        pass_on(c).start()

    def on_pass(c):
        pass_on(c).wait_recv()
        for slot in range(SLOTS):
            stack[c // 2, 0, step_rows(slot, 0, c), :] = (
                got[c][columns[slot] * 2] * level_with[slot] + near_land[c, slot] * opposed[slot])
        for slot in range(SLOTS):
            beside(slot, c).start()
            hop(0, slot, 0, c).start()

    def on_side(c):
        for slot in range(SLOTS):
            beside(slot, c).wait_recv()
            hop(0, slot, 1, c).start()

    def on_hop(step, part, c):
        for slot in range(SLOTS):
            hop(step - 1, slot, part, c).wait_recv()
            if step < 3:
                hop(step, slot, part, c).start()

    def on_sum(step, c):
        for part in (1, 0):
            for slot in range(SLOTS):
                if step > 1:
                    sum_hop(step - 1, slot, part, c).wait_recv()
                    call, rows = sum_place(step, slot, part, c)
                    sums[call, rows, :] += landed[c // 2, step - 2, step_rows(slot, part, c), :]
        for part in (1, 0):
            for slot in range(SLOTS):
                sum_hop(step, slot, part, c).start()

    def on_home(c):
        for part in (1, 0):
            for slot in range(SLOTS):
                sum_hop(3, slot, part, c).wait_recv()
                call, rows = sum_place(0, slot, part, c)
                value = sums[call, rows, :] + landed[c // 2, 2, step_rows(slot, part, c), :]
                if part:
                    side_send[side_rows(slot, c), :] = value
                else:
                    home[c, slot] = value
            if part:
                for slot in range(SLOTS):
                    cross(slot, c).start()

    def on_cross(c):
        for slot in range(SLOTS):
            cross(slot, c).wait_recv()
            home[c, slot] += side_land[side_rows(slot, c), :]
        pass_back(c).start()

    def on_ship(c):
        for step in range(1, 4):
            fetch(step, c, column).wait_send()
        pass_on(c).wait_send()

        def blend(rows, source, step):
            picks = [jnp.where(row // OWN == held_by(step, 0), one, none) for row in rows]
            return picks[0] * source[c, 0] + picks[1] * source[c, 1]

        for step in range(4):
            box[c][step * 2] = blend(mine, home, step)
        pass_back(c).wait_recv()
        for step in range(4):
            box[c][step * 2 + 1] = blend(theirs, near_back, step)
        for step in range(1, 4):
            ship(step, c, column).start()
        stay(c).start()

    def play(*actions):
        for action, *where in actions:
            action(*where)

    on_fetch(0)
    swap.wait()
    prepare(total, OWN)
    play((on_pass, 0), (on_fetch, 1), (on_hop, 1, 0, 0), (on_side, 0), (on_pass, 1), (on_hop, 1, 1, 0),
         (on_hop, 2, 0, 0), (on_fetch, 2), (on_hop, 1, 0, 1), (on_side, 1), (on_hop, 2, 1, 0), (on_hop, 2, 0, 1),
         (on_pass, 2), (on_hop, 1, 1, 1))

    open_events = {
        1: [(on_hop, 3, 0, 0), (on_hop, 3, 1, 0), (on_hop, 3, 0, 1), (on_hop, 3, 1, 1)],
        3: [(on_hop, 3, 0, 2), (on_hop, 3, 1, 2), (on_hop, 3, 0, 3), (on_hop, 3, 1, 3)],
    }
    pair_events = {
        (0, 0): [(on_fetch, 3)],
        (0, 1): [(on_hop, 1, 0, 2), (on_side, 2)],
        (0, 2): [(on_hop, 2, 1, 1)],
        (1, 1): [(on_hop, 2, 0, 3), (on_hop, 1, 1, 3)],
        (3, 2): [(on_home, 0)],
    }
    back_events = {
        (0, 1): [(on_hop, 2, 0, 2), (on_pass, 3)],
        (0, 2): [(on_hop, 1, 1, 2), (on_sum, 1, 0), (on_sum, 1, 1)],
        (1, 2): [(on_hop, 2, 1, 3), (on_sum, 2, 0), (on_sum, 2, 1)],
        (2, 0): [(on_sum, 3, 0)],
        (2, 2): [(on_sum, 3, 1), (on_sum, 1, 2), (on_sum, 1, 3)],
        (3, 0): [(on_sum, 2, 2)],
        (3, 1): [(on_home, 1)],
        (3, 2): [(on_sum, 2, 3)],
    }
    own_events = {
        (0, 1): [(on_hop, 1, 0, 3)],
        (0, 2): [(on_hop, 2, 1, 2), (on_side, 3)],
        (3, 0): [(on_cross, 0)],
        (3, 1): [(on_cross, 1)],
        (3, 2): [(on_ship, 0)],
    }

    def run(events, call, index):
        for (at_call, at_index), actions in events.items():
            @pl.when((call == at_call) & (index == at_index))
            def _():
                play(*actions)

    def one_call(call, carry):
        for at_call, actions in open_events.items():
            @pl.when(call == at_call)
            def _():
                play(*actions)

        h = call // 2
        first = (call % 2) * 2 + h
        second = (first + 1) % 4

        def cut(index, carry):
            for half, step in ((0, first), (1, second)):
                upper, lower = split(stack[h, step, pl.ds(pl.multiple_of(index * 64, 64), 64), :])
                start = half * STEP_ROWS + index * 64
                travel[pl.ds(pl.multiple_of(start, 64), 64), :] = upper
                travel[pl.ds(pl.multiple_of(STACK + start, 64), 64), :] = lower
                travel[pl.ds(pl.multiple_of(2 * STACK + start, 64), 64), :] = upper
                sums[call, pl.ds(pl.multiple_of(start, 64), 64), :] = jnp.zeros((64, AUX), F32)
            return carry

        lax.fori_loop(0, STEP_ROWS // 64, cut, 0)

        def pair_tile(index, carry):
            rows = pl.ds(pl.multiple_of(index * TILE, TILE), TILE)
            upper = high[rows, :]
            near = travel[pl.ds(0, STACK), :]
            pair = lax.dot_general(upper, near, NT, preferred_element_type=F32)
            pair += lax.dot_general(upper, travel[pl.ds(STACK, STACK), :], NT, preferred_element_type=F32)
            pair += lax.dot_general(low[rows, :], near, NT, preferred_element_type=F32)
            big, small = split(pair / (row_part[rows, :] + column_part[call]))
            amp[rows, pl.ds(0, STACK)] = big
            amp[rows, pl.ds(STACK, STACK)] = big
            amp[rows, pl.ds(2 * STACK, STACK)] = small
            run(pair_events, call, index)
            return carry

        lax.fori_loop(0, TILES, pair_tile, 0)

        def back_tile(index, carry):
            rows = pl.ds(pl.multiple_of(index * TILE, TILE), TILE)
            upper = high[rows, :]
            big = amp[rows, pl.ds(0, STACK)]
            back = lax.dot_general(big, upper, TN, preferred_element_type=F32)
            back += lax.dot_general(big, low[rows, :], TN, preferred_element_type=F32)
            back += lax.dot_general(amp[rows, pl.ds(2 * STACK, STACK)], upper, TN, preferred_element_type=F32)
            sums[call] += back
            run(back_events, call, index)
            return carry

        lax.fori_loop(0, TILES, back_tile, 0)

        def own_tile(index, carry):
            rows = pl.ds(pl.multiple_of(index * TILE, TILE), TILE)
            held = pl.ds(index * (TILE // WIDTH), TILE // WIDTH)
            forward = jnp.dot(amp[rows, :], travel[...], preferred_element_type=F32)
            total[held] += forward.reshape(TILE // WIDTH, WIDTH, AUX)
            run(own_events, call, index)
            return carry

        lax.fori_loop(0, TILES, own_tile, 0)
        return carry

    lax.fori_loop(0, 4, one_call, 0)

    give = remote(total.at[pl.ds(OWN, OWN)], other, own_sem.at[0], own_sem.at[1], twin)
    on_sum(3, 2)
    give.start()
    play((on_sum, 3, 3), (on_ship, 1), (on_home, 2), (on_home, 3), (on_cross, 2), (on_cross, 3), (on_ship, 2), (on_ship, 3))
    give.wait()

    def merge(index, carry):
        total[index] += other[index]
        return carry

    lax.fori_loop(0, OWN, merge, 0)
    store = pltpu.make_async_copy(total.at[pl.ds(0, OWN)], own_out, local_sem.at[0])
    store.start()
    for step in range(1, GROUPS):
        to_group(step, group).wait_send()
    for step in range(1, BLOCKS):
        to_block(step, block).wait_send()
    for c in range(CHUNKS):
        for slot in range(SLOTS):
            beside(slot, c).wait_send()
            cross(slot, c).wait_send()
            for part in range(2):
                for step in range(3):
                    hop(step, slot, part, c).wait_send()
                    sum_hop(step + 1, slot, part, c).wait_send()
    for c in range(CHUNKS):
        stay(c).wait()
        pass_back(c).wait_send()
        for step in range(1, 4):
            ship(step, c, column).wait_send()
            ship(step, c, lax.rem(column + step, 4)).wait_recv()
    store.wait()


def run_main(lists, orbitals, occ, vir, held):
    smem = pl.BlockSpec(memory_space=pltpu.SMEM)
    vmem = pl.BlockSpec(memory_space=pltpu.VMEM)
    hbm = pl.BlockSpec(memory_space=pl.ANY)
    dma = pltpu.SemaphoreType.DMA
    chunk = pltpu.VMEM((GROUPS, PART, AUX), F32)
    return pl.pallas_call(
        main_kernel,
        out_shape=(
            jax.ShapeDtypeStruct((OWN, WIDTH, AUX), F32),
            jax.ShapeDtypeStruct((GROUPS, WIDTH, AUX), F32),
            jax.ShapeDtypeStruct((2, GROUPS), jnp.int32),
        ),
        in_specs=[smem, smem, smem, vmem, hbm],
        out_specs=(hbm, hbm, smem),
        scratch_shapes=[
            pltpu.VMEM((1, LANES), jnp.int32),
            pltpu.VMEM((GROUPS, 1, LANES), jnp.int32),
            pltpu.VMEM((1, 2 * STACK), F32),
            pltpu.VMEM((BLOCKS, 1, 2 * STACK), F32),
            pltpu.SMEM((GROUPS, 1, LANES), jnp.int32),
            pltpu.VMEM((ALL, AUX), BF16),
            pltpu.VMEM((ALL, AUX), BF16),
            pltpu.VMEM((2 * OWN, WIDTH, AUX), F32),
            pltpu.VMEM((2, 4, STEP_ROWS, AUX), F32),
            pltpu.VMEM((3 * STACK, AUX), BF16),
            pltpu.VMEM((ALL, 3 * STACK), BF16),
            pltpu.VMEM((4, STACK, AUX), F32),
            pltpu.VMEM((2, 3, STEP_ROWS, AUX), F32),
            pltpu.VMEM((SLOTS * WIDTH, AUX), F32),
            pltpu.VMEM((SLOTS * WIDTH, AUX), F32),
            pltpu.VMEM((CHUNKS, SLOTS, PART, AUX), F32),
            pltpu.VMEM((OWN, WIDTH, AUX), F32),
            pltpu.VMEM((ALL, 1), F32),
            pltpu.VMEM((4, 1, STACK), F32),
            pltpu.VMEM((CHUNKS, SLOTS, PART, AUX), F32),
            pltpu.VMEM((CHUNKS, SLOTS, PART, AUX), F32),
            chunk, chunk, chunk, chunk, chunk, chunk, chunk, chunk,
            dma((GROUPS,)),
            dma((GROUPS,)),
            dma((BLOCKS,)),
            dma((BLOCKS,)),
            dma((2 + CHUNKS,)),
            dma((2,)),
            dma((CHUNKS, 4)),
            dma((CHUNKS, 4)),
            dma((SLOTS, CHUNKS)),
            dma((SLOTS, CHUNKS)),
            dma((3, SLOTS, 2, CHUNKS)),
            dma((3, SLOTS, 2, CHUNKS)),
            dma((3, SLOTS, 2, CHUNKS)),
            dma((3, SLOTS, 2, CHUNKS)),
            dma((SLOTS, CHUNKS)),
            dma((SLOTS, CHUNKS)),
            dma((CHUNKS, 4)),
            dma((CHUNKS, 4)),
            dma((2,)),
            dma((CHUNKS,)),
            dma((CHUNKS,)),
            dma((CHUNKS,)),
            dma((CHUNKS,)),
        ],
        compiler_params=pltpu.CompilerParams(
            collective_id=0, has_side_effects=True, vmem_limit_bytes=66_000_000),
        name="main",
    )(lists, orbitals, occ, vir, held)


def join_kernel(flags, own_ref, arrived_ref, out_ref):
    out_ref[...] = own_ref[...]
    for peer in range(GROUPS):
        @pl.when(flags[1, peer] > 0)
        def _():
            out_ref[flags[0, peer]] += arrived_ref[peer]


def join(flags, own, arrived):
    height = 16
    return pl.pallas_call(
        join_kernel,
        out_shape=jax.ShapeDtypeStruct((OWN, WIDTH, AUX), F32),
        grid_spec=pltpu.PrefetchScalarGridSpec(
            num_scalar_prefetch=1,
            grid=(WIDTH // height,),
            in_specs=[
                pl.BlockSpec((OWN, height, AUX), lambda i, *_: (0, i, 0)),
                pl.BlockSpec((GROUPS, height, AUX), lambda i, *_: (0, i, 0)),
            ],
            out_specs=pl.BlockSpec((OWN, height, AUX), lambda i, *_: (0, i, 0)),
        ),
        name="join",
    )(flags, own, arrived)


def body(integrals, pair_lists, row_orbital, occ_energy, vir_energy):
    own, arrived, flags = run_main(
        pair_lists, row_orbital, occ_energy, vir_energy.reshape(1, WIDTH), integrals)
    return join(flags, own, arrived)


def solution(mesh):
    in_specs = (P("grp", "blk", None), P("grp", None), P("grp"), P(), P("blk"))
    out_specs = P("grp", "blk", None)
    return jax.shard_map(body, mesh=mesh, in_specs=in_specs, out_specs=out_specs, check_vma=False)
```

```python
import jax
import jax.numpy as jnp
from jax import lax
from jax.experimental import pallas as pl
from jax.experimental.pallas import tpu as pltpu
from jax.sharding import PartitionSpec as P

MESH = pl.DeviceIdType.MESH
F32 = jnp.float32
BF16 = jnp.bfloat16
GROUPS = 8
BLOCKS = 16
OWN = 12
SLOTS = 2
WIDTH = 64
AUX = 1536
HELD = OWN * WIDTH
ALL = 2 * HELD
CHUNKS = 8
SWAPPED = (3, 5)
PART = WIDTH // CHUNKS
CALLS = 4
PIECE = WIDTH // CALLS
STEP_ROWS = 2 * SLOTS * PIECE
STACK = 4 * STEP_ROWS
TILE = 512
TILES = ALL // TILE
LANES = 128
NT = (((1,), (1,)), ((), ()))
TN = (((0,), (0,)), ((), ()))
OPENING = {
    0: [("fetch", 0), ("pass", 0), ("fetch", 1), ("hop", 1, 0, 0), ("side", 0, 0), ("fetch", 2),
        ("hop", 2, 0, 0), ("hop", 1, 1, 0), ("pass", 1), ("hop", 3, 0, 0), ("hop", 2, 1, 0), ("pass", 2),
        ("fetch", 3), ("hop", 1, 0, 1), ("side", 0, 1), ("hop", 3, 1, 0), ("hop", 1, 0, 2), ("side", 0, 2),
        ("fetch", 4), ("hop", 2, 0, 1), ("hop", 1, 1, 1), ("pass", 3), ("hop", 2, 0, 2), ("hop", 1, 1, 2),
        ("pass", 4), ("fetch", 5), ("hop", 3, 0, 1), ("hop", 2, 1, 1), ("side", 0, 3), ("hop", 1, 0, 3),
        ("hop", 3, 0, 2), ("side", 0, 4), ("fetch", 6), ("hop", 2, 1, 2), ("hop", 1, 0, 4), ("pass", 5),
        ("hop", 3, 1, 1)],
    4: [("sum", 2, 6), ("ship", 2), ("sum", 2, 7), ("cross", 4), ("home", 5), ("sum", 3, 6), ("ship", 4),
        ("sum", 3, 7), ("ship", 5), ("home", 6), ("home", 7), ("cross", 6), ("cross", 7), ("ship", 6),
        ("ship", 7)],
}
BETWEEN = {
    (0, 0, 0): [("hop", 2, 0, 3), ("fetch", 7), ("side", 1, 3)],
    (0, 0, 1): [("hop", 3, 1, 2), ("hop", 1, 1, 4)],
    (0, 0, 2): [("pass", 6), ("hop", 2, 0, 4)],
    (0, 1, 0): [("hop", 3, 0, 3), ("hop", 1, 0, 5), ("side", 0, 5)],
    (0, 1, 1): [("hop", 2, 1, 4), ("side", 2, 3)],
    (0, 1, 2): [("hop", 3, 0, 4), ("hop", 1, 0, 6), ("sum", 1, 0), ("sum", 1, 1)],
    (0, 2, 0): [("pass", 7), ("hop", 2, 0, 5)],
    (0, 2, 1): [("hop", 3, 1, 4), ("hop", 2, 0, 6), ("side", 0, 6)],
    (0, 2, 2): [("side", 3, 3)],
    (1, 0, 0): [("side", 1, 5), ("sum", 2, 0)],
    (1, 0, 1): [("sum", 2, 1)],
    (1, 0, 2): [("hop", 3, 0, 5), ("hop", 1, 0, 7), ("side", 0, 7)],
    (1, 1, 0): [("hop", 3, 0, 6), ("side", 2, 5)],
    (1, 1, 1): [("hop", 1, 1, 6)],
    (1, 1, 2): [("side", 3, 5), ("swap", 0, 3), ("swap", 1, 3), ("swap", 2, 3), ("swap", 3, 3), ("sum", 3, 0),
        ("sum", 1, 2)],
    (1, 2, 0): [("sum", 3, 1)],
    (1, 2, 1): [("hop", 2, 0, 7)],
    (1, 2, 2): [("hop", 1, 1, 7), ("hop", 2, 1, 6)],
    (2, 0, 0): [("sum", 1, 3)],
    (2, 0, 1): [("home", 0)],
    (2, 0, 2): [("sum", 2, 2)],
    (2, 1, 0): [("home", 1)],
    (2, 1, 1): [("hop", 3, 0, 7), ("cross", 0)],
    (2, 1, 2): [("hop", 2, 1, 7), ("swap", 0, 5), ("swap", 1, 5), ("hop", 3, 1, 6), ("swap", 2, 5),
        ("swap", 3, 5), ("sum", 1, 4)],
    (2, 2, 0): [("sum", 2, 3), ("cross", 1)],
    (2, 2, 1): [("ship", 0), ("sum", 3, 2)],
    (2, 2, 2): [("hop", 3, 1, 7)],
    (3, 0, 0): [("sum", 2, 4), ("sum", 1, 5)],
    (3, 0, 1): [("sum", 3, 3)],
    (3, 0, 2): [("home", 2)],
    (3, 1, 1): [("sum", 3, 4)],
    (3, 1, 2): [("sum", 2, 5), ("sum", 1, 6), ("sum", 1, 7), ("home", 3), ("ship", 1)],
    (3, 2, 0): [("cross", 2)],
    (3, 2, 1): [("sum", 3, 5), ("home", 4)],
    (3, 2, 2): [("ship", 3)],
}


def split(values):
    high = values.astype(BF16)
    return high, (values - high.astype(F32)).astype(BF16)


def step_rows(step, slot, part, c):
    return pl.ds(step * STEP_ROWS + (slot * 2 + part) * PIECE + (c % 2) * PART, PART)


def main_kernel(
    lists_ref, orbitals_ref, occ_ref, vir_ref, held_ref,
    own_out, arrived, flags,
    ints_mine, ints_all, vir_mine, vir_all, ints,
    high, low, total, stack, travel, amp, sums, landed,
    side_send, side_land, home, other, row_part, column_part,
    near_land, near_back, swapped,
    note_a, note_b, note_c, note_d, local_sem, swap_sem,
    fetch_send, fetch_recv, side_a, side_b,
    hop_send, hop_recv, sum_send, sum_recv, back_a, back_b,
    out_send, out_recv, own_sem, near_a, near_b, far_a, far_b, trade_a, trade_b,
    *chunks,
):
    group = lax.axis_index("grp")
    block = lax.axis_index("blk")
    column = group // 2
    upper_side = lax.rem(group, 2)
    opposite = group + 1 - 2 * upper_side
    facing = {"grp": opposite}
    core = lax.rem(block, 2)
    level = lax.rem(block // 2, 4)
    side = block // 8
    twin_block = block + 1 - 2 * core
    twin = {"blk": twin_block}
    across = {"blk": lax.rem(block + 8, 16)}
    ring = (
        {"blk": side * 8 + lax.rem(level + 1, 4) * 2 + core},
        {"blk": side * 8 + lax.rem(level + 3, 4) * 2 + core},
    )
    got, box = chunks[:CHUNKS], chunks[CHUNKS:]

    barrier = pltpu.get_barrier_semaphore()
    for step in range(1, GROUPS):
        pl.semaphore_signal(barrier, 1, device_id={"grp": lax.rem(group + step, GROUPS)}, device_id_type=MESH)
    for step in range(1, BLOCKS):
        pl.semaphore_signal(barrier, 1, device_id={"blk": lax.rem(block + step, BLOCKS)}, device_id_type=MESH)

    keep = pltpu.make_async_copy(held_ref, other, local_sem.at[0])
    keep.start()
    lane = lax.broadcasted_iota(jnp.int32, (1, LANES), 1)
    row = jnp.zeros((1, LANES), jnp.int32)
    for j in range(SLOTS):
        row = jnp.where(lane == j, lists_ref[0, j], row)
    for j in range(OWN):
        row = jnp.where(lane == SLOTS + j, orbitals_ref[j], row)
    ints_mine[...] = row
    ints_all[group] = row
    vir = vir_ref[...]
    vir_row = jnp.concatenate([vir, vir], axis=1)
    vir_mine[...] = vir_row
    vir_all[block] = vir_row
    pl.semaphore_wait(barrier, GROUPS + BLOCKS - 2)

    def remote(src, dst, send, recv, peer):
        return pltpu.make_async_remote_copy(src, dst, send, recv, device_id=peer, device_id_type=MESH)

    def to_group(step, slot):
        return remote(ints_mine, ints_all.at[slot], note_a.at[step], note_b.at[slot],
                      {"grp": lax.rem(group + step, GROUPS)})

    def to_block(step, slot):
        return remote(vir_mine, vir_all.at[slot], note_c.at[step], note_d.at[slot],
                      {"blk": lax.rem(block + step, BLOCKS)})

    for step in range(1, GROUPS):
        to_group(step, group).start()
    for step in range(1, BLOCKS):
        to_block(step, block).start()
    keep.wait()
    for step in range(1, GROUPS):
        to_group(step, lax.rem(group + step, GROUPS)).wait_recv()
    to_scalar = pltpu.make_async_copy(ints_all, ints, local_sem.at[1])
    to_scalar.start()
    to_scalar.wait()

    def held_by(step, turn):
        return lax.rem(column + step, 4) * 2 + lax.rem(upper_side + turn, 2)

    for x in range(4):
        for turn in range(2):
            peer = x * 2 + lax.rem(upper_side + turn, 2)
            place = jnp.int32(0)
            found = jnp.int32(0)
            for slot in range(SLOTS):
                listed = ints[peer, 0, slot]
                match = listed // OWN == group
                place = jnp.where(match, listed % OWN, place)
                found = jnp.where(match, 1, found)
            flags[0, x * 2 + turn] = place
            flags[1, x * 2 + turn] = found

    def fetch(step, c, x):
        return remote(box[c].at[pl.ds(step * 2, 2)], got[c].at[pl.ds(x * 2, 2)],
                      fetch_send.at[c, step], fetch_recv.at[c, x], {"grp": held_by(step, 0)})

    def fill(c):
        for step in range(4):
            for turn in range(2):
                values = other[flags[0, lax.rem(column + step, 4) * 2 + turn], pl.ds(c * PART, PART), :]
                if step == 0:
                    got[c][column * 2 + turn] = values
                else:
                    box[c][step * 2 + turn] = values

    fill(0)
    for c in range(CHUNKS):
        if c + 1 < CHUNKS:
            fill(c + 1)
        for step in range(1, 4):
            fetch(step, c, column).start()

    swap = remote(held_ref, total.at[pl.ds(OWN, OWN)], swap_sem.at[0], swap_sem.at[1], twin)

    def prepare(source, first):
        def tile(index, carry):
            rows = pl.ds(pl.multiple_of((first + index) * WIDTH, WIDTH), WIDTH)
            upper, lower = split(source[index + (first if source is total else 0)])
            high[rows, :] = upper
            low[rows, :] = lower
            total[first + index] = jnp.zeros((WIDTH, AUX), F32)
            return carry
        lax.fori_loop(0, OWN, tile, 0)

    prepare(other, 0)
    swap.start()

    mine = [ints[group, 0, slot] for slot in range(SLOTS)]
    theirs = [ints[opposite, 0, slot] for slot in range(SLOTS)]
    one, none = jnp.float32(1), jnp.float32(0)
    sources = [jnp.minimum(row // OWN, GROUPS - 1) for row in mine]
    columns = [source // 2 for source in sources]
    their_columns = [jnp.minimum(row // OWN, GROUPS - 1) // 2 for row in theirs]
    level_with = [jnp.where((row < GROUPS * OWN) & (lax.rem(row // OWN, 2) == upper_side), one, none) for row in mine]
    opposed = [jnp.where((row < GROUPS * OWN) & (lax.rem(row // OWN, 2) != upper_side), one, none) for row in mine]
    partner_energy = [
        occ_ref[ints[sources[slot], 0, SLOTS + mine[slot] % OWN]] for slot in range(SLOTS)
    ]
    for step in range(1, BLOCKS):
        to_block(step, lax.rem(block + step, BLOCKS)).wait_recv()
    square = (lax.broadcasted_iota(jnp.int32, (WIDTH, WIDTH), 0)
              == lax.broadcasted_iota(jnp.int32, (WIDTH, WIDTH), 1))
    for owner, place in ((block, 0), (twin_block, 1)):
        line = vir_all[owner][:, :WIDTH]
        upright = jnp.sum(jnp.where(square, line, 0.0), axis=1, keepdims=True)
        for i in range(OWN):
            energy = occ_ref[ints[group, 0, SLOTS + i]]
            row_part[pl.ds((place * OWN + i) * WIDTH, WIDTH), :] = energy - upright
    lines = []
    for step in range(4):
        for slot in range(SLOTS):
            for part in range(2):
                from_level = lax.rem(level + (4 - step if slot == 0 else step), 4)
                from_side = side + part - 2 * part * side
                lines.append(partner_energy[slot] - vir_all[from_side * 8 + from_level * 2 + core])
    for call in range(CALLS):
        pieces = [line[:, call * PIECE:(call + 1) * PIECE] for line in lines]
        column_part[call] = jnp.concatenate(pieces, axis=1)

    def beside(step, slot, c):
        return remote(stack.at[c // 2, step_rows(step, slot, 0, c)], stack.at[c // 2, step_rows(step, slot, 1, c)],
                      side_a.at[step, slot, c], side_b.at[step, slot, c], across)

    def hop(step, slot, part, c):
        return remote(stack.at[c // 2, step_rows(step, slot, part, c)],
                      stack.at[c // 2, step_rows(step + 1, slot, part, c)],
                      hop_send.at[step, slot, part, c], hop_recv.at[step, slot, part, c], ring[slot])

    def landing(step, slot, part, c):
        return landed.at[c // 2, step_rows(step - 1, slot, part, c)]

    def sum_hop(step, slot, part, c):
        return remote(sums.at[c // 2, step_rows(step, slot, part, c)], landing(step, slot, part, c),
                      sum_send.at[step - 1, slot, part, c], sum_recv.at[step - 1, slot, part, c], ring[slot])

    def traded(step, slot, c):
        return swapped.at[SWAPPED.index(c), step, slot]

    def trade(step, slot, c):
        place = SWAPPED.index(c)
        return remote(sums.at[c // 2, step_rows(step, slot, 1, c)], traded(step, slot, c),
                      trade_a.at[place, step, slot], trade_b.at[place, step, slot], across)

    def side_rows(slot, c):
        return pl.ds(slot * WIDTH + c * PART, PART)

    def cross(slot, c):
        rows = side_rows(slot, c)
        return remote(side_send.at[rows], side_land.at[rows], back_a.at[slot, c], back_b.at[slot, c], across)

    def pass_on(c):
        return remote(box[c].at[pl.ds(0, 2)], near_land.at[c], near_a.at[c], near_b.at[c], facing)

    def pass_back(c):
        return remote(home.at[c], near_back.at[c], far_a.at[c], far_b.at[c], facing)

    def ship(step, c, x):
        return remote(box[c].at[pl.ds(step * 2, 2)], arrived.at[pl.ds(x * 2, 2), pl.ds(c * PART, PART)],
                      out_send.at[c, step], out_recv.at[c, x], {"grp": held_by(step, 0)})

    def stay(c):
        return pltpu.make_async_copy(
            box[c].at[pl.ds(0, 2)], arrived.at[pl.ds(column * 2, 2), pl.ds(c * PART, PART)], local_sem.at[2 + c])

    def on_fetch(c):
        for step in range(1, 4):
            fetch(step, c, lax.rem(column + step, 4)).wait_recv()
        for slot in range(SLOTS):
            box[c][slot] = got[c][their_columns[slot] * 2 + 1]
        pass_on(c).start()

    def on_pass(c):
        pass_on(c).wait_recv()
        for slot in range(SLOTS):
            stack[c // 2, step_rows(0, slot, 0, c), :] = (
                got[c][columns[slot] * 2] * level_with[slot] + near_land[c, slot] * opposed[slot])
        for slot in range(SLOTS):
            beside(0, slot, c).start()
            hop(0, slot, 0, c).start()

    def on_side(step, c):
        for slot in range(SLOTS):
            beside(step, slot, c).wait_recv()
            if c not in SWAPPED:
                hop(0, slot, 1, c).start()

    def on_hop(step, part, c):
        for slot in range(SLOTS):
            hop(step - 1, slot, part, c).wait_recv()
            if step < 3:
                hop(step, slot, part, c).start()
            if c in SWAPPED:
                beside(step, slot, c).start()

    def on_swap(step, c):
        for slot in range(SLOTS):
            trade(step, slot, c).start()

    def parts_of(c):
        return (0,) if c in SWAPPED else (1, 0)

    def on_sum(step, c):
        for part in parts_of(c):
            for slot in range(SLOTS):
                rows = step_rows(step, slot, part, c)
                if c in SWAPPED:
                    trade(step, slot, c).wait_recv()
                    sums[c // 2, rows, :] += traded(step, slot, c)[...]
                if step > 1:
                    sum_hop(step - 1, slot, part, c).wait_recv()
                    sums[c // 2, rows, :] += landing(step - 1, slot, part, c)[...]
        for part in parts_of(c):
            for slot in range(SLOTS):
                sum_hop(step, slot, part, c).start()

    def on_home(c):
        for part in parts_of(c):
            for slot in range(SLOTS):
                sum_hop(3, slot, part, c).wait_recv()
                value = sums[c // 2, step_rows(0, slot, part, c), :] + landing(3, slot, part, c)[...]
                if part:
                    side_send[side_rows(slot, c), :] = value
                    continue
                if c in SWAPPED:
                    trade(0, slot, c).wait_recv()
                    value += traded(0, slot, c)[...]
                home[c, slot] = value
            if part:
                for slot in range(SLOTS):
                    cross(slot, c).start()
        if c in SWAPPED:
            pass_back(c).start()

    def on_cross(c):
        for slot in range(SLOTS):
            cross(slot, c).wait_recv()
            home[c, slot] += side_land[side_rows(slot, c), :]
        pass_back(c).start()

    def on_ship(c):
        for step in range(1, 4):
            fetch(step, c, column).wait_send()
        pass_on(c).wait_send()

        def blend(rows, source, step):
            picks = [jnp.where(row // OWN == held_by(step, 0), one, none) for row in rows]
            return picks[0] * source[c, 0] + picks[1] * source[c, 1]

        for step in range(4):
            box[c][step * 2] = blend(mine, home, step)
        pass_back(c).wait_recv()
        for step in range(4):
            box[c][step * 2 + 1] = blend(theirs, near_back, step)
        for step in range(1, 4):
            ship(step, c, column).start()
        stay(c).start()

    act = {"fetch": on_fetch, "pass": on_pass, "side": on_side, "hop": on_hop, "swap": on_swap,
           "sum": on_sum, "home": on_home, "cross": on_cross, "ship": on_ship}

    def play(actions):
        for name, *where in actions:
            act[name](*where)

    play(OPENING[0][:1])
    swap.wait()
    prepare(total, OWN)
    play(OPENING[0][1:])

    def run(call, loop, index):
        for (at_call, at_loop, at_index), actions in BETWEEN.items():
            if at_loop != loop:
                continue

            @pl.when((call == at_call) & (index == at_index))
            def _():
                play(actions)

    def one_call(call, carry):
        for at_call in range(1, CALLS):
            if OPENING.get(at_call):
                @pl.when(call == at_call)
                def _():
                    play(OPENING[at_call])

        def cut(index, carry):
            start = index * 64
            rows = pl.ds(pl.multiple_of(start, 64), 64)
            upper, lower = split(stack[call, rows, :])
            travel[rows, :] = upper
            travel[pl.ds(pl.multiple_of(STACK + start, 64), 64), :] = lower
            travel[pl.ds(pl.multiple_of(2 * STACK + start, 64), 64), :] = upper
            sums[call, rows, :] = jnp.zeros((64, AUX), F32)
            return carry

        lax.fori_loop(0, STACK // 64, cut, 0)

        def pair_tile(index, carry):
            rows = pl.ds(pl.multiple_of(index * TILE, TILE), TILE)
            upper = high[rows, :]
            near = travel[pl.ds(0, STACK), :]
            pair = lax.dot_general(upper, near, NT, preferred_element_type=F32)
            pair += lax.dot_general(upper, travel[pl.ds(STACK, STACK), :], NT, preferred_element_type=F32)
            pair += lax.dot_general(low[rows, :], near, NT, preferred_element_type=F32)
            big, small = split(pair / (row_part[rows, :] + column_part[call]))
            amp[rows, pl.ds(0, STACK)] = big
            amp[rows, pl.ds(STACK, STACK)] = big
            amp[rows, pl.ds(2 * STACK, STACK)] = small
            run(call, 0, index)
            return carry

        lax.fori_loop(0, TILES, pair_tile, 0)

        def back_tile(index, carry):
            rows = pl.ds(pl.multiple_of(index * TILE, TILE), TILE)
            upper = high[rows, :]
            big = amp[rows, pl.ds(0, STACK)]
            back = lax.dot_general(big, upper, TN, preferred_element_type=F32)
            back += lax.dot_general(big, low[rows, :], TN, preferred_element_type=F32)
            back += lax.dot_general(amp[rows, pl.ds(2 * STACK, STACK)], upper, TN, preferred_element_type=F32)
            sums[call] += back
            run(call, 1, index)
            return carry

        lax.fori_loop(0, TILES, back_tile, 0)

        def own_tile(index, carry):
            rows = pl.ds(pl.multiple_of(index * TILE, TILE), TILE)
            held = pl.ds(index * (TILE // WIDTH), TILE // WIDTH)
            forward = jnp.dot(amp[rows, :], travel[...], preferred_element_type=F32)
            total[held] += forward.reshape(TILE // WIDTH, WIDTH, AUX)
            run(call, 2, index)
            return carry

        lax.fori_loop(0, TILES, own_tile, 0)
        return carry

    lax.fori_loop(0, CALLS, one_call, 0)

    give = remote(total.at[pl.ds(OWN, OWN)], other, own_sem.at[0], own_sem.at[1], twin)
    give.start()
    play(OPENING[4])
    give.wait()

    def merge(index, carry):
        total[index] += other[index]
        return carry

    lax.fori_loop(0, OWN, merge, 0)
    store = pltpu.make_async_copy(total.at[pl.ds(0, OWN)], own_out, local_sem.at[0])
    store.start()
    for step in range(1, GROUPS):
        to_group(step, group).wait_send()
    for step in range(1, BLOCKS):
        to_block(step, block).wait_send()
    for c in range(CHUNKS):
        for slot in range(SLOTS):
            for step in range(4 if c in SWAPPED else 1):
                beside(step, slot, c).wait_send()
                if c in SWAPPED:
                    trade(step, slot, c).wait_send()
            if c not in SWAPPED:
                cross(slot, c).wait_send()
            for part in parts_of(c):
                for step in range(3):
                    hop(step, slot, part, c).wait_send()
                    sum_hop(step + 1, slot, part, c).wait_send()
    for c in range(CHUNKS):
        stay(c).wait()
        pass_back(c).wait_send()
        for step in range(1, 4):
            ship(step, c, column).wait_send()
            ship(step, c, lax.rem(column + step, 4)).wait_recv()
    store.wait()


def run_main(lists, orbitals, occ, vir, held):
    smem = pl.BlockSpec(memory_space=pltpu.SMEM)
    vmem = pl.BlockSpec(memory_space=pltpu.VMEM)
    hbm = pl.BlockSpec(memory_space=pl.ANY)
    dma = pltpu.SemaphoreType.DMA
    chunk = pltpu.VMEM((GROUPS, PART, AUX), F32)
    return pl.pallas_call(
        main_kernel,
        out_shape=(
            jax.ShapeDtypeStruct((OWN, WIDTH, AUX), F32),
            jax.ShapeDtypeStruct((GROUPS, WIDTH, AUX), F32),
            jax.ShapeDtypeStruct((2, GROUPS), jnp.int32),
        ),
        in_specs=[smem, smem, smem, vmem, hbm],
        out_specs=(hbm, hbm, smem),
        scratch_shapes=[
            pltpu.VMEM((1, LANES), jnp.int32),
            pltpu.VMEM((GROUPS, 1, LANES), jnp.int32),
            pltpu.VMEM((1, LANES), F32),
            pltpu.VMEM((BLOCKS, 1, LANES), F32),
            pltpu.SMEM((GROUPS, 1, LANES), jnp.int32),
            pltpu.VMEM((ALL, AUX), BF16),
            pltpu.VMEM((ALL, AUX), BF16),
            pltpu.VMEM((2 * OWN, WIDTH, AUX), F32),
            pltpu.VMEM((CALLS, STACK, AUX), F32),
            pltpu.VMEM((3 * STACK, AUX), BF16),
            pltpu.VMEM((ALL, 3 * STACK), BF16),
            pltpu.VMEM((CALLS, STACK, AUX), F32),
            pltpu.VMEM((CALLS, 3 * STEP_ROWS, AUX), F32),
            pltpu.VMEM((SLOTS * WIDTH, AUX), F32),
            pltpu.VMEM((SLOTS * WIDTH, AUX), F32),
            pltpu.VMEM((CHUNKS, SLOTS, PART, AUX), F32),
            pltpu.VMEM((OWN, WIDTH, AUX), F32),
            pltpu.VMEM((ALL, 1), F32),
            pltpu.VMEM((4, 1, STACK), F32),
            pltpu.VMEM((CHUNKS, SLOTS, PART, AUX), F32),
            pltpu.VMEM((CHUNKS, SLOTS, PART, AUX), F32),
            pltpu.VMEM((len(SWAPPED), 4, SLOTS, PART, AUX), F32),
            dma((GROUPS,)),
            dma((GROUPS,)),
            dma((BLOCKS,)),
            dma((BLOCKS,)),
            dma((2 + CHUNKS,)),
            dma((2,)),
            dma((CHUNKS, 4)),
            dma((CHUNKS, 4)),
            dma((4, SLOTS, CHUNKS)),
            dma((4, SLOTS, CHUNKS)),
            dma((3, SLOTS, 2, CHUNKS)),
            dma((3, SLOTS, 2, CHUNKS)),
            dma((3, SLOTS, 2, CHUNKS)),
            dma((3, SLOTS, 2, CHUNKS)),
            dma((SLOTS, CHUNKS)),
            dma((SLOTS, CHUNKS)),
            dma((CHUNKS, 4)),
            dma((CHUNKS, 4)),
            dma((2,)),
            dma((CHUNKS,)),
            dma((CHUNKS,)),
            dma((CHUNKS,)),
            dma((CHUNKS,)),
            dma((len(SWAPPED), 4, SLOTS)),
            dma((len(SWAPPED), 4, SLOTS)),
        ] + [chunk] * (2 * CHUNKS),
        compiler_params=pltpu.CompilerParams(
            collective_id=0, has_side_effects=True, vmem_limit_bytes=66_000_000),
        name="main",
    )(lists, orbitals, occ, vir, held)


def join_kernel(flags, own_ref, arrived_ref, out_ref):
    out_ref[...] = own_ref[...]
    for peer in range(GROUPS):
        @pl.when(flags[1, peer] > 0)
        def _():
            out_ref[flags[0, peer]] += arrived_ref[peer]


def join(flags, own, arrived):
    height = 16
    return pl.pallas_call(
        join_kernel,
        out_shape=jax.ShapeDtypeStruct((OWN, WIDTH, AUX), F32),
        grid_spec=pltpu.PrefetchScalarGridSpec(
            num_scalar_prefetch=1,
            grid=(WIDTH // height,),
            in_specs=[
                pl.BlockSpec((OWN, height, AUX), lambda i, *_: (0, i, 0)),
                pl.BlockSpec((GROUPS, height, AUX), lambda i, *_: (0, i, 0)),
            ],
            out_specs=pl.BlockSpec((OWN, height, AUX), lambda i, *_: (0, i, 0)),
        ),
        name="join",
    )(flags, own, arrived)


def body(integrals, pair_lists, row_orbital, occ_energy, vir_energy):
    own, arrived, flags = run_main(
        pair_lists, row_orbital, occ_energy, vir_energy.reshape(1, WIDTH), integrals)
    return join(flags, own, arrived)


def solution(mesh):
    in_specs = (P("grp", "blk", None), P("grp", None), P("grp"), P(), P("blk"))
    out_specs = P("grp", "blk", None)
    return jax.shard_map(body, mesh=mesh, in_specs=in_specs, out_specs=out_specs, check_vma=False)
```

```python
import jax
import jax.numpy as jnp
from jax import lax
from jax.experimental import pallas as pl
from jax.experimental.pallas import tpu as pltpu
from jax.sharding import PartitionSpec as P

MESH = pl.DeviceIdType.MESH
F32 = jnp.float32
BF16 = jnp.bfloat16
GROUPS = 8
BLOCKS = 16
OWN = 12
SLOTS = 2
WIDTH = 64
AUX = 1536
HELD = OWN * WIDTH
ALL = 2 * HELD
CHUNKS = 8
SWAPPED = (2, 5)
HEAD = 8
PART = WIDTH // CHUNKS
CALLS = 4
PIECE = WIDTH // CALLS
STEP_ROWS = 2 * SLOTS * PIECE
STACK = 4 * STEP_ROWS
TILE = 512
TILES = ALL // TILE
LANES = 128
NT = (((1,), (1,)), ((), ()))
TN = (((0,), (0,)), ((), ()))
OPENING = {
    0: [("fetch", 0), ("fetch", 1), ("pass", 0), ("hop", 1, 0, 0), ("fetch", 2), ("pass", 1), ("side", 0, 0),
        ("hop", 2, 0, 0), ("hop", 1, 0, 1), ("fetch", 3), ("pass", 2), ("hop", 1, 1, 0), ("hop", 3, 0, 0),
        ("side", 0, 1), ("hop", 2, 0, 1), ("hop", 1, 0, 2), ("fetch", 4), ("pass", 3), ("hop", 2, 1, 0),
        ("hop", 1, 1, 1), ("side", 0, 2), ("hop", 3, 0, 1), ("hop", 2, 0, 2), ("side", 1, 2), ("fetch", 5),
        ("hop", 1, 0, 3), ("hop", 3, 1, 0), ("pass", 4), ("hop", 2, 1, 1), ("hop", 3, 0, 2), ("side", 0, 3),
        ("fetch", 6), ("hop", 2, 0, 3), ("hop", 1, 0, 4), ("side", 2, 2), ("hop", 3, 1, 1)],
    4: [("ship", 1), ("cross", 3), ("sum", 2, 7), ("home", 5), ("cross", 4), ("sum", 3, 6), ("ship", 3),
        ("sum", 3, 7), ("ship", 5), ("home", 6), ("ship", 4), ("home", 7), ("cross", 6), ("cross", 7),
        ("ship", 6), ("ship", 7)],
}
BETWEEN = {
    (0, 0, 0): [("fetch", 7), ("hop", 1, 1, 3), ("pass", 5), ("hop", 3, 0, 3)],
    (0, 0, 1): [("side", 0, 4), ("hop", 2, 0, 4)],
    (0, 0, 2): [("side", 3, 2), ("hop", 2, 1, 3)],
    (0, 1, 0): [("hop", 1, 0, 5)],
    (0, 1, 1): [("pass", 6), ("hop", 1, 1, 4), ("hop", 3, 0, 4)],
    (0, 1, 2): [("hop", 3, 1, 3), ("sum", 1, 0), ("sum", 1, 1)],
    (0, 2, 0): [("pass", 7), ("side", 0, 5), ("hop", 2, 0, 5), ("hop", 1, 0, 6)],
    (0, 2, 1): [("hop", 2, 1, 4)],
    (0, 2, 2): [("side", 1, 5)],
    (1, 0, 0): [("side", 0, 6)],
    (1, 0, 1): [("side", 0, 7), ("hop", 1, 0, 7)],
    (1, 0, 2): [("side", 2, 5), ("hop", 3, 0, 5), ("hop", 2, 0, 6)],
    (1, 1, 0): [("hop", 3, 1, 4), ("sum", 2, 0)],
    (1, 1, 1): [("hop", 1, 1, 6), ("hop", 1, 1, 7)],
    (1, 1, 2): [("side", 3, 5), ("hop", 2, 0, 7), ("swap", 0, 2), ("swap", 1, 2), ("swap", 2, 2), ("swap", 3, 2)],
    (1, 2, 0): [("hop", 3, 0, 6), ("sum", 2, 1)],
    (1, 2, 1): [("sum", 3, 0)],
    (1, 2, 2): [("hop", 2, 1, 6), ("hop", 2, 1, 7)],
    (2, 0, 0): [("hop", 3, 0, 7)],
    (2, 0, 1): [("sum", 3, 1)],
    (2, 0, 2): [("home", 0), ("sum", 1, 2)],
    (2, 1, 0): [("hop", 3, 1, 6), ("sum", 1, 3)],
    (2, 1, 1): [("hop", 3, 1, 7)],
    (2, 1, 2): [("swap", 0, 5), ("swap", 1, 5), ("swap", 2, 5), ("swap", 3, 5), ("cross", 0), ("home", 1),
        ("sum", 1, 4)],
    (2, 2, 0): [("sum", 2, 2)],
    (2, 2, 1): [("sum", 2, 3)],
    (2, 2, 2): [("sum", 2, 4)],
    (3, 0, 0): [("sum", 3, 2), ("sum", 1, 5)],
    (3, 0, 1): [("sum", 3, 3)],
    (3, 0, 2): [("sum", 3, 4)],
    (3, 1, 0): [("home", 2)],
    (3, 1, 1): [("sum", 2, 5)],
    (3, 1, 2): [("ship", 0), ("cross", 1), ("home", 3), ("sum", 1, 6), ("sum", 1, 7)],
    (3, 2, 0): [("home", 4)],
    (3, 2, 1): [("ship", 2), ("sum", 3, 5)],
    (3, 2, 2): [("sum", 2, 6)],
}


def split(values):
    high = values.astype(BF16)
    return high, (values - high.astype(F32)).astype(BF16)


def step_rows(step, slot, part, c):
    return pl.ds(step * STEP_ROWS + (slot * 2 + part) * PIECE + (c % 2) * PART, PART)


def main_kernel(
    lists_ref, orbitals_ref, occ_ref, vir_ref, held_ref,
    own_out, arrived, flags,
    ints_mine, ints_all, vir_mine, vir_all, ints,
    high, low, total, stack, travel, amp, sums, landed,
    side_send, side_land, home, other, row_part, column_part,
    near_land, near_back, swapped,
    note_sem, sent_sem, local_sem, swap_sem, box_sem, fetch_recv, side_recv, side_more,
    hop_recv, sum_recv, cross_recv, out_recv, own_sem, near_recv, far_recv, trade_recv,
    *chunks,
):
    group = lax.axis_index("grp")
    block = lax.axis_index("blk")
    column = group // 2
    upper_side = lax.rem(group, 2)
    opposite = group + 1 - 2 * upper_side
    facing = {"grp": opposite}
    core = lax.rem(block, 2)
    level = lax.rem(block // 2, 4)
    side = block // 8
    twin_block = block + 1 - 2 * core
    twin = {"blk": twin_block}
    across = {"blk": lax.rem(block + 8, 16)}
    ring = (
        {"blk": side * 8 + lax.rem(level + 1, 4) * 2 + core},
        {"blk": side * 8 + lax.rem(level + 3, 4) * 2 + core},
    )
    got, box = chunks[:CHUNKS], chunks[CHUNKS:]

    barrier = pltpu.get_barrier_semaphore()
    for step in range(1, GROUPS):
        pl.semaphore_signal(barrier, 1, device_id={"grp": lax.rem(group + step, GROUPS)}, device_id_type=MESH)
    for step in range(1, BLOCKS):
        pl.semaphore_signal(barrier, 1, device_id={"blk": lax.rem(block + step, BLOCKS)}, device_id_type=MESH)

    keep = pltpu.make_async_copy(held_ref, other, local_sem.at[0])
    keep.start()
    lane = lax.broadcasted_iota(jnp.int32, (1, LANES), 1)
    row = jnp.zeros((1, LANES), jnp.int32)
    for j in range(SLOTS):
        row = jnp.where(lane == j, lists_ref[0, j], row)
    for j in range(OWN):
        row = jnp.where(lane == SLOTS + j, orbitals_ref[j], row)
    ints_mine[...] = row
    ints_all[group] = row
    vir = vir_ref[...]
    vir_row = jnp.concatenate([vir, vir], axis=1)
    vir_mine[...] = vir_row
    vir_all[block] = vir_row
    pl.semaphore_wait(barrier, GROUPS + BLOCKS - 2)

    def remote(src, dst, send, recv, peer):
        return pltpu.make_async_remote_copy(src, dst, send, recv, device_id=peer, device_id_type=MESH)

    def drain(like, sem):
        pltpu.make_async_copy(like, like, sem).wait()

    def drain_rows(count, sem):
        if count < WIDTH:
            drain(total.at[0, pl.ds(0, count)], sem)
        else:
            drain(total.at[pl.ds(0, count // WIDTH)], sem)

    def to_group(step, slot):
        return remote(ints_mine, ints_all.at[slot], note_sem.at[0], note_sem.at[1],
                      {"grp": lax.rem(group + step, GROUPS)})

    def to_block(step, slot):
        return remote(vir_mine, vir_all.at[slot], note_sem.at[2], note_sem.at[3],
                      {"blk": lax.rem(block + step, BLOCKS)})

    for step in range(1, GROUPS):
        to_group(step, group).start()
    for step in range(1, BLOCKS):
        to_block(step, block).start()
    keep.wait()
    few, most = ints_all.at[pl.ds(0, GROUPS - 1)], vir_all.at[pl.ds(0, BLOCKS - 1)]
    drain(few, note_sem.at[1])
    to_scalar = pltpu.make_async_copy(ints_all, ints, local_sem.at[1])
    to_scalar.start()
    to_scalar.wait()

    def held_by(step, turn):
        return lax.rem(column + step, 4) * 2 + lax.rem(upper_side + turn, 2)

    for x in range(4):
        for turn in range(2):
            peer = x * 2 + lax.rem(upper_side + turn, 2)
            place = jnp.int32(0)
            found = jnp.int32(0)
            for slot in range(SLOTS):
                listed = ints[peer, 0, slot]
                match = listed // OWN == group
                place = jnp.where(match, listed % OWN, place)
                found = jnp.where(match, 1, found)
            flags[0, x * 2 + turn] = place
            flags[1, x * 2 + turn] = found

    def fetch(step, c, x):
        return remote(box[c].at[pl.ds(step * 2, 2)], got[c].at[pl.ds(x * 2, 2)],
                      box_sem.at[c], fetch_recv.at[c], {"grp": held_by(step, 0)})

    def fill(c):
        for step in range(4):
            for turn in range(2):
                values = other[flags[0, lax.rem(column + step, 4) * 2 + turn], pl.ds(c * PART, PART), :]
                if step == 0:
                    got[c][column * 2 + turn] = values
                else:
                    box[c][step * 2 + turn] = values

    fill(0)
    for c in range(CHUNKS):
        if c + 1 < CHUNKS:
            fill(c + 1)
        for step in range(1, 4):
            fetch(step, c, column).start()

    swap = remote(held_ref, total.at[pl.ds(OWN, OWN)], swap_sem.at[0], swap_sem.at[1], twin)

    def prepare(source, first):
        def tile(index, carry):
            rows = pl.ds(pl.multiple_of((first + index) * WIDTH, WIDTH), WIDTH)
            upper, lower = split(source[index + (first if source is total else 0)])
            high[rows, :] = upper
            low[rows, :] = lower
            total[first + index] = jnp.zeros((WIDTH, AUX), F32)
            return carry
        lax.fori_loop(0, OWN, tile, 0)

    prepare(other, 0)
    swap.start()

    mine = [ints[group, 0, slot] for slot in range(SLOTS)]
    theirs = [ints[opposite, 0, slot] for slot in range(SLOTS)]
    one, none = jnp.float32(1), jnp.float32(0)
    sources = [jnp.minimum(row // OWN, GROUPS - 1) for row in mine]
    columns = [source // 2 for source in sources]
    their_columns = [jnp.minimum(row // OWN, GROUPS - 1) // 2 for row in theirs]
    level_with = [jnp.where((row < GROUPS * OWN) & (lax.rem(row // OWN, 2) == upper_side), one, none) for row in mine]
    opposed = [jnp.where((row < GROUPS * OWN) & (lax.rem(row // OWN, 2) != upper_side), one, none) for row in mine]
    partner_energy = [
        occ_ref[ints[sources[slot], 0, SLOTS + mine[slot] % OWN]] for slot in range(SLOTS)
    ]
    drain(most, note_sem.at[3])
    square = (lax.broadcasted_iota(jnp.int32, (WIDTH, WIDTH), 0)
              == lax.broadcasted_iota(jnp.int32, (WIDTH, WIDTH), 1))
    for owner, place in ((block, 0), (twin_block, 1)):
        line = vir_all[owner][:, :WIDTH]
        upright = jnp.sum(jnp.where(square, line, 0.0), axis=1, keepdims=True)
        for i in range(OWN):
            energy = occ_ref[ints[group, 0, SLOTS + i]]
            row_part[pl.ds((place * OWN + i) * WIDTH, WIDTH), :] = energy - upright
    lines = []
    for step in range(4):
        for slot in range(SLOTS):
            for part in range(2):
                from_level = lax.rem(level + (4 - step if slot == 0 else step), 4)
                from_side = side + part - 2 * part * side
                lines.append(partner_energy[slot] - vir_all[from_side * 8 + from_level * 2 + core])
    for call in range(CALLS):
        pieces = [line[:, call * PIECE:(call + 1) * PIECE] for line in lines]
        column_part[call] = jnp.concatenate(pieces, axis=1)

    def side_came(step, c):
        return side_more.at[SWAPPED.index(c), step - 1] if step else side_recv.at[c]

    def beside(step, slot, c):
        came = side_came(step, c)
        return remote(stack.at[c // 2, step_rows(step, slot, 0, c)], stack.at[c // 2, step_rows(step, slot, 1, c)],
                      sent_sem.at[1], came, across)

    def hop(step, slot, part, c):
        return remote(stack.at[c // 2, step_rows(step, slot, part, c)],
                      stack.at[c // 2, step_rows(step + 1, slot, part, c)],
                      sent_sem.at[0], hop_recv.at[step, part, c], ring[slot])

    def landing(step, slot, part, c):
        return landed.at[c // 2, step_rows(step - 1, slot, part, c)]

    def sum_hop(step, slot, part, c):
        return remote(sums.at[c // 2, step_rows(step, slot, part, c)], landing(step, slot, part, c),
                      sent_sem.at[0], sum_recv.at[step - 1, part, c], ring[slot])

    def traded(step, slot, c):
        return swapped.at[SWAPPED.index(c), step, slot]

    def trade(step, slot, c):
        place = SWAPPED.index(c)
        return remote(sums.at[c // 2, step_rows(step, slot, 1, c)], traded(step, slot, c),
                      sent_sem.at[1], trade_recv.at[place, step], across)

    def side_rows(slot, c):
        return pl.ds(slot * WIDTH + c * PART, PART)

    def cross(slot, c):
        rows = side_rows(slot, c)
        return remote(side_send.at[rows], side_land.at[rows], sent_sem.at[1], cross_recv.at[c], across)

    def pass_on(c):
        return remote(box[c].at[pl.ds(0, 2)], near_land.at[c], box_sem.at[c], near_recv.at[c], facing)

    def pass_back(c):
        return remote(home.at[c], near_back.at[c], sent_sem.at[1], far_recv.at[c], facing)

    def ship(step, c, x):
        return remote(box[c].at[pl.ds(step * 2, 2)], arrived.at[pl.ds(x * 2, 2), pl.ds(c * PART, PART)],
                      sent_sem.at[1], out_recv.at[0], {"grp": held_by(step, 0)})

    def stay(c):
        return pltpu.make_async_copy(
            box[c].at[pl.ds(0, 2)], arrived.at[pl.ds(column * 2, 2), pl.ds(c * PART, PART)], local_sem.at[2 + c])

    def on_fetch(c):
        drain_rows(6 * PART, fetch_recv.at[c])
        for slot in range(SLOTS):
            box[c][slot] = got[c][their_columns[slot] * 2 + 1]
        pass_on(c).start()

    def on_pass(c):
        pass_on(c).wait_recv()
        for slot in range(SLOTS):
            stack[c // 2, step_rows(0, slot, 0, c), :] = (
                got[c][columns[slot] * 2] * level_with[slot] + near_land[c, slot] * opposed[slot])
        for slot in range(SLOTS):
            beside(0, slot, c).start()
            hop(0, slot, 0, c).start()

    def on_side(step, c):
        drain_rows(2 * PART, side_came(step, c))
        if c not in SWAPPED:
            for slot in range(SLOTS):
                hop(0, slot, 1, c).start()

    def on_hop(step, part, c):
        drain_rows(2 * PART, hop_recv.at[step - 1, part, c])
        for slot in range(SLOTS):
            if step < 3:
                hop(step, slot, part, c).start()
            if c in SWAPPED:
                beside(step, slot, c).start()

    def on_swap(step, c):
        for slot in range(SLOTS):
            trade(step, slot, c).start()

    def parts_of(c):
        return (0,) if c in SWAPPED else (1, 0)

    def on_sum(step, c):
        if c in SWAPPED:
            drain_rows(2 * PART, trade_recv.at[SWAPPED.index(c), step])
        for part in parts_of(c):
            if step > 1:
                drain_rows(2 * PART, sum_recv.at[step - 2, part, c])
            for slot in range(SLOTS):
                rows = step_rows(step, slot, part, c)
                if c in SWAPPED:
                    sums[c // 2, rows, :] += traded(step, slot, c)[...]
                if step > 1:
                    sums[c // 2, rows, :] += landing(step - 1, slot, part, c)[...]
        for part in parts_of(c):
            for slot in range(SLOTS):
                sum_hop(step, slot, part, c).start()

    def on_home(c):
        if c in SWAPPED:
            drain_rows(2 * PART, trade_recv.at[SWAPPED.index(c), 0])
        for part in parts_of(c):
            drain_rows(2 * PART, sum_recv.at[2, part, c])
            for slot in range(SLOTS):
                value = sums[c // 2, step_rows(0, slot, part, c), :] + landing(3, slot, part, c)[...]
                if part:
                    side_send[side_rows(slot, c), :] = value
                    continue
                if c in SWAPPED:
                    value += traded(0, slot, c)[...]
                home[c, slot] = value
            if part:
                for slot in range(SLOTS):
                    cross(slot, c).start()
        if c in SWAPPED:
            pass_back(c).start()

    def on_cross(c):
        drain_rows(2 * PART, cross_recv.at[c])
        for slot in range(SLOTS):
            home[c, slot] += side_land[side_rows(slot, c), :]
        pass_back(c).start()

    def on_ship(c):
        drain_rows(8 * PART, box_sem.at[c])

        def blend(rows, source, step):
            picks = [jnp.where(row // OWN == held_by(step, 0), one, none) for row in rows]
            return picks[0] * source[c, 0] + picks[1] * source[c, 1]

        for step in range(4):
            box[c][step * 2] = blend(mine, home, step)
        pass_back(c).wait_recv()
        for step in range(4):
            box[c][step * 2 + 1] = blend(theirs, near_back, step)
        for step in range(1, 4):
            ship(step, c, column).start()
        stay(c).start()

    act = {"fetch": on_fetch, "pass": on_pass, "side": on_side, "hop": on_hop, "swap": on_swap,
           "sum": on_sum, "home": on_home, "cross": on_cross, "ship": on_ship}

    def play(actions):
        for name, *where in actions:
            act[name](*where)

    play(OPENING[0][:HEAD])
    swap.wait()
    prepare(total, OWN)
    play(OPENING[0][HEAD:])

    def run(call, loop, index):
        for (at_call, at_loop, at_index), actions in BETWEEN.items():
            if at_loop != loop:
                continue

            @pl.when((call == at_call) & (index == at_index))
            def _():
                play(actions)

    def one_call(call, carry):
        for at_call in range(1, CALLS):
            if OPENING.get(at_call):
                @pl.when(call == at_call)
                def _():
                    play(OPENING[at_call])

        def cut(index, carry):
            start = index * 64
            rows = pl.ds(pl.multiple_of(start, 64), 64)
            upper, lower = split(stack[call, rows, :])
            travel[rows, :] = upper
            travel[pl.ds(pl.multiple_of(STACK + start, 64), 64), :] = lower
            travel[pl.ds(pl.multiple_of(2 * STACK + start, 64), 64), :] = upper
            sums[call, rows, :] = jnp.zeros((64, AUX), F32)
            return carry

        lax.fori_loop(0, STACK // 64, cut, 0)

        def pair_tile(index, carry):
            rows = pl.ds(pl.multiple_of(index * TILE, TILE), TILE)
            upper = high[rows, :]
            near = travel[pl.ds(0, STACK), :]
            pair = lax.dot_general(upper, near, NT, preferred_element_type=F32)
            pair += lax.dot_general(upper, travel[pl.ds(STACK, STACK), :], NT, preferred_element_type=F32)
            pair += lax.dot_general(low[rows, :], near, NT, preferred_element_type=F32)
            big, small = split(pair / (row_part[rows, :] + column_part[call]))
            amp[rows, pl.ds(0, STACK)] = big
            amp[rows, pl.ds(STACK, STACK)] = big
            amp[rows, pl.ds(2 * STACK, STACK)] = small
            run(call, 0, index)
            return carry

        lax.fori_loop(0, TILES, pair_tile, 0)

        def back_tile(index, carry):
            rows = pl.ds(pl.multiple_of(index * TILE, TILE), TILE)
            upper = high[rows, :]
            big = amp[rows, pl.ds(0, STACK)]
            back = lax.dot_general(big, upper, TN, preferred_element_type=F32)
            back += lax.dot_general(big, low[rows, :], TN, preferred_element_type=F32)
            back += lax.dot_general(amp[rows, pl.ds(2 * STACK, STACK)], upper, TN, preferred_element_type=F32)
            sums[call] += back
            run(call, 1, index)
            return carry

        lax.fori_loop(0, TILES, back_tile, 0)

        def own_tile(index, carry):
            rows = pl.ds(pl.multiple_of(index * TILE, TILE), TILE)
            held = pl.ds(index * (TILE // WIDTH), TILE // WIDTH)
            forward = jnp.dot(amp[rows, :], travel[...], preferred_element_type=F32)
            total[held] += forward.reshape(TILE // WIDTH, WIDTH, AUX)
            run(call, 2, index)
            return carry

        lax.fori_loop(0, TILES, own_tile, 0)
        return carry

    lax.fori_loop(0, CALLS, one_call, 0)

    give = remote(total.at[pl.ds(OWN, OWN)], other, own_sem.at[0], own_sem.at[1], twin)
    give.start()
    play(OPENING[4])
    give.wait()

    def merge(index, carry):
        total[index] += other[index]
        return carry

    lax.fori_loop(0, OWN, merge, 0)
    store = pltpu.make_async_copy(total.at[pl.ds(0, OWN)], own_out, local_sem.at[0])
    store.start()
    swaps = len(SWAPPED)
    ring_rows = 2 * 3 * SLOTS * PART * (2 * CHUNKS - swaps)
    other_rows = SLOTS * PART * (CHUNKS + 7 * swaps + (CHUNKS - swaps) + CHUNKS + 3 * CHUNKS)
    for c in range(CHUNKS):
        stay(c).wait()
    drain(few, note_sem.at[0])
    drain(most, note_sem.at[2])
    drain_rows(ring_rows, sent_sem.at[0])
    drain_rows(other_rows, sent_sem.at[1])
    drain_rows(3 * SLOTS * WIDTH, out_recv.at[0])
    store.wait()


def run_main(lists, orbitals, occ, vir, held):
    smem = pl.BlockSpec(memory_space=pltpu.SMEM)
    vmem = pl.BlockSpec(memory_space=pltpu.VMEM)
    hbm = pl.BlockSpec(memory_space=pl.ANY)
    dma = pltpu.SemaphoreType.DMA
    chunk = pltpu.VMEM((GROUPS, PART, AUX), F32)
    return pl.pallas_call(
        main_kernel,
        out_shape=(
            jax.ShapeDtypeStruct((OWN, WIDTH, AUX), F32),
            jax.ShapeDtypeStruct((GROUPS, WIDTH, AUX), F32),
            jax.ShapeDtypeStruct((2, GROUPS), jnp.int32),
        ),
        in_specs=[smem, smem, smem, vmem, hbm],
        out_specs=(hbm, hbm, smem),
        scratch_shapes=[
            pltpu.VMEM((1, LANES), jnp.int32),
            pltpu.VMEM((GROUPS, 1, LANES), jnp.int32),
            pltpu.VMEM((1, LANES), F32),
            pltpu.VMEM((BLOCKS, 1, LANES), F32),
            pltpu.SMEM((GROUPS, 1, LANES), jnp.int32),
            pltpu.VMEM((ALL, AUX), BF16),
            pltpu.VMEM((ALL, AUX), BF16),
            pltpu.VMEM((2 * OWN, WIDTH, AUX), F32),
            pltpu.VMEM((CALLS, STACK, AUX), F32),
            pltpu.VMEM((3 * STACK, AUX), BF16),
            pltpu.VMEM((ALL, 3 * STACK), BF16),
            pltpu.VMEM((CALLS, STACK, AUX), F32),
            pltpu.VMEM((CALLS, 3 * STEP_ROWS, AUX), F32),
            pltpu.VMEM((SLOTS * WIDTH, AUX), F32),
            pltpu.VMEM((SLOTS * WIDTH, AUX), F32),
            pltpu.VMEM((CHUNKS, SLOTS, PART, AUX), F32),
            pltpu.VMEM((OWN, WIDTH, AUX), F32),
            pltpu.VMEM((ALL, 1), F32),
            pltpu.VMEM((4, 1, STACK), F32),
            pltpu.VMEM((CHUNKS, SLOTS, PART, AUX), F32),
            pltpu.VMEM((CHUNKS, SLOTS, PART, AUX), F32),
            pltpu.VMEM((len(SWAPPED), 4, SLOTS, PART, AUX), F32),
            dma((4,)),
            dma((2,)),
            dma((2 + CHUNKS,)),
            dma((2,)),
            dma((CHUNKS,)),
            dma((CHUNKS,)),
            dma((CHUNKS,)),
            dma((len(SWAPPED), 3)),
            dma((3, 2, CHUNKS)),
            dma((3, 2, CHUNKS)),
            dma((CHUNKS,)),
            dma((1,)),
            dma((2,)),
            dma((CHUNKS,)),
            dma((CHUNKS,)),
            dma((len(SWAPPED), 4)),
        ] + [chunk] * (2 * CHUNKS),
        compiler_params=pltpu.CompilerParams(
            collective_id=0, has_side_effects=True, vmem_limit_bytes=66_000_000),
        name="main",
    )(lists, orbitals, occ, vir, held)


def join_kernel(flags, own_ref, arrived_ref, out_ref):
    out_ref[...] = own_ref[...]
    for peer in range(GROUPS):
        @pl.when(flags[1, peer] > 0)
        def _():
            out_ref[flags[0, peer]] += arrived_ref[peer]


def join(flags, own, arrived):
    height = 16
    return pl.pallas_call(
        join_kernel,
        out_shape=jax.ShapeDtypeStruct((OWN, WIDTH, AUX), F32),
        grid_spec=pltpu.PrefetchScalarGridSpec(
            num_scalar_prefetch=1,
            grid=(WIDTH // height,),
            in_specs=[
                pl.BlockSpec((OWN, height, AUX), lambda i, *_: (0, i, 0)),
                pl.BlockSpec((GROUPS, height, AUX), lambda i, *_: (0, i, 0)),
            ],
            out_specs=pl.BlockSpec((OWN, height, AUX), lambda i, *_: (0, i, 0)),
        ),
        name="join",
    )(flags, own, arrived)


def body(integrals, pair_lists, row_orbital, occ_energy, vir_energy):
    own, arrived, flags = run_main(
        pair_lists, row_orbital, occ_energy, vir_energy.reshape(1, WIDTH), integrals)
    return join(flags, own, arrived)


def solution(mesh):
    in_specs = (P("grp", "blk", None), P("grp", None), P("grp"), P(), P("blk"))
    out_specs = P("grp", "blk", None)
    return jax.shard_map(body, mesh=mesh, in_specs=in_specs, out_specs=out_specs, check_vma=False)
```

```python
import jax
import jax.numpy as jnp
from jax import lax
from jax.experimental import pallas as pl
from jax.experimental.pallas import tpu as pltpu
from jax.sharding import PartitionSpec as P

MESH = pl.DeviceIdType.MESH
F32 = jnp.float32
BF16 = jnp.bfloat16
GROUPS = 8
BLOCKS = 16
OWN = 12
SLOTS = 2
WIDTH = 64
AUX = 1536
HELD = OWN * WIDTH
ALL = 2 * HELD
CHUNKS = 8
SWAPPED = (2, 5)
HEAD = 8
PART = WIDTH // CHUNKS
CALLS = 4
PIECE = WIDTH // CALLS
STEP_ROWS = 2 * SLOTS * PIECE
STACK = 4 * STEP_ROWS
TILE = 512
TILES = ALL // TILE
LANES = 128
NT = (((1,), (1,)), ((), ()))
TN = (((0,), (0,)), ((), ()))
OPENING = {
    0: [("fetch", 0), ("fetch", 1), ("pass", 0), ("hop", 1, 0, 0), ("fetch", 2), ("hop", 3, 0, 0), ("pass", 1),
        ("side", 0, 0), ("hop", 2, 0, 0), ("hop", 1, 0, 1), ("fetch", 3), ("pass", 2), ("hop", 3, 0, 1),
        ("hop", 1, 1, 0), ("side", 0, 1), ("hop", 3, 1, 0), ("hop", 2, 0, 1), ("fetch", 4), ("pass", 3),
        ("hop", 3, 0, 2), ("side", 0, 2), ("hop", 2, 1, 0), ("hop", 1, 0, 2), ("hop", 1, 1, 1), ("fetch", 5),
        ("hop", 3, 1, 1), ("pass", 4), ("hop", 3, 0, 3), ("side", 0, 3), ("hop", 2, 0, 2), ("side", 3, 2),
        ("fetch", 6), ("hop", 2, 1, 1)],
    4: [("sum", 3, 6), ("ship", 1), ("cross", 4), ("sum", 1, 7), ("home", 5), ("ship", 3), ("sum", 3, 7),
        ("ship", 4), ("home", 6), ("ship", 5), ("cross", 6), ("home", 7), ("ship", 6), ("cross", 7), ("ship", 7)],
}
BETWEEN = {
    (0, 0, 0): [("side", 1, 2), ("hop", 1, 0, 3), ("hop", 1, 0, 4), ("hop", 3, 0, 4)],
    (0, 0, 1): [("fetch", 7), ("hop", 1, 1, 3)],
    (0, 0, 2): [("pass", 5), ("hop", 2, 0, 3), ("hop", 3, 1, 3), ("side", 0, 4)],
    (0, 1, 0): [("hop", 2, 0, 4)],
    (0, 1, 1): [("side", 2, 2), ("hop", 2, 1, 3), ("hop", 1, 0, 5)],
    (0, 1, 2): [("hop", 3, 0, 5), ("sum", 2, 0), ("sum", 1, 0)],
    (0, 2, 0): [("hop", 1, 1, 4), ("hop", 3, 1, 4)],
    (0, 2, 1): [("hop", 2, 0, 5), ("sum", 2, 1)],
    (0, 2, 2): [("side", 0, 5)],
    (1, 0, 0): [("pass", 6), ("side", 1, 5)],
    (1, 0, 1): [("pass", 7), ("hop", 2, 1, 4), ("side", 3, 5)],
    (1, 0, 2): [("side", 2, 5), ("sum", 3, 0)],
    (1, 1, 0): [("hop", 1, 0, 6)],
    (1, 1, 1): [("side", 0, 6), ("hop", 3, 0, 6), ("hop", 1, 0, 7)],
    (1, 1, 2): [("side", 0, 7), ("hop", 3, 0, 7), ("swap", 0, 2), ("swap", 1, 2), ("swap", 2, 2), ("swap", 3, 2)],
    (1, 2, 0): [("home", 0)],
    (1, 2, 1): [("hop", 2, 0, 6), ("sum", 3, 1)],
    (1, 2, 2): [("hop", 1, 1, 6), ("hop", 3, 1, 6)],
    (2, 0, 0): [("hop", 1, 1, 7), ("hop", 2, 0, 7)],
    (2, 0, 1): [("hop", 3, 1, 7), ("sum", 1, 1)],
    (2, 0, 2): [("sum", 2, 2), ("sum", 1, 2)],
    (2, 1, 0): [("hop", 2, 1, 6), ("sum", 2, 3)],
    (2, 1, 1): [("hop", 2, 1, 7), ("cross", 0)],
    (2, 1, 2): [("swap", 0, 5), ("swap", 1, 5), ("swap", 2, 5), ("swap", 3, 5), ("home", 1), ("sum", 1, 3)],
    (2, 2, 0): [("sum", 3, 2)],
    (2, 2, 1): [("sum", 2, 4)],
    (2, 2, 2): [("ship", 0), ("sum", 3, 3)],
    (3, 0, 0): [("home", 2), ("sum", 1, 4)],
    (3, 0, 1): [("sum", 1, 5)],
    (3, 0, 2): [("sum", 3, 4)],
    (3, 1, 0): [("home", 3), ("sum", 2, 5)],
    (3, 1, 1): [("cross", 1)],
    (3, 1, 2): [("sum", 2, 6), ("sum", 1, 6)],
    (3, 2, 0): [("ship", 2), ("home", 4)],
    (3, 2, 1): [("cross", 3), ("sum", 3, 5), ("sum", 2, 7)],
}


def split(values):
    high = values.astype(BF16)
    return high, (values - high.astype(F32)).astype(BF16)


def step_rows(step, slot, part, c):
    return pl.ds(step * STEP_ROWS + (slot * 2 + part) * PIECE + (c % 2) * PART, PART)


def main_kernel(
    lists_ref, orbitals_ref, occ_ref, vir_ref, held_ref,
    own_out, arrived, flags,
    ints_mine, ints_all, vir_mine, vir_all, ints,
    high, low, total, stack, travel, amp, sums, landed,
    side_send, side_land, home, other, row_part, column_part,
    near_land, near_back, swapped,
    note_sem, sent_sem, local_sem, swap_sem, box_sem, fetch_recv, side_recv, side_more,
    hop_recv, sum_recv, cross_recv, out_recv, own_sem, near_recv, far_recv, trade_recv, clear_sem,
    *chunks,
):
    group = lax.axis_index("grp")
    block = lax.axis_index("blk")
    column = group // 2
    upper_side = lax.rem(group, 2)
    opposite = group + 1 - 2 * upper_side
    facing = {"grp": opposite}
    core = lax.rem(block, 2)
    level = lax.rem(block // 2, 4)
    side = block // 8
    twin_block = block + 1 - 2 * core
    twin = {"blk": twin_block}
    across = {"blk": lax.rem(block + 8, 16)}
    ring = (
        {"blk": side * 8 + lax.rem(level + 1, 4) * 2 + core},
        {"blk": side * 8 + lax.rem(level + 3, 4) * 2 + core},
    )
    got, box = chunks[:CHUNKS], chunks[CHUNKS:]

    barrier = pltpu.get_barrier_semaphore()
    for step in range(1, GROUPS):
        pl.semaphore_signal(barrier, 1, device_id={"grp": lax.rem(group + step, GROUPS)}, device_id_type=MESH)
    for step in range(1, BLOCKS):
        pl.semaphore_signal(barrier, 1, device_id={"blk": lax.rem(block + step, BLOCKS)}, device_id_type=MESH)

    keep = pltpu.make_async_copy(held_ref, other, local_sem.at[0])
    keep.start()
    lane = lax.broadcasted_iota(jnp.int32, (1, LANES), 1)
    row = jnp.zeros((1, LANES), jnp.int32)
    for j in range(SLOTS):
        row = jnp.where(lane == j, lists_ref[0, j], row)
    for j in range(OWN):
        row = jnp.where(lane == SLOTS + j, orbitals_ref[j], row)
    ints_mine[...] = row
    ints_all[group] = row
    vir = vir_ref[...]
    vir_row = jnp.concatenate([vir, vir], axis=1)
    vir_mine[...] = vir_row
    vir_all[block] = vir_row
    pl.semaphore_wait(barrier, GROUPS + BLOCKS - 2)

    def remote(src, dst, send, recv, peer):
        return pltpu.make_async_remote_copy(src, dst, send, recv, device_id=peer, device_id_type=MESH)

    swap = remote(held_ref, total.at[pl.ds(OWN, OWN)], swap_sem.at[0], swap_sem.at[1], twin)

    def drain(like, sem):
        pltpu.make_async_copy(like, like, sem).wait()

    def drain_rows(count, sem):
        if count < WIDTH:
            drain(total.at[0, pl.ds(0, count)], sem)
        else:
            drain(total.at[pl.ds(0, count // WIDTH)], sem)

    def to_group(step, slot):
        return remote(ints_mine, ints_all.at[slot], note_sem.at[0], note_sem.at[1],
                      {"grp": lax.rem(group + step, GROUPS)})

    def to_block(step, slot):
        return remote(vir_mine, vir_all.at[slot], note_sem.at[2], note_sem.at[3],
                      {"blk": lax.rem(block + step, BLOCKS)})

    for step in range(1, GROUPS):
        to_group(step, group).start()
    for step in range(1, BLOCKS):
        to_block(step, block).start()
    swap.start()
    keep.wait()
    few, most = ints_all.at[pl.ds(0, GROUPS - 1)], vir_all.at[pl.ds(0, BLOCKS - 1)]
    drain(few, note_sem.at[1])
    to_scalar = pltpu.make_async_copy(ints_all, ints, local_sem.at[1])
    to_scalar.start()
    to_scalar.wait()

    def held_by(step, turn):
        return lax.rem(column + step, 4) * 2 + lax.rem(upper_side + turn, 2)

    for x in range(4):
        for turn in range(2):
            peer = x * 2 + lax.rem(upper_side + turn, 2)
            place = jnp.int32(0)
            found = jnp.int32(0)
            for slot in range(SLOTS):
                listed = ints[peer, 0, slot]
                match = listed // OWN == group
                place = jnp.where(match, listed % OWN, place)
                found = jnp.where(match, 1, found)
            flags[0, x * 2 + turn] = place
            flags[1, x * 2 + turn] = found

    def fetch(step, c, x):
        return remote(box[c].at[pl.ds(step * 2, 2)], got[c].at[pl.ds(x * 2, 2)],
                      box_sem.at[c], fetch_recv.at[c], {"grp": held_by(step, 0)})

    def fill(c):
        for step in range(4):
            for turn in range(2):
                values = other[flags[0, lax.rem(column + step, 4) * 2 + turn], pl.ds(c * PART, PART), :]
                if step == 0:
                    got[c][column * 2 + turn] = values
                else:
                    box[c][step * 2 + turn] = values

    fill(0)
    for c in range(CHUNKS):
        if c + 1 < CHUNKS:
            fill(c + 1)
        for step in range(1, 4):
            fetch(step, c, column).start()

    def prepare(source, first):
        def tile(index, carry):
            rows = pl.ds(pl.multiple_of((first + index) * WIDTH, WIDTH), WIDTH)
            upper, lower = split(source[index + (first if source is total else 0)])
            high[rows, :] = upper
            low[rows, :] = lower
            total[first + index] = jnp.zeros((WIDTH, AUX), F32)
            return carry
        lax.fori_loop(0, OWN, tile, 0)

    prepare(other, 0)
    pl.semaphore_signal(clear_sem, 1, device_id=twin, device_id_type=MESH)

    mine = [ints[group, 0, slot] for slot in range(SLOTS)]
    theirs = [ints[opposite, 0, slot] for slot in range(SLOTS)]
    one, none = jnp.float32(1), jnp.float32(0)
    sources = [jnp.minimum(row // OWN, GROUPS - 1) for row in mine]
    columns = [source // 2 for source in sources]
    their_columns = [jnp.minimum(row // OWN, GROUPS - 1) // 2 for row in theirs]
    level_with = [jnp.where((row < GROUPS * OWN) & (lax.rem(row // OWN, 2) == upper_side), one, none) for row in mine]
    opposed = [jnp.where((row < GROUPS * OWN) & (lax.rem(row // OWN, 2) != upper_side), one, none) for row in mine]
    partner_energy = [
        occ_ref[ints[sources[slot], 0, SLOTS + mine[slot] % OWN]] for slot in range(SLOTS)
    ]
    drain(most, note_sem.at[3])
    square = (lax.broadcasted_iota(jnp.int32, (WIDTH, WIDTH), 0)
              == lax.broadcasted_iota(jnp.int32, (WIDTH, WIDTH), 1))
    for owner, place in ((block, 0), (twin_block, 1)):
        line = vir_all[owner][:, :WIDTH]
        upright = jnp.sum(jnp.where(square, line, 0.0), axis=1, keepdims=True)
        for i in range(OWN):
            energy = occ_ref[ints[group, 0, SLOTS + i]]
            row_part[pl.ds((place * OWN + i) * WIDTH, WIDTH), :] = energy - upright
    lines = []
    for step in range(4):
        for slot in range(SLOTS):
            for part in range(2):
                from_level = lax.rem(level + (4 - step if slot == 0 else step), 4)
                from_side = side + part - 2 * part * side
                lines.append(partner_energy[slot] - vir_all[from_side * 8 + from_level * 2 + core])
    for call in range(CALLS):
        pieces = [line[:, call * PIECE:(call + 1) * PIECE] for line in lines]
        column_part[call] = jnp.concatenate(pieces, axis=1)

    def side_came(step, c):
        return side_more.at[SWAPPED.index(c), step - 1] if step else side_recv.at[c]

    def beside(step, slot, c):
        came = side_came(step, c)
        return remote(stack.at[c // 2, step_rows(step, slot, 0, c)], stack.at[c // 2, step_rows(step, slot, 1, c)],
                      sent_sem.at[1], came, across)

    def hop(step, slot, part, c):
        source = 1 if step == 2 else 0
        return remote(stack.at[c // 2, step_rows(source, slot, part, c)],
                      stack.at[c // 2, step_rows(step, slot, part, c)],
                      sent_sem.at[0], hop_recv.at[step - 1, part, c], ring[1 - slot if step == 3 else slot])

    def landing(step, slot, part, c):
        return landed.at[c // 2, step_rows(step - 1, slot, part, c)]

    def sum_hop(step, slot, part, c):
        return remote(sums.at[c // 2, step_rows(step, slot, part, c)], landing(step, slot, part, c),
                      sent_sem.at[0], sum_recv.at[step - 1, part, c], ring[1 - slot if step == 1 else slot])

    def traded(step, slot, c):
        return swapped.at[SWAPPED.index(c), step, slot]

    def trade(step, slot, c):
        place = SWAPPED.index(c)
        return remote(sums.at[c // 2, step_rows(step, slot, 1, c)], traded(step, slot, c),
                      sent_sem.at[1], trade_recv.at[place, step], across)

    def side_rows(slot, c):
        return pl.ds(slot * WIDTH + c * PART, PART)

    def cross(slot, c):
        rows = side_rows(slot, c)
        return remote(side_send.at[rows], side_land.at[rows], sent_sem.at[1], cross_recv.at[c], across)

    def pass_on(c):
        return remote(box[c].at[pl.ds(0, 2)], near_land.at[c], box_sem.at[c], near_recv.at[c], facing)

    def pass_back(c):
        return remote(home.at[c], near_back.at[c], sent_sem.at[1], far_recv.at[c], facing)

    def ship(step, c, x):
        return remote(box[c].at[pl.ds(step * 2, 2)], arrived.at[pl.ds(x * 2, 2), pl.ds(c * PART, PART)],
                      sent_sem.at[1], out_recv.at[0], {"grp": held_by(step, 0)})

    def stay(c):
        return pltpu.make_async_copy(
            box[c].at[pl.ds(0, 2)], arrived.at[pl.ds(column * 2, 2), pl.ds(c * PART, PART)], local_sem.at[2 + c])

    def on_fetch(c):
        drain_rows(6 * PART, fetch_recv.at[c])
        for slot in range(SLOTS):
            box[c][slot] = got[c][their_columns[slot] * 2 + 1]
        pass_on(c).start()

    def on_pass(c):
        pass_on(c).wait_recv()
        for slot in range(SLOTS):
            stack[c // 2, step_rows(0, slot, 0, c), :] = (
                got[c][columns[slot] * 2] * level_with[slot] + near_land[c, slot] * opposed[slot])
        for slot in range(SLOTS):
            beside(0, slot, c).start()
            hop(1, slot, 0, c).start()
            hop(3, slot, 0, c).start()

    def on_side(step, c):
        drain_rows(2 * PART, side_came(step, c))
        if c not in SWAPPED:
            for slot in range(SLOTS):
                hop(1, slot, 1, c).start()
                hop(3, slot, 1, c).start()

    def on_hop(step, part, c):
        drain_rows(2 * PART, hop_recv.at[step - 1, part, c])
        for slot in range(SLOTS):
            if step == 1:
                hop(2, slot, part, c).start()
            if c in SWAPPED:
                beside(step, slot, c).start()

    def on_swap(step, c):
        for slot in range(SLOTS):
            trade(step, slot, c).start()

    def parts_of(c):
        return (0,) if c in SWAPPED else (1, 0)

    def on_sum(step, c):
        if c in SWAPPED:
            drain_rows(2 * PART, trade_recv.at[SWAPPED.index(c), step])
        for part in parts_of(c):
            if step == 3:
                drain_rows(2 * PART, sum_recv.at[1, part, c])
            for slot in range(SLOTS):
                rows = step_rows(step, slot, part, c)
                if c in SWAPPED:
                    sums[c // 2, rows, :] += traded(step, slot, c)[...]
                if step == 3:
                    sums[c // 2, rows, :] += landing(2, slot, part, c)[...]
        for part in parts_of(c):
            for slot in range(SLOTS):
                sum_hop(step, slot, part, c).start()

    def on_home(c):
        if c in SWAPPED:
            drain_rows(2 * PART, trade_recv.at[SWAPPED.index(c), 0])
        for part in parts_of(c):
            drain_rows(2 * PART, sum_recv.at[0, part, c])
            drain_rows(2 * PART, sum_recv.at[2, part, c])
            for slot in range(SLOTS):
                value = sums[c // 2, step_rows(0, slot, part, c), :] + landing(1, slot, part, c)[...]
                value += landing(3, slot, part, c)[...]
                if part:
                    side_send[side_rows(slot, c), :] = value
                    continue
                if c in SWAPPED:
                    value += traded(0, slot, c)[...]
                home[c, slot] = value
            if part:
                for slot in range(SLOTS):
                    cross(slot, c).start()
        if c in SWAPPED:
            pass_back(c).start()

    def on_cross(c):
        drain_rows(2 * PART, cross_recv.at[c])
        for slot in range(SLOTS):
            home[c, slot] += side_land[side_rows(slot, c), :]
        pass_back(c).start()

    def on_ship(c):
        drain_rows(8 * PART, box_sem.at[c])

        def blend(rows, source, step):
            picks = [jnp.where(row // OWN == held_by(step, 0), one, none) for row in rows]
            return picks[0] * source[c, 0] + picks[1] * source[c, 1]

        for step in range(4):
            box[c][step * 2] = blend(mine, home, step)
        pass_back(c).wait_recv()
        for step in range(4):
            box[c][step * 2 + 1] = blend(theirs, near_back, step)
        for step in range(1, 4):
            ship(step, c, column).start()
        stay(c).start()

    act = {"fetch": on_fetch, "pass": on_pass, "side": on_side, "hop": on_hop, "swap": on_swap,
           "sum": on_sum, "home": on_home, "cross": on_cross, "ship": on_ship}

    def play(actions):
        for name, *where in actions:
            act[name](*where)

    play(OPENING[0][:HEAD])
    swap.wait()
    prepare(total, OWN)
    play(OPENING[0][HEAD:])

    def run(call, loop, index):
        for (at_call, at_loop, at_index), actions in BETWEEN.items():
            if at_loop != loop:
                continue

            @pl.when((call == at_call) & (index == at_index))
            def _():
                play(actions)

    def one_call(call, carry):
        for at_call in range(1, CALLS):
            if OPENING.get(at_call):
                @pl.when(call == at_call)
                def _():
                    play(OPENING[at_call])

        def cut(index, carry):
            start = index * 64
            rows = pl.ds(pl.multiple_of(start, 64), 64)
            upper, lower = split(stack[call, rows, :])
            travel[rows, :] = upper
            travel[pl.ds(pl.multiple_of(STACK + start, 64), 64), :] = lower
            travel[pl.ds(pl.multiple_of(2 * STACK + start, 64), 64), :] = upper
            sums[call, rows, :] = jnp.zeros((64, AUX), F32)
            return carry

        lax.fori_loop(0, STACK // 64, cut, 0)

        def pair_tile(index, carry):
            rows = pl.ds(pl.multiple_of(index * TILE, TILE), TILE)
            upper = high[rows, :]
            near = travel[pl.ds(0, STACK), :]
            pair = lax.dot_general(upper, near, NT, preferred_element_type=F32)
            pair += lax.dot_general(upper, travel[pl.ds(STACK, STACK), :], NT, preferred_element_type=F32)
            pair += lax.dot_general(low[rows, :], near, NT, preferred_element_type=F32)
            big, small = split(pair / (row_part[rows, :] + column_part[call]))
            amp[rows, pl.ds(0, STACK)] = big
            amp[rows, pl.ds(STACK, STACK)] = big
            amp[rows, pl.ds(2 * STACK, STACK)] = small
            run(call, 0, index)
            return carry

        lax.fori_loop(0, TILES, pair_tile, 0)

        def back_tile(index, carry):
            rows = pl.ds(pl.multiple_of(index * TILE, TILE), TILE)
            upper = high[rows, :]
            big = amp[rows, pl.ds(0, STACK)]
            back = lax.dot_general(big, upper, TN, preferred_element_type=F32)
            back += lax.dot_general(big, low[rows, :], TN, preferred_element_type=F32)
            back += lax.dot_general(amp[rows, pl.ds(2 * STACK, STACK)], upper, TN, preferred_element_type=F32)
            sums[call] += back
            run(call, 1, index)
            return carry

        lax.fori_loop(0, TILES, back_tile, 0)

        def own_tile(index, carry):
            rows = pl.ds(pl.multiple_of(index * TILE, TILE), TILE)
            held = pl.ds(index * (TILE // WIDTH), TILE // WIDTH)
            forward = jnp.dot(amp[rows, :], travel[...], preferred_element_type=F32)
            total[held] += forward.reshape(TILE // WIDTH, WIDTH, AUX)
            run(call, 2, index)
            return carry

        lax.fori_loop(0, TILES, own_tile, 0)
        return carry

    lax.fori_loop(0, CALLS, one_call, 0)

    give = remote(total.at[pl.ds(OWN, OWN)], other, own_sem.at[0], own_sem.at[1], twin)
    pl.semaphore_wait(clear_sem, 1)
    give.start()
    play(OPENING[4])
    give.wait()

    def merge(index, carry):
        total[index] += other[index]
        return carry

    lax.fori_loop(0, OWN, merge, 0)
    store = pltpu.make_async_copy(total.at[pl.ds(0, OWN)], own_out, local_sem.at[0])
    store.start()
    swaps = len(SWAPPED)
    ring_rows = 2 * 3 * SLOTS * PART * (2 * CHUNKS - swaps)
    other_rows = SLOTS * PART * (CHUNKS + 7 * swaps + (CHUNKS - swaps) + CHUNKS + 3 * CHUNKS)
    for c in range(CHUNKS):
        stay(c).wait()
    drain(few, note_sem.at[0])
    drain(most, note_sem.at[2])
    drain_rows(ring_rows, sent_sem.at[0])
    drain_rows(other_rows, sent_sem.at[1])
    drain_rows(3 * SLOTS * WIDTH, out_recv.at[0])
    store.wait()


def run_main(lists, orbitals, occ, vir, held):
    smem = pl.BlockSpec(memory_space=pltpu.SMEM)
    vmem = pl.BlockSpec(memory_space=pltpu.VMEM)
    hbm = pl.BlockSpec(memory_space=pl.ANY)
    dma = pltpu.SemaphoreType.DMA
    chunk = pltpu.VMEM((GROUPS, PART, AUX), F32)
    return pl.pallas_call(
        main_kernel,
        out_shape=(
            jax.ShapeDtypeStruct((OWN, WIDTH, AUX), F32),
            jax.ShapeDtypeStruct((GROUPS, WIDTH, AUX), F32),
            jax.ShapeDtypeStruct((2, GROUPS), jnp.int32),
        ),
        in_specs=[smem, smem, smem, vmem, hbm],
        out_specs=(hbm, hbm, smem),
        scratch_shapes=[
            pltpu.VMEM((1, LANES), jnp.int32),
            pltpu.VMEM((GROUPS, 1, LANES), jnp.int32),
            pltpu.VMEM((1, LANES), F32),
            pltpu.VMEM((BLOCKS, 1, LANES), F32),
            pltpu.SMEM((GROUPS, 1, LANES), jnp.int32),
            pltpu.VMEM((ALL, AUX), BF16),
            pltpu.VMEM((ALL, AUX), BF16),
            pltpu.VMEM((2 * OWN, WIDTH, AUX), F32),
            pltpu.VMEM((CALLS, STACK, AUX), F32),
            pltpu.VMEM((3 * STACK, AUX), BF16),
            pltpu.VMEM((ALL, 3 * STACK), BF16),
            pltpu.VMEM((CALLS, STACK, AUX), F32),
            pltpu.VMEM((CALLS, 3 * STEP_ROWS, AUX), F32),
            pltpu.VMEM((SLOTS * WIDTH, AUX), F32),
            pltpu.VMEM((SLOTS * WIDTH, AUX), F32),
            pltpu.VMEM((CHUNKS, SLOTS, PART, AUX), F32),
            pltpu.VMEM((OWN, WIDTH, AUX), F32),
            pltpu.VMEM((ALL, 1), F32),
            pltpu.VMEM((4, 1, STACK), F32),
            pltpu.VMEM((CHUNKS, SLOTS, PART, AUX), F32),
            pltpu.VMEM((CHUNKS, SLOTS, PART, AUX), F32),
            pltpu.VMEM((len(SWAPPED), 4, SLOTS, PART, AUX), F32),
            dma((4,)),
            dma((2,)),
            dma((2 + CHUNKS,)),
            dma((2,)),
            dma((CHUNKS,)),
            dma((CHUNKS,)),
            dma((CHUNKS,)),
            dma((len(SWAPPED), 3)),
            dma((3, 2, CHUNKS)),
            dma((3, 2, CHUNKS)),
            dma((CHUNKS,)),
            dma((1,)),
            dma((2,)),
            dma((CHUNKS,)),
            dma((CHUNKS,)),
            dma((len(SWAPPED), 4)),
            pltpu.SemaphoreType.REGULAR,
        ] + [chunk] * (2 * CHUNKS),
        compiler_params=pltpu.CompilerParams(
            collective_id=0, has_side_effects=True, vmem_limit_bytes=66_000_000),
        name="main",
    )(lists, orbitals, occ, vir, held)


def join_kernel(flags, own_ref, arrived_ref, out_ref):
    out_ref[...] = own_ref[...]
    for peer in range(GROUPS):
        @pl.when(flags[1, peer] > 0)
        def _():
            out_ref[flags[0, peer]] += arrived_ref[peer]


def join(flags, own, arrived):
    height = 16
    return pl.pallas_call(
        join_kernel,
        out_shape=jax.ShapeDtypeStruct((OWN, WIDTH, AUX), F32),
        grid_spec=pltpu.PrefetchScalarGridSpec(
            num_scalar_prefetch=1,
            grid=(WIDTH // height,),
            in_specs=[
                pl.BlockSpec((OWN, height, AUX), lambda i, *_: (0, i, 0)),
                pl.BlockSpec((GROUPS, height, AUX), lambda i, *_: (0, i, 0)),
            ],
            out_specs=pl.BlockSpec((OWN, height, AUX), lambda i, *_: (0, i, 0)),
        ),
        name="join",
    )(flags, own, arrived)


def body(integrals, pair_lists, row_orbital, occ_energy, vir_energy):
    own, arrived, flags = run_main(
        pair_lists, row_orbital, occ_energy, vir_energy.reshape(1, WIDTH), integrals)
    return join(flags, own, arrived)


def solution(mesh):
    in_specs = (P("grp", "blk", None), P("grp", None), P("grp"), P(), P("blk"))
    out_specs = P("grp", "blk", None)
    return jax.shard_map(body, mesh=mesh, in_specs=in_specs, out_specs=out_specs, check_vma=False)
```

```python
import jax
import jax.numpy as jnp
from jax import lax
from jax.experimental import pallas as pl
from jax.experimental.pallas import tpu as pltpu
from jax.sharding import PartitionSpec as P

MESH = pl.DeviceIdType.MESH
F32 = jnp.float32
BF16 = jnp.bfloat16
GROUPS = 8
BLOCKS = 16
OWN = 12
SLOTS = 2
WIDTH = 64
AUX = 1536
HELD = OWN * WIDTH
ALL = 2 * HELD
CHUNKS = 8
SWAPPED = (2, 5)
HEAD = 8
PART = WIDTH // CHUNKS
CALLS = 4
PIECE = WIDTH // CALLS
STEP_ROWS = 2 * SLOTS * PIECE
STACK = 4 * STEP_ROWS
TILE = 512
TILES = ALL // TILE
LANES = 128
NT = (((1,), (1,)), ((), ()))
TN = (((0,), (0,)), ((), ()))
OPENING = {
    0: [("fetch", 0), ("fetch", 1), ("pass", 0), ("hop", 1, 0, 0), ("fetch", 2), ("hop", 3, 0, 0), ("pass", 1),
        ("side", 0, 0), ("hop", 2, 0, 0), ("hop", 1, 0, 1), ("fetch", 3), ("pass", 2), ("hop", 3, 0, 1),
        ("hop", 1, 1, 0), ("side", 0, 1), ("hop", 3, 1, 0), ("hop", 2, 0, 1), ("fetch", 4), ("pass", 3),
        ("hop", 3, 0, 2), ("side", 0, 2), ("hop", 2, 1, 0), ("hop", 1, 0, 2), ("hop", 1, 1, 1), ("fetch", 5),
        ("hop", 3, 1, 1), ("pass", 4), ("hop", 3, 0, 3), ("side", 0, 3), ("hop", 2, 0, 2), ("side", 3, 2),
        ("fetch", 6), ("hop", 2, 1, 1)],
    4: [("sum", 3, 6), ("ship", 1), ("cross", 4), ("sum", 1, 7), ("home", 5), ("ship", 3), ("sum", 3, 7),
        ("ship", 4), ("home", 6), ("ship", 5), ("cross", 6), ("home", 7), ("ship", 6), ("cross", 7), ("ship", 7)],
}
BETWEEN = {
    (0, 0, 0): [("side", 1, 2), ("hop", 1, 0, 3), ("hop", 1, 0, 4), ("hop", 3, 0, 4)],
    (0, 0, 1): [("fetch", 7), ("hop", 1, 1, 3)],
    (0, 0, 2): [("pass", 5), ("hop", 2, 0, 3), ("hop", 3, 1, 3), ("side", 0, 4)],
    (0, 1, 0): [("hop", 2, 0, 4)],
    (0, 1, 1): [("side", 2, 2), ("hop", 2, 1, 3), ("hop", 1, 0, 5)],
    (0, 1, 2): [("hop", 3, 0, 5), ("sum", 2, 0), ("sum", 1, 0)],
    (0, 2, 0): [("hop", 1, 1, 4), ("hop", 3, 1, 4)],
    (0, 2, 1): [("hop", 2, 0, 5), ("sum", 2, 1)],
    (0, 2, 2): [("side", 0, 5)],
    (1, 0, 0): [("pass", 6), ("side", 1, 5)],
    (1, 0, 1): [("pass", 7), ("hop", 2, 1, 4), ("side", 3, 5)],
    (1, 0, 2): [("side", 2, 5), ("sum", 3, 0)],
    (1, 1, 0): [("hop", 1, 0, 6)],
    (1, 1, 1): [("side", 0, 6), ("hop", 3, 0, 6), ("hop", 1, 0, 7)],
    (1, 1, 2): [("side", 0, 7), ("hop", 3, 0, 7), ("swap", 0, 2), ("swap", 1, 2), ("swap", 2, 2), ("swap", 3, 2)],
    (1, 2, 0): [("home", 0)],
    (1, 2, 1): [("hop", 2, 0, 6), ("sum", 3, 1)],
    (1, 2, 2): [("hop", 1, 1, 6), ("hop", 3, 1, 6)],
    (2, 0, 0): [("hop", 1, 1, 7), ("hop", 2, 0, 7)],
    (2, 0, 1): [("hop", 3, 1, 7), ("sum", 1, 1)],
    (2, 0, 2): [("sum", 2, 2), ("sum", 1, 2)],
    (2, 1, 0): [("hop", 2, 1, 6), ("sum", 2, 3)],
    (2, 1, 1): [("hop", 2, 1, 7), ("cross", 0)],
    (2, 1, 2): [("swap", 0, 5), ("swap", 1, 5), ("swap", 2, 5), ("swap", 3, 5), ("home", 1), ("sum", 1, 3)],
    (2, 2, 0): [("sum", 3, 2)],
    (2, 2, 1): [("sum", 2, 4)],
    (2, 2, 2): [("ship", 0), ("sum", 3, 3)],
    (3, 0, 0): [("home", 2), ("sum", 1, 4)],
    (3, 0, 1): [("sum", 1, 5)],
    (3, 0, 2): [("sum", 3, 4)],
    (3, 1, 0): [("home", 3), ("sum", 2, 5)],
    (3, 1, 1): [("cross", 1)],
    (3, 1, 2): [("sum", 2, 6), ("sum", 1, 6)],
    (3, 2, 0): [("ship", 2), ("home", 4)],
    (3, 2, 1): [("cross", 3), ("sum", 3, 5), ("sum", 2, 7)],
}


def split(values):
    high = values.astype(BF16)
    return high, (values - high.astype(F32)).astype(BF16)


def step_rows(step, slot, part, c):
    return pl.ds(step * STEP_ROWS + (slot * 2 + part) * PIECE + (c % 2) * PART, PART)


def main_kernel(
    lists_ref, orbitals_ref, occ_ref, vir_ref, held_ref,
    other,
    ints_mine, ints_all, vir_mine, vir_all, ints,
    high, low, total, stack, travel, amp, sums, landed,
    side_send, side_land, home, row_part, column_part,
    near_land, near_back, swapped, came, flags,
    note_sem, sent_sem, local_sem, swap_sem, box_sem, fetch_recv, side_recv, side_more,
    hop_recv, sum_recv, cross_recv, out_recv, own_sem, near_recv, far_recv, trade_recv, clear_sem,
    *chunks,
):
    group = lax.axis_index("grp")
    block = lax.axis_index("blk")
    column = group // 2
    upper_side = lax.rem(group, 2)
    opposite = group + 1 - 2 * upper_side
    facing = {"grp": opposite}
    core = lax.rem(block, 2)
    level = lax.rem(block // 2, 4)
    side = block // 8
    twin_block = block + 1 - 2 * core
    twin = {"blk": twin_block}
    across = {"blk": lax.rem(block + 8, 16)}
    ring = (
        {"blk": side * 8 + lax.rem(level + 1, 4) * 2 + core},
        {"blk": side * 8 + lax.rem(level + 3, 4) * 2 + core},
    )
    got, box = chunks[:CHUNKS], chunks[CHUNKS:]

    barrier = pltpu.get_barrier_semaphore()
    for step in range(1, GROUPS):
        pl.semaphore_signal(barrier, 1, device_id={"grp": lax.rem(group + step, GROUPS)}, device_id_type=MESH)
    for step in range(1, BLOCKS):
        pl.semaphore_signal(barrier, 1, device_id={"blk": lax.rem(block + step, BLOCKS)}, device_id_type=MESH)

    keep = pltpu.make_async_copy(held_ref, other, local_sem.at[0])
    keep.start()
    lane = lax.broadcasted_iota(jnp.int32, (1, LANES), 1)
    row = jnp.zeros((1, LANES), jnp.int32)
    for j in range(SLOTS):
        row = jnp.where(lane == j, lists_ref[0, j], row)
    for j in range(OWN):
        row = jnp.where(lane == SLOTS + j, orbitals_ref[j], row)
    ints_mine[...] = row
    ints_all[group] = row
    vir = vir_ref[...]
    vir_row = jnp.concatenate([vir, vir], axis=1)
    vir_mine[...] = vir_row
    vir_all[block] = vir_row
    pl.semaphore_wait(barrier, GROUPS + BLOCKS - 2)

    def remote(src, dst, send, recv, peer):
        return pltpu.make_async_remote_copy(src, dst, send, recv, device_id=peer, device_id_type=MESH)

    swap = remote(held_ref, total.at[pl.ds(OWN, OWN)], swap_sem.at[0], swap_sem.at[1], twin)

    def drain(like, sem):
        pltpu.make_async_copy(like, like, sem).wait()

    def drain_rows(count, sem):
        if count < WIDTH:
            drain(total.at[0, pl.ds(0, count)], sem)
        else:
            drain(total.at[pl.ds(0, count // WIDTH)], sem)

    def to_group(step, slot):
        return remote(ints_mine, ints_all.at[slot], note_sem.at[0], note_sem.at[1],
                      {"grp": lax.rem(group + step, GROUPS)})

    def to_block(step, slot):
        return remote(vir_mine, vir_all.at[slot], note_sem.at[2], note_sem.at[3],
                      {"blk": lax.rem(block + step, BLOCKS)})

    for step in range(1, GROUPS):
        to_group(step, group).start()
    for step in range(1, BLOCKS):
        to_block(step, block).start()
    swap.start()
    keep.wait()
    few, most = ints_all.at[pl.ds(0, GROUPS - 1)], vir_all.at[pl.ds(0, BLOCKS - 1)]
    drain(few, note_sem.at[1])
    to_scalar = pltpu.make_async_copy(ints_all, ints, local_sem.at[1])
    to_scalar.start()
    to_scalar.wait()

    def held_by(step, turn):
        return lax.rem(column + step, 4) * 2 + lax.rem(upper_side + turn, 2)

    for x in range(4):
        for turn in range(2):
            peer = x * 2 + lax.rem(upper_side + turn, 2)
            place = jnp.int32(0)
            found = jnp.int32(0)
            for slot in range(SLOTS):
                listed = ints[peer, 0, slot]
                match = listed // OWN == group
                place = jnp.where(match, listed % OWN, place)
                found = jnp.where(match, 1, found)
            flags[0, x * 2 + turn] = place
            flags[1, x * 2 + turn] = found

    def fetch(step, c, x):
        return remote(box[c].at[pl.ds(step * 2, 2)], got[c].at[pl.ds(x * 2, 2)],
                      box_sem.at[c], fetch_recv.at[c], {"grp": held_by(step, 0)})

    def fill(c):
        for step in range(4):
            for turn in range(2):
                values = other[flags[0, lax.rem(column + step, 4) * 2 + turn], pl.ds(c * PART, PART), :]
                if step == 0:
                    got[c][column * 2 + turn] = values
                else:
                    box[c][step * 2 + turn] = values

    fill(0)
    for c in range(CHUNKS):
        if c + 1 < CHUNKS:
            fill(c + 1)
        for step in range(1, 4):
            fetch(step, c, column).start()

    def prepare(source, first):
        def tile(index, carry):
            rows = pl.ds(pl.multiple_of((first + index) * WIDTH, WIDTH), WIDTH)
            upper, lower = split(source[index + (first if source is total else 0)])
            high[rows, :] = upper
            low[rows, :] = lower
            total[first + index] = jnp.zeros((WIDTH, AUX), F32)
            return carry
        lax.fori_loop(0, OWN, tile, 0)

    prepare(other, 0)
    pl.semaphore_signal(clear_sem, 1, device_id=twin, device_id_type=MESH)

    mine = [ints[group, 0, slot] for slot in range(SLOTS)]
    theirs = [ints[opposite, 0, slot] for slot in range(SLOTS)]
    one, none = jnp.float32(1), jnp.float32(0)
    sources = [jnp.minimum(row // OWN, GROUPS - 1) for row in mine]
    columns = [source // 2 for source in sources]
    their_columns = [jnp.minimum(row // OWN, GROUPS - 1) // 2 for row in theirs]
    level_with = [jnp.where((row < GROUPS * OWN) & (lax.rem(row // OWN, 2) == upper_side), one, none) for row in mine]
    opposed = [jnp.where((row < GROUPS * OWN) & (lax.rem(row // OWN, 2) != upper_side), one, none) for row in mine]
    partner_energy = [
        occ_ref[ints[sources[slot], 0, SLOTS + mine[slot] % OWN]] for slot in range(SLOTS)
    ]
    drain(most, note_sem.at[3])
    square = (lax.broadcasted_iota(jnp.int32, (WIDTH, WIDTH), 0)
              == lax.broadcasted_iota(jnp.int32, (WIDTH, WIDTH), 1))
    for owner, place in ((block, 0), (twin_block, 1)):
        line = vir_all[owner][:, :WIDTH]
        upright = jnp.sum(jnp.where(square, line, 0.0), axis=1, keepdims=True)
        for i in range(OWN):
            energy = occ_ref[ints[group, 0, SLOTS + i]]
            row_part[pl.ds((place * OWN + i) * WIDTH, WIDTH), :] = energy - upright
    lines = []
    for step in range(4):
        for slot in range(SLOTS):
            for part in range(2):
                from_level = lax.rem(level + (4 - step if slot == 0 else step), 4)
                from_side = side + part - 2 * part * side
                lines.append(partner_energy[slot] - vir_all[from_side * 8 + from_level * 2 + core])
    for call in range(CALLS):
        pieces = [line[:, call * PIECE:(call + 1) * PIECE] for line in lines]
        column_part[call] = jnp.concatenate(pieces, axis=1)

    def side_came(step, c):
        return side_more.at[SWAPPED.index(c), step - 1] if step else side_recv.at[c]

    def beside(step, slot, c):
        came = side_came(step, c)
        return remote(stack.at[c // 2, step_rows(step, slot, 0, c)], stack.at[c // 2, step_rows(step, slot, 1, c)],
                      sent_sem.at[1], came, across)

    def hop(step, slot, part, c):
        source = 1 if step == 2 else 0
        return remote(stack.at[c // 2, step_rows(source, slot, part, c)],
                      stack.at[c // 2, step_rows(step, slot, part, c)],
                      sent_sem.at[0], hop_recv.at[step - 1, part, c], ring[1 - slot if step == 3 else slot])

    def landing(step, slot, part, c):
        return landed.at[c // 2, step_rows(step - 1, slot, part, c)]

    def sum_hop(step, slot, part, c):
        return remote(sums.at[c // 2, step_rows(step, slot, part, c)], landing(step, slot, part, c),
                      sent_sem.at[0], sum_recv.at[step - 1, part, c], ring[1 - slot if step == 1 else slot])

    def traded(step, slot, c):
        return swapped.at[SWAPPED.index(c), step, slot]

    def trade(step, slot, c):
        place = SWAPPED.index(c)
        return remote(sums.at[c // 2, step_rows(step, slot, 1, c)], traded(step, slot, c),
                      sent_sem.at[1], trade_recv.at[place, step], across)

    def side_rows(slot, c):
        return pl.ds(slot * WIDTH + c * PART, PART)

    def cross(slot, c):
        rows = side_rows(slot, c)
        return remote(side_send.at[rows], side_land.at[rows], sent_sem.at[1], cross_recv.at[c], across)

    def pass_on(c):
        return remote(box[c].at[pl.ds(0, 2)], near_land.at[c], box_sem.at[c], near_recv.at[c], facing)

    def pass_back(c):
        return remote(home.at[c], near_back.at[c], sent_sem.at[1], far_recv.at[c], facing)

    def ship(step, c, x):
        return remote(box[c].at[pl.ds(step * 2, 2)], came.at[c, pl.ds(x * 2, 2)],
                      sent_sem.at[1], out_recv.at[c], {"grp": held_by(step, 0)})

    def on_fetch(c):
        drain_rows(6 * PART, fetch_recv.at[c])
        for slot in range(SLOTS):
            box[c][slot] = got[c][their_columns[slot] * 2 + 1]
        pass_on(c).start()

    def on_pass(c):
        pass_on(c).wait_recv()
        for slot in range(SLOTS):
            stack[c // 2, step_rows(0, slot, 0, c), :] = (
                got[c][columns[slot] * 2] * level_with[slot] + near_land[c, slot] * opposed[slot])
        for slot in range(SLOTS):
            beside(0, slot, c).start()
            hop(1, slot, 0, c).start()
            hop(3, slot, 0, c).start()

    def on_side(step, c):
        drain_rows(2 * PART, side_came(step, c))
        if c not in SWAPPED:
            for slot in range(SLOTS):
                hop(1, slot, 1, c).start()
                hop(3, slot, 1, c).start()

    def on_hop(step, part, c):
        drain_rows(2 * PART, hop_recv.at[step - 1, part, c])
        for slot in range(SLOTS):
            if step == 1:
                hop(2, slot, part, c).start()
            if c in SWAPPED:
                beside(step, slot, c).start()

    def on_swap(step, c):
        for slot in range(SLOTS):
            trade(step, slot, c).start()

    def parts_of(c):
        return (0,) if c in SWAPPED else (1, 0)

    def on_sum(step, c):
        if c in SWAPPED:
            drain_rows(2 * PART, trade_recv.at[SWAPPED.index(c), step])
        for part in parts_of(c):
            if step == 3:
                drain_rows(2 * PART, sum_recv.at[1, part, c])
            for slot in range(SLOTS):
                rows = step_rows(step, slot, part, c)
                if c in SWAPPED:
                    sums[c // 2, rows, :] += traded(step, slot, c)[...]
                if step == 3:
                    sums[c // 2, rows, :] += landing(2, slot, part, c)[...]
        for part in parts_of(c):
            for slot in range(SLOTS):
                sum_hop(step, slot, part, c).start()

    def on_home(c):
        if c in SWAPPED:
            drain_rows(2 * PART, trade_recv.at[SWAPPED.index(c), 0])
        for part in parts_of(c):
            drain_rows(2 * PART, sum_recv.at[0, part, c])
            drain_rows(2 * PART, sum_recv.at[2, part, c])
            for slot in range(SLOTS):
                value = sums[c // 2, step_rows(0, slot, part, c), :] + landing(1, slot, part, c)[...]
                value += landing(3, slot, part, c)[...]
                if part:
                    side_send[side_rows(slot, c), :] = value
                    continue
                if c in SWAPPED:
                    value += traded(0, slot, c)[...]
                home[c, slot] = value
            if part:
                for slot in range(SLOTS):
                    cross(slot, c).start()
        if c in SWAPPED:
            pass_back(c).start()

    def on_cross(c):
        drain_rows(2 * PART, cross_recv.at[c])
        for slot in range(SLOTS):
            home[c, slot] += side_land[side_rows(slot, c), :]
        pass_back(c).start()

    def on_ship(c):
        drain_rows(8 * PART, box_sem.at[c])

        def blend(rows, source, step):
            picks = [jnp.where(row // OWN == held_by(step, 0), one, none) for row in rows]
            return picks[0] * source[c, 0] + picks[1] * source[c, 1]

        def place(step, turn, values):
            if step:
                box[c][step * 2 + turn] = values
            else:
                came[c, column * 2 + turn] = values

        for step in range(4):
            place(step, 0, blend(mine, home, step))
        drain_rows(2 * PART, far_recv.at[c])
        for step in range(4):
            place(step, 1, blend(theirs, near_back, step))
        for step in range(1, 4):
            ship(step, c, column).start()

    def finish(c):
        drain_rows(6 * PART, out_recv.at[c])
        rows = pl.ds(c * PART, PART)

        def add(index, carry):
            value = total[index, rows, :] + other[index, rows, :]
            for peer in range(GROUPS):
                here = (flags[0, peer] == index) & (flags[1, peer] > 0)
                value += jnp.where(here, one, none) * came[c, peer]
            other[index, rows, :] = value
            return carry

        lax.fori_loop(0, OWN, add, 0)

    act = {"fetch": on_fetch, "pass": on_pass, "side": on_side, "hop": on_hop, "swap": on_swap,
           "sum": on_sum, "home": on_home, "cross": on_cross, "ship": on_ship}

    def play(actions):
        for name, *where in actions:
            act[name](*where)

    play(OPENING[0][:HEAD])
    swap.wait()
    prepare(total, OWN)
    play(OPENING[0][HEAD:])

    def run(call, loop, index):
        for (at_call, at_loop, at_index), actions in BETWEEN.items():
            if at_loop != loop:
                continue

            @pl.when((call == at_call) & (index == at_index))
            def _():
                play(actions)

    def one_call(call, carry):
        for at_call in range(1, CALLS):
            if OPENING.get(at_call):
                @pl.when(call == at_call)
                def _():
                    play(OPENING[at_call])

        def cut(index, carry):
            start = index * 64
            rows = pl.ds(pl.multiple_of(start, 64), 64)
            upper, lower = split(stack[call, rows, :])
            travel[rows, :] = upper
            travel[pl.ds(pl.multiple_of(STACK + start, 64), 64), :] = lower
            travel[pl.ds(pl.multiple_of(2 * STACK + start, 64), 64), :] = upper
            sums[call, rows, :] = jnp.zeros((64, AUX), F32)
            return carry

        lax.fori_loop(0, STACK // 64, cut, 0)

        def pair_tile(index, carry):
            rows = pl.ds(pl.multiple_of(index * TILE, TILE), TILE)
            upper = high[rows, :]
            near = travel[pl.ds(0, STACK), :]
            pair = lax.dot_general(upper, near, NT, preferred_element_type=F32)
            pair += lax.dot_general(upper, travel[pl.ds(STACK, STACK), :], NT, preferred_element_type=F32)
            pair += lax.dot_general(low[rows, :], near, NT, preferred_element_type=F32)
            big, small = split(pair / (row_part[rows, :] + column_part[call]))
            amp[rows, pl.ds(0, STACK)] = big
            amp[rows, pl.ds(STACK, STACK)] = big
            amp[rows, pl.ds(2 * STACK, STACK)] = small
            run(call, 0, index)
            return carry

        lax.fori_loop(0, TILES, pair_tile, 0)

        def back_tile(index, carry):
            rows = pl.ds(pl.multiple_of(index * TILE, TILE), TILE)
            upper = high[rows, :]
            big = amp[rows, pl.ds(0, STACK)]
            back = lax.dot_general(big, upper, TN, preferred_element_type=F32)
            back += lax.dot_general(big, low[rows, :], TN, preferred_element_type=F32)
            back += lax.dot_general(amp[rows, pl.ds(2 * STACK, STACK)], upper, TN, preferred_element_type=F32)
            sums[call] += back
            run(call, 1, index)
            return carry

        lax.fori_loop(0, TILES, back_tile, 0)

        def own_tile(index, carry):
            rows = pl.ds(pl.multiple_of(index * TILE, TILE), TILE)
            held = pl.ds(index * (TILE // WIDTH), TILE // WIDTH)
            forward = jnp.dot(amp[rows, :], travel[...], preferred_element_type=F32)
            total[held] += forward.reshape(TILE // WIDTH, WIDTH, AUX)
            run(call, 2, index)
            return carry

        lax.fori_loop(0, TILES, own_tile, 0)
        return carry

    lax.fori_loop(0, CALLS, one_call, 0)

    give = remote(total.at[pl.ds(OWN, OWN)], other, own_sem.at[0], own_sem.at[1], twin)
    pl.semaphore_wait(clear_sem, 1)
    give.start()
    play(OPENING[4])
    give.wait()

    order = [place for name, place in [event[:2] for event in OPENING[4]] if name == "ship"]
    order = [c for c in range(CHUNKS) if c not in order] + order
    for c in order:
        finish(c)
    swaps = len(SWAPPED)
    ring_rows = 2 * 3 * SLOTS * PART * (2 * CHUNKS - swaps)
    other_rows = SLOTS * PART * (CHUNKS + 7 * swaps + (CHUNKS - swaps) + CHUNKS + 3 * CHUNKS)
    drain(few, note_sem.at[0])
    drain(most, note_sem.at[2])
    drain_rows(ring_rows, sent_sem.at[0])
    drain_rows(other_rows, sent_sem.at[1])


def run_main(lists, orbitals, occ, vir, held):
    smem = pl.BlockSpec(memory_space=pltpu.SMEM)
    vmem = pl.BlockSpec(memory_space=pltpu.VMEM)
    hbm = pl.BlockSpec(memory_space=pl.ANY)
    dma = pltpu.SemaphoreType.DMA
    chunk = pltpu.VMEM((GROUPS, PART, AUX), F32)
    return pl.pallas_call(
        main_kernel,
        out_shape=pltpu.VMEM((OWN, WIDTH, AUX), F32),
        in_specs=[smem, smem, smem, vmem, hbm],
        out_specs=vmem,
        scratch_shapes=[
            pltpu.VMEM((1, LANES), jnp.int32),
            pltpu.VMEM((GROUPS, 1, LANES), jnp.int32),
            pltpu.VMEM((1, LANES), F32),
            pltpu.VMEM((BLOCKS, 1, LANES), F32),
            pltpu.SMEM((GROUPS, 1, LANES), jnp.int32),
            pltpu.VMEM((ALL, AUX), BF16),
            pltpu.VMEM((ALL, AUX), BF16),
            pltpu.VMEM((2 * OWN, WIDTH, AUX), F32),
            pltpu.VMEM((CALLS, STACK, AUX), F32),
            pltpu.VMEM((3 * STACK, AUX), BF16),
            pltpu.VMEM((ALL, 3 * STACK), BF16),
            pltpu.VMEM((CALLS, STACK, AUX), F32),
            pltpu.VMEM((CALLS, 3 * STEP_ROWS, AUX), F32),
            pltpu.VMEM((SLOTS * WIDTH, AUX), F32),
            pltpu.VMEM((SLOTS * WIDTH, AUX), F32),
            pltpu.VMEM((CHUNKS, SLOTS, PART, AUX), F32),
            pltpu.VMEM((ALL, 1), F32),
            pltpu.VMEM((4, 1, STACK), F32),
            pltpu.VMEM((CHUNKS, SLOTS, PART, AUX), F32),
            pltpu.VMEM((CHUNKS, SLOTS, PART, AUX), F32),
            pltpu.VMEM((len(SWAPPED), 4, SLOTS, PART, AUX), F32),
            pltpu.VMEM((CHUNKS, GROUPS, PART, AUX), F32),
            pltpu.SMEM((2, GROUPS), jnp.int32),
            dma((4,)),
            dma((2,)),
            dma((2,)),
            dma((2,)),
            dma((CHUNKS,)),
            dma((CHUNKS,)),
            dma((CHUNKS,)),
            dma((len(SWAPPED), 3)),
            dma((3, 2, CHUNKS)),
            dma((3, 2, CHUNKS)),
            dma((CHUNKS,)),
            dma((CHUNKS,)),
            dma((2,)),
            dma((CHUNKS,)),
            dma((CHUNKS,)),
            dma((len(SWAPPED), 4)),
            pltpu.SemaphoreType.REGULAR,
        ] + [chunk] * (2 * CHUNKS),
        compiler_params=pltpu.CompilerParams(
            collective_id=0, has_side_effects=True, vmem_limit_bytes=62_000_000),
        name="main",
    )(lists, orbitals, occ, vir, held)


def body(integrals, pair_lists, row_orbital, occ_energy, vir_energy):
    return run_main(pair_lists, row_orbital, occ_energy, vir_energy.reshape(1, WIDTH), integrals)


def solution(mesh):
    in_specs = (P("grp", "blk", None), P("grp", None), P("grp"), P(), P("blk"))
    out_specs = P("grp", "blk", None)
    return jax.shard_map(body, mesh=mesh, in_specs=in_specs, out_specs=out_specs, check_vma=False)
```

```python
import jax
import jax.numpy as jnp
from jax import lax
from jax.experimental import pallas as pl
from jax.experimental.pallas import tpu as pltpu
from jax.sharding import PartitionSpec as P

MESH = pl.DeviceIdType.MESH
F32 = jnp.float32
BF16 = jnp.bfloat16
GROUPS = 8
BLOCKS = 16
OWN = 12
SLOTS = 2
WIDTH = 64
AUX = 1536
HELD = OWN * WIDTH
ALL = 2 * HELD
CHUNKS = 8
SWAPPED = (3, 5)
HEAD = 8
STRAIGHT_IN = (0, 1)
STRAIGHT_OUT = (7,)
PART = WIDTH // CHUNKS
CALLS = 4
PIECE = WIDTH // CALLS
STEP_ROWS = 2 * SLOTS * PIECE
STACK = 4 * STEP_ROWS
TILE = 512
TILES = ALL // TILE
LANES = 128
NT = (((1,), (1,)), ((), ()))
TN = (((0,), (0,)), ((), ()))
OPENING = {
    0: [("fetch", 0), ("hop", 1, 0, 0), ("side", 0, 0), ("fetch", 1), ("hop", 3, 0, 0), ("fetch", 2),
        ("hop", 2, 0, 0), ("side", 0, 1), ("hop", 1, 1, 0), ("hop", 3, 1, 0), ("hop", 1, 0, 1), ("fetch", 3),
        ("hop", 3, 0, 1), ("pass", 2), ("hop", 1, 1, 1), ("hop", 3, 1, 1), ("hop", 2, 1, 0), ("fetch", 4),
        ("hop", 2, 0, 1), ("pass", 3), ("hop", 1, 0, 2), ("side", 0, 2), ("hop", 3, 0, 2), ("hop", 2, 1, 1)],
    1: [("hop", 3, 1, 4), ("pass", 6), ("side", 0, 5), ("sum", 3, 0), ("side", 2, 3)],
    4: [("ship", 2), ("cross", 4), ("sum", 3, 6), ("sum", 3, 7), ("ship", 5), ("ship", 4), ("home", 6),
        ("home", 7), ("cross", 6), ("cross", 7), ("ship", 7), ("ship", 6)],
}
BETWEEN = {
    (0, 0, 0): [("fetch", 5), ("pass", 4), ("hop", 1, 0, 3)],
    (0, 0, 1): [("hop", 2, 0, 2), ("side", 0, 3), ("hop", 3, 0, 3)],
    (0, 0, 2): [("fetch", 6), ("hop", 1, 1, 2)],
    (0, 1, 0): [("hop", 3, 1, 2), ("hop", 1, 0, 4)],
    (0, 1, 1): [("pass", 5), ("hop", 2, 0, 3), ("side", 0, 4), ("hop", 3, 0, 4)],
    (0, 1, 2): [("fetch", 7), ("hop", 2, 1, 2), ("side", 1, 3), ("sum", 2, 0)],
    (0, 2, 0): [("hop", 2, 0, 4), ("sum", 1, 0)],
    (0, 2, 1): [("side", 3, 3), ("hop", 1, 0, 5), ("hop", 3, 0, 5)],
    (0, 2, 2): [("hop", 1, 1, 4)],
    (1, 0, 0): [("sum", 2, 1)],
    (1, 0, 1): [("pass", 7), ("hop", 2, 1, 4), ("hop", 2, 0, 5)],
    (1, 0, 2): [("side", 1, 5), ("hop", 1, 0, 6), ("hop", 3, 0, 6)],
    (1, 1, 0): [("side", 3, 5), ("sum", 1, 1)],
    (1, 1, 1): [("side", 0, 6), ("home", 0)],
    (1, 1, 2): [("swap", 0, 3), ("swap", 1, 3), ("swap", 2, 3), ("side", 0, 7), ("hop", 1, 0, 7), ("swap", 3, 3)],
    (1, 2, 0): [("hop", 3, 0, 7)],
    (1, 2, 1): [("side", 2, 5), ("hop", 2, 0, 6)],
    (1, 2, 2): [("cross", 0), ("sum", 3, 1)],
    (2, 0, 0): [("hop", 1, 1, 6), ("hop", 3, 1, 6), ("sum", 2, 2)],
    (2, 0, 1): [("hop", 1, 1, 7), ("hop", 3, 1, 7)],
    (2, 0, 2): [("hop", 2, 0, 7), ("sum", 1, 2)],
    (2, 1, 0): [("home", 1)],
    (2, 1, 1): [("hop", 2, 1, 6), ("sum", 2, 3), ("sum", 1, 3)],
    (2, 1, 2): [("swap", 0, 5), ("swap", 1, 5), ("swap", 2, 5), ("swap", 3, 5), ("sum", 3, 2)],
    (2, 2, 0): [("hop", 2, 1, 7), ("ship", 0), ("cross", 1), ("sum", 2, 4)],
    (2, 2, 2): [("sum", 3, 3), ("sum", 1, 4)],
    (3, 0, 0): [("home", 2), ("sum", 1, 5)],
    (3, 0, 1): [("sum", 2, 5)],
    (3, 0, 2): [("home", 3), ("sum", 3, 4)],
    (3, 1, 2): [("ship", 1), ("cross", 2), ("sum", 3, 5), ("sum", 2, 6)],
    (3, 2, 0): [("home", 4), ("sum", 1, 6)],
    (3, 2, 1): [("ship", 3), ("sum", 2, 7)],
    (3, 2, 2): [("home", 5), ("sum", 1, 7)],
}


def split(values):
    high = values.astype(BF16)
    return high, (values - high.astype(F32)).astype(BF16)


def step_rows(step, slot, part, c):
    return pl.ds(step * STEP_ROWS + (slot * 2 + part) * PIECE + (c % 2) * PART, PART)


def main_kernel(
    lists_ref, orbitals_ref, occ_ref, vir_ref, held_ref,
    other,
    ints_mine, ints_all, vir_mine, vir_all, ints,
    high, low, total, stack, travel, amp, sums, landed,
    side_send, side_land, home, row_part, column_part,
    near_land, near_back, swapped, came, flags,
    note_sem, sent_sem, local_sem, swap_sem, box_sem, fetch_recv, side_recv, side_more,
    hop_recv, sum_recv, cross_recv, out_recv, own_sem, near_recv, far_recv, trade_recv, clear_sem,
    *chunks,
):
    group = lax.axis_index("grp")
    block = lax.axis_index("blk")
    column = group // 2
    upper_side = lax.rem(group, 2)
    opposite = group + 1 - 2 * upper_side
    facing = {"grp": opposite}
    core = lax.rem(block, 2)
    level = lax.rem(block // 2, 4)
    side = block // 8
    twin_block = block + 1 - 2 * core
    twin = {"blk": twin_block}
    across = {"blk": lax.rem(block + 8, 16)}
    ring = (
        {"blk": side * 8 + lax.rem(level + 1, 4) * 2 + core},
        {"blk": side * 8 + lax.rem(level + 3, 4) * 2 + core},
    )
    got, box = chunks[:CHUNKS], chunks[CHUNKS:]

    barrier = pltpu.get_barrier_semaphore()
    for step in range(1, GROUPS):
        pl.semaphore_signal(barrier, 1, device_id={"grp": lax.rem(group + step, GROUPS)}, device_id_type=MESH)
    for step in range(1, BLOCKS):
        pl.semaphore_signal(barrier, 1, device_id={"blk": lax.rem(block + step, BLOCKS)}, device_id_type=MESH)

    keep = pltpu.make_async_copy(held_ref, other, local_sem.at[0])
    keep.start()
    lane = lax.broadcasted_iota(jnp.int32, (1, LANES), 1)
    row = jnp.zeros((1, LANES), jnp.int32)
    for j in range(SLOTS):
        row = jnp.where(lane == j, lists_ref[0, j], row)
    for j in range(OWN):
        row = jnp.where(lane == SLOTS + j, orbitals_ref[j], row)
    ints_mine[...] = row
    ints_all[group] = row
    vir = vir_ref[...]
    vir_row = jnp.concatenate([vir, vir], axis=1)
    vir_mine[...] = vir_row
    vir_all[block] = vir_row
    pl.semaphore_wait(barrier, GROUPS + BLOCKS - 2)

    def remote(src, dst, send, recv, peer):
        return pltpu.make_async_remote_copy(src, dst, send, recv, device_id=peer, device_id_type=MESH)

    swap = remote(held_ref, total.at[pl.ds(OWN, OWN)], swap_sem.at[0], swap_sem.at[1], twin)

    def drain(like, sem):
        pltpu.make_async_copy(like, like, sem).wait()

    def drain_rows(count, sem):
        if count < WIDTH:
            drain(total.at[0, pl.ds(0, count)], sem)
        else:
            drain(total.at[pl.ds(0, count // WIDTH)], sem)

    def to_group(step, slot):
        return remote(ints_mine, ints_all.at[slot], note_sem.at[0], note_sem.at[1],
                      {"grp": lax.rem(group + step, GROUPS)})

    def to_block(step, slot):
        return remote(vir_mine, vir_all.at[slot], note_sem.at[2], note_sem.at[3],
                      {"blk": lax.rem(block + step, BLOCKS)})

    for step in range(1, GROUPS):
        to_group(step, group).start()
    for step in range(1, BLOCKS):
        to_block(step, block).start()
    swap.start()
    keep.wait()
    few, most = ints_all.at[pl.ds(0, GROUPS - 1)], vir_all.at[pl.ds(0, BLOCKS - 1)]
    drain(few, note_sem.at[1])
    to_scalar = pltpu.make_async_copy(ints_all, ints, local_sem.at[1])
    to_scalar.start()
    to_scalar.wait()

    def held_by(step, turn):
        return lax.rem(column + step, 4) * 2 + lax.rem(upper_side + turn, 2)

    for x in range(4):
        for turn in range(2):
            peer = x * 2 + lax.rem(upper_side + turn, 2)
            place = jnp.int32(0)
            found = jnp.int32(0)
            for slot in range(SLOTS):
                listed = ints[peer, 0, slot]
                match = listed // OWN == group
                place = jnp.where(match, listed % OWN, place)
                found = jnp.where(match, 1, found)
            flags[0, x * 2 + turn] = place
            flags[1, x * 2 + turn] = found

    def fetch(step, c, x):
        return remote(box[c].at[pl.ds(step * 2, 2)], got[c].at[pl.ds(x * 2, 2)],
                      box_sem.at[c], fetch_recv.at[c], {"grp": held_by(step, 0)})

    def fetch_straight(step, turn, c):
        return remote(box[c].at[step * 2 + turn], got[c].at[column * 2 + turn],
                      box_sem.at[c], fetch_recv.at[c], {"grp": held_by(step, turn)})

    others = [(step, turn) for step in range(4) for turn in range(2) if step or turn]

    def fill(c):
        for step in range(4):
            for turn in range(2):
                values = other[flags[0, lax.rem(column + step, 4) * 2 + turn], pl.ds(c * PART, PART), :]
                if step == 0 and not (turn and c in STRAIGHT_IN):
                    got[c][column * 2 + turn] = values
                else:
                    box[c][step * 2 + turn] = values

    fill(0)
    for c in range(CHUNKS):
        if c + 1 < CHUNKS:
            fill(c + 1)
        if c in STRAIGHT_IN:
            for step, turn in others:
                fetch_straight(step, turn, c).start()
            continue
        for step in range(1, 4):
            fetch(step, c, column).start()

    def prepare(source, first):
        def tile(index, carry):
            rows = pl.ds(pl.multiple_of((first + index) * WIDTH, WIDTH), WIDTH)
            upper, lower = split(source[index + (first if source is total else 0)])
            high[rows, :] = upper
            low[rows, :] = lower
            total[first + index] = jnp.zeros((WIDTH, AUX), F32)
            return carry
        lax.fori_loop(0, OWN, tile, 0)

    prepare(other, 0)
    pl.semaphore_signal(clear_sem, 1, device_id=twin, device_id_type=MESH)

    mine = [ints[group, 0, slot] for slot in range(SLOTS)]
    theirs = [ints[opposite, 0, slot] for slot in range(SLOTS)]
    one, none = jnp.float32(1), jnp.float32(0)
    sources = [jnp.minimum(row // OWN, GROUPS - 1) for row in mine]
    columns = [source // 2 for source in sources]
    their_columns = [jnp.minimum(row // OWN, GROUPS - 1) // 2 for row in theirs]
    level_with = [jnp.where((row < GROUPS * OWN) & (lax.rem(row // OWN, 2) == upper_side), one, none) for row in mine]
    opposed = [jnp.where((row < GROUPS * OWN) & (lax.rem(row // OWN, 2) != upper_side), one, none) for row in mine]
    partner_energy = [
        occ_ref[ints[sources[slot], 0, SLOTS + mine[slot] % OWN]] for slot in range(SLOTS)
    ]
    drain(most, note_sem.at[3])
    square = (lax.broadcasted_iota(jnp.int32, (WIDTH, WIDTH), 0)
              == lax.broadcasted_iota(jnp.int32, (WIDTH, WIDTH), 1))
    for owner, place in ((block, 0), (twin_block, 1)):
        line = vir_all[owner][:, :WIDTH]
        upright = jnp.sum(jnp.where(square, line, 0.0), axis=1, keepdims=True)
        for i in range(OWN):
            energy = occ_ref[ints[group, 0, SLOTS + i]]
            row_part[pl.ds((place * OWN + i) * WIDTH, WIDTH), :] = energy - upright
    lines = []
    for step in range(4):
        for slot in range(SLOTS):
            for part in range(2):
                from_level = lax.rem(level + (4 - step if slot == 0 else step), 4)
                from_side = side + part - 2 * part * side
                lines.append(partner_energy[slot] - vir_all[from_side * 8 + from_level * 2 + core])
    for call in range(CALLS):
        pieces = [line[:, call * PIECE:(call + 1) * PIECE] for line in lines]
        column_part[call] = jnp.concatenate(pieces, axis=1)

    def side_came(step, c):
        return side_more.at[SWAPPED.index(c), step - 1] if step else side_recv.at[c]

    def beside(step, slot, c):
        came = side_came(step, c)
        return remote(stack.at[c // 2, step_rows(step, slot, 0, c)], stack.at[c // 2, step_rows(step, slot, 1, c)],
                      sent_sem.at[1], came, across)

    def hop(step, slot, part, c):
        source = 1 if step == 2 else 0
        return remote(stack.at[c // 2, step_rows(source, slot, part, c)],
                      stack.at[c // 2, step_rows(step, slot, part, c)],
                      sent_sem.at[0], hop_recv.at[step - 1, part, c], ring[1 - slot if step == 3 else slot])

    def landing(step, slot, part, c):
        return landed.at[c // 2, step_rows(step - 1, slot, part, c)]

    def sum_hop(step, slot, part, c):
        return remote(sums.at[c // 2, step_rows(step, slot, part, c)], landing(step, slot, part, c),
                      sent_sem.at[0], sum_recv.at[step - 1, part, c], ring[1 - slot if step == 1 else slot])

    def traded(step, slot, c):
        return swapped.at[SWAPPED.index(c), step, slot]

    def trade(step, slot, c):
        place = SWAPPED.index(c)
        return remote(sums.at[c // 2, step_rows(step, slot, 1, c)], traded(step, slot, c),
                      sent_sem.at[1], trade_recv.at[place, step], across)

    def side_rows(slot, c):
        return pl.ds(slot * WIDTH + c * PART, PART)

    def cross(slot, c):
        rows = side_rows(slot, c)
        return remote(side_send.at[rows], side_land.at[rows], sent_sem.at[1], cross_recv.at[c], across)

    def pass_on(c):
        return remote(box[c].at[pl.ds(0, 2)], near_land.at[c], box_sem.at[c], near_recv.at[c], facing)

    def pass_back(c):
        return remote(home.at[c], near_back.at[c], sent_sem.at[1], far_recv.at[c], facing)

    def ship(step, c, x):
        return remote(box[c].at[pl.ds(step * 2, 2)], came.at[c, pl.ds(x * 2, 2)],
                      sent_sem.at[1], out_recv.at[c], {"grp": held_by(step, 0)})

    def on_fetch(c):
        if c in STRAIGHT_IN:
            drain_rows(7 * PART, fetch_recv.at[c])
            spread(c)
            return
        drain_rows(6 * PART, fetch_recv.at[c])
        for slot in range(SLOTS):
            box[c][slot] = got[c][their_columns[slot] * 2 + 1]
        pass_on(c).start()

    def on_pass(c):
        drain_rows(2 * PART, near_recv.at[c])
        spread(c)

    def spread(c):
        for slot in range(SLOTS):
            near = got[c][columns[slot] * 2] * level_with[slot]
            if c in STRAIGHT_IN:
                near += got[c][columns[slot] * 2 + 1] * opposed[slot]
            else:
                near += near_land[c, slot] * opposed[slot]
            stack[c // 2, step_rows(0, slot, 0, c), :] = near
        for slot in range(SLOTS):
            beside(0, slot, c).start()
            hop(1, slot, 0, c).start()
            hop(3, slot, 0, c).start()

    def on_side(step, c):
        drain_rows(2 * PART, side_came(step, c))
        if c not in SWAPPED:
            for slot in range(SLOTS):
                hop(1, slot, 1, c).start()
                hop(3, slot, 1, c).start()

    def on_hop(step, part, c):
        drain_rows(2 * PART, hop_recv.at[step - 1, part, c])
        for slot in range(SLOTS):
            if step == 1:
                hop(2, slot, part, c).start()
            if c in SWAPPED:
                beside(step, slot, c).start()

    def on_swap(step, c):
        for slot in range(SLOTS):
            trade(step, slot, c).start()

    def parts_of(c):
        return (0,) if c in SWAPPED else (1, 0)

    def on_sum(step, c):
        if c in SWAPPED:
            drain_rows(2 * PART, trade_recv.at[SWAPPED.index(c), step])
        for part in parts_of(c):
            if step == 3:
                drain_rows(2 * PART, sum_recv.at[1, part, c])
            for slot in range(SLOTS):
                rows = step_rows(step, slot, part, c)
                if c in SWAPPED:
                    sums[c // 2, rows, :] += traded(step, slot, c)[...]
                if step == 3:
                    sums[c // 2, rows, :] += landing(2, slot, part, c)[...]
        for part in parts_of(c):
            for slot in range(SLOTS):
                sum_hop(step, slot, part, c).start()

    def on_home(c):
        if c in SWAPPED:
            drain_rows(2 * PART, trade_recv.at[SWAPPED.index(c), 0])
        for part in parts_of(c):
            drain_rows(2 * PART, sum_recv.at[0, part, c])
            drain_rows(2 * PART, sum_recv.at[2, part, c])
            for slot in range(SLOTS):
                value = sums[c // 2, step_rows(0, slot, part, c), :] + landing(1, slot, part, c)[...]
                value += landing(3, slot, part, c)[...]
                if part:
                    side_send[side_rows(slot, c), :] = value
                    continue
                if c in SWAPPED:
                    value += traded(0, slot, c)[...]
                home[c, slot] = value
            if part:
                for slot in range(SLOTS):
                    cross(slot, c).start()
        if c in SWAPPED:
            pass_back(c).start()

    def on_cross(c):
        drain_rows(2 * PART, cross_recv.at[c])
        for slot in range(SLOTS):
            home[c, slot] += side_land[side_rows(slot, c), :]
        if c not in STRAIGHT_OUT:
            pass_back(c).start()

    def ship_straight(step, turn, c):
        return remote(box[c].at[step * 2 + turn], came.at[c, column * 2 + turn],
                      sent_sem.at[2], out_recv.at[c], {"grp": held_by(step, turn)})

    def on_ship(c):
        drain_rows((7 if c in STRAIGHT_IN else 8) * PART, box_sem.at[c])

        def blend(rows, source, step, turn):
            picks = [jnp.where(row // OWN == held_by(step, turn), one, none) for row in rows]
            return picks[0] * source[c, 0] + picks[1] * source[c, 1]

        def place(step, turn, values):
            if step or (turn and c in STRAIGHT_OUT):
                box[c][step * 2 + turn] = values
            else:
                came[c, column * 2 + turn] = values

        if c in STRAIGHT_OUT:
            for step in range(4):
                for turn in range(2):
                    place(step, turn, blend(mine, home, step, turn))
            for step, turn in others:
                ship_straight(step, turn, c).start()
            return
        for step in range(4):
            place(step, 0, blend(mine, home, step, 0))
        drain_rows(2 * PART, far_recv.at[c])
        for step in range(4):
            place(step, 1, blend(theirs, near_back, step, 0))
        for step in range(1, 4):
            ship(step, c, column).start()

    def finish(c):
        drain_rows((7 if c in STRAIGHT_OUT else 6) * PART, out_recv.at[c])
        rows = pl.ds(c * PART, PART)

        def add(index, carry):
            value = total[index, rows, :] + other[index, rows, :]
            for peer in range(GROUPS):
                here = (flags[0, peer] == index) & (flags[1, peer] > 0)
                value += jnp.where(here, one, none) * came[c, peer]
            other[index, rows, :] = value
            return carry

        lax.fori_loop(0, OWN, add, 0)

    act = {"fetch": on_fetch, "pass": on_pass, "side": on_side, "hop": on_hop, "swap": on_swap,
           "sum": on_sum, "home": on_home, "cross": on_cross, "ship": on_ship}

    def play(actions):
        for name, *where in actions:
            act[name](*where)

    play(OPENING[0][:HEAD])
    swap.wait()
    prepare(total, OWN)
    play(OPENING[0][HEAD:])

    def run(call, loop, index):
        for (at_call, at_loop, at_index), actions in BETWEEN.items():
            if at_loop != loop:
                continue

            @pl.when((call == at_call) & (index == at_index))
            def _():
                play(actions)

    def one_call(call, carry):
        for at_call in range(1, CALLS):
            if OPENING.get(at_call):
                @pl.when(call == at_call)
                def _():
                    play(OPENING[at_call])

        def cut(index, carry):
            start = index * 64
            rows = pl.ds(pl.multiple_of(start, 64), 64)
            upper, lower = split(stack[call, rows, :])
            travel[rows, :] = upper
            travel[pl.ds(pl.multiple_of(STACK + start, 64), 64), :] = lower
            travel[pl.ds(pl.multiple_of(2 * STACK + start, 64), 64), :] = upper
            sums[call, rows, :] = jnp.zeros((64, AUX), F32)
            return carry

        lax.fori_loop(0, STACK // 64, cut, 0)

        def pair_tile(index, carry):
            rows = pl.ds(pl.multiple_of(index * TILE, TILE), TILE)
            upper = high[rows, :]
            near = travel[pl.ds(0, STACK), :]
            pair = lax.dot_general(upper, near, NT, preferred_element_type=F32)
            pair += lax.dot_general(upper, travel[pl.ds(STACK, STACK), :], NT, preferred_element_type=F32)
            pair += lax.dot_general(low[rows, :], near, NT, preferred_element_type=F32)
            big, small = split(pair / (row_part[rows, :] + column_part[call]))
            amp[rows, pl.ds(0, STACK)] = big
            amp[rows, pl.ds(STACK, STACK)] = big
            amp[rows, pl.ds(2 * STACK, STACK)] = small
            run(call, 0, index)
            return carry

        lax.fori_loop(0, TILES, pair_tile, 0)

        def back_tile(index, carry):
            rows = pl.ds(pl.multiple_of(index * TILE, TILE), TILE)
            upper = high[rows, :]
            big = amp[rows, pl.ds(0, STACK)]
            back = lax.dot_general(big, upper, TN, preferred_element_type=F32)
            back += lax.dot_general(big, low[rows, :], TN, preferred_element_type=F32)
            back += lax.dot_general(amp[rows, pl.ds(2 * STACK, STACK)], upper, TN, preferred_element_type=F32)
            sums[call] += back
            run(call, 1, index)
            return carry

        lax.fori_loop(0, TILES, back_tile, 0)

        def own_tile(index, carry):
            rows = pl.ds(pl.multiple_of(index * TILE, TILE), TILE)
            held = pl.ds(index * (TILE // WIDTH), TILE // WIDTH)
            forward = jnp.dot(amp[rows, :], travel[...], preferred_element_type=F32)
            total[held] += forward.reshape(TILE // WIDTH, WIDTH, AUX)
            run(call, 2, index)
            return carry

        lax.fori_loop(0, TILES, own_tile, 0)
        return carry

    lax.fori_loop(0, CALLS, one_call, 0)

    give = remote(total.at[pl.ds(OWN, OWN)], other, own_sem.at[0], own_sem.at[1], twin)
    pl.semaphore_wait(clear_sem, 1)
    give.start()
    play(OPENING[4])
    give.wait()

    order = [place for name, place in [event[:2] for event in OPENING[4]] if name == "ship"]
    order = [c for c in range(CHUNKS) if c not in order] + order
    for c in order:
        finish(c)
    swaps = len(SWAPPED)
    ring_rows = 2 * 3 * SLOTS * PART * (2 * CHUNKS - swaps)
    other_rows = SLOTS * PART * (
        CHUNKS + 7 * swaps + (CHUNKS - swaps) + 4 * (CHUNKS - len(STRAIGHT_OUT)))
    drain(few, note_sem.at[0])
    drain(most, note_sem.at[2])
    drain_rows(ring_rows, sent_sem.at[0])
    drain_rows(other_rows, sent_sem.at[1])
    drain(total.at[pl.ds(0, 7 * len(STRAIGHT_OUT)), pl.ds(0, PART)], sent_sem.at[2])


def run_main(lists, orbitals, occ, vir, held):
    smem = pl.BlockSpec(memory_space=pltpu.SMEM)
    vmem = pl.BlockSpec(memory_space=pltpu.VMEM)
    hbm = pl.BlockSpec(memory_space=pl.ANY)
    dma = pltpu.SemaphoreType.DMA
    chunk = pltpu.VMEM((GROUPS, PART, AUX), F32)
    return pl.pallas_call(
        main_kernel,
        out_shape=pltpu.VMEM((OWN, WIDTH, AUX), F32),
        in_specs=[smem, smem, smem, vmem, hbm],
        out_specs=vmem,
        scratch_shapes=[
            pltpu.VMEM((1, LANES), jnp.int32),
            pltpu.VMEM((GROUPS, 1, LANES), jnp.int32),
            pltpu.VMEM((1, LANES), F32),
            pltpu.VMEM((BLOCKS, 1, LANES), F32),
            pltpu.SMEM((GROUPS, 1, LANES), jnp.int32),
            pltpu.VMEM((ALL, AUX), BF16),
            pltpu.VMEM((ALL, AUX), BF16),
            pltpu.VMEM((2 * OWN, WIDTH, AUX), F32),
            pltpu.VMEM((CALLS, STACK, AUX), F32),
            pltpu.VMEM((3 * STACK, AUX), BF16),
            pltpu.VMEM((ALL, 3 * STACK), BF16),
            pltpu.VMEM((CALLS, STACK, AUX), F32),
            pltpu.VMEM((CALLS, 3 * STEP_ROWS, AUX), F32),
            pltpu.VMEM((SLOTS * WIDTH, AUX), F32),
            pltpu.VMEM((SLOTS * WIDTH, AUX), F32),
            pltpu.VMEM((CHUNKS, SLOTS, PART, AUX), F32),
            pltpu.VMEM((ALL, 1), F32),
            pltpu.VMEM((4, 1, STACK), F32),
            pltpu.VMEM((CHUNKS, SLOTS, PART, AUX), F32),
            pltpu.VMEM((CHUNKS, SLOTS, PART, AUX), F32),
            pltpu.VMEM((len(SWAPPED), 4, SLOTS, PART, AUX), F32),
            pltpu.VMEM((CHUNKS, GROUPS, PART, AUX), F32),
            pltpu.SMEM((2, GROUPS), jnp.int32),
            dma((4,)),
            dma((3,)),
            dma((2,)),
            dma((2,)),
            dma((CHUNKS,)),
            dma((CHUNKS,)),
            dma((CHUNKS,)),
            dma((len(SWAPPED), 3)),
            dma((3, 2, CHUNKS)),
            dma((3, 2, CHUNKS)),
            dma((CHUNKS,)),
            dma((CHUNKS,)),
            dma((2,)),
            dma((CHUNKS,)),
            dma((CHUNKS,)),
            dma((len(SWAPPED), 4)),
            pltpu.SemaphoreType.REGULAR,
        ] + [chunk] * (2 * CHUNKS),
        compiler_params=pltpu.CompilerParams(
            collective_id=0, has_side_effects=True, vmem_limit_bytes=62_000_000),
        name="main",
    )(lists, orbitals, occ, vir, held)


def body(integrals, pair_lists, row_orbital, occ_energy, vir_energy):
    return run_main(pair_lists, row_orbital, occ_energy, vir_energy.reshape(1, WIDTH), integrals)


def solution(mesh):
    in_specs = (P("grp", "blk", None), P("grp", None), P("grp"), P(), P("blk"))
    out_specs = P("grp", "blk", None)
    return jax.shard_map(body, mesh=mesh, in_specs=in_specs, out_specs=out_specs, check_vma=False)
```

```python
import jax
import jax.numpy as jnp
from jax import lax
from jax.experimental import pallas as pl
from jax.experimental.pallas import tpu as pltpu
from jax.sharding import PartitionSpec as P

MESH = pl.DeviceIdType.MESH
F32 = jnp.float32
BF16 = jnp.bfloat16
GROUPS = 8
BLOCKS = 16
OWN = 12
SLOTS = 2
WIDTH = 64
AUX = 1536
HELD = OWN * WIDTH
ALL = 2 * HELD
CHUNKS = 8
SWAPPED = (3, 5)
HEAD = 8
STRAIGHT_IN = (0, 1)
STRAIGHT_OUT = (7,)
PART = WIDTH // CHUNKS
CALLS = 4
PIECE = WIDTH // CALLS
STEP_ROWS = 2 * SLOTS * PIECE
STACK = 4 * STEP_ROWS
TILE = 512
TILES = ALL // TILE
LANES = 128
NT = (((1,), (1,)), ((), ()))
TN = (((0,), (0,)), ((), ()))
OPENING = {
    0: [("fetch", 0), ("hop", 1, 0, 0), ("side", 0, 0), ("fetch", 1), ("hop", 3, 0, 0), ("fetch", 2),
        ("hop", 2, 0, 0), ("side", 0, 1), ("hop", 1, 1, 0), ("hop", 3, 1, 0), ("hop", 1, 0, 1), ("fetch", 3),
        ("hop", 3, 0, 1), ("pass", 2), ("hop", 1, 1, 1), ("hop", 3, 1, 1), ("hop", 2, 1, 0), ("fetch", 4),
        ("hop", 2, 0, 1), ("pass", 3), ("hop", 1, 0, 2), ("side", 0, 2), ("hop", 3, 0, 2), ("hop", 2, 1, 1)],
    1: [("hop", 3, 1, 4), ("pass", 6), ("side", 0, 5), ("sum", 3, 0), ("side", 2, 3)],
    4: [("ship", 2), ("cross", 4), ("sum", 3, 6), ("sum", 3, 7), ("ship", 5), ("home", 6), ("home", 7),
        ("ship", 4), ("cross", 6), ("cross", 7), ("ship", 7), ("ship", 6)],
}
BETWEEN = {
    (0, 0, 0): [("fetch", 5), ("pass", 4), ("hop", 1, 0, 3)],
    (0, 0, 1): [("hop", 2, 0, 2), ("side", 0, 3), ("hop", 3, 0, 3)],
    (0, 0, 2): [("fetch", 6), ("hop", 1, 1, 2)],
    (0, 1, 0): [("hop", 3, 1, 2), ("hop", 1, 0, 4)],
    (0, 1, 1): [("pass", 5), ("hop", 2, 0, 3), ("side", 0, 4), ("hop", 3, 0, 4)],
    (0, 1, 2): [("fetch", 7), ("hop", 2, 1, 2), ("side", 1, 3), ("sum", 2, 0)],
    (0, 2, 0): [("hop", 2, 0, 4), ("sum", 1, 0)],
    (0, 2, 1): [("side", 3, 3), ("hop", 1, 0, 5), ("hop", 3, 0, 5)],
    (0, 2, 2): [("hop", 1, 1, 4)],
    (1, 0, 0): [("sum", 2, 1)],
    (1, 0, 1): [("pass", 7), ("hop", 2, 1, 4), ("hop", 2, 0, 5)],
    (1, 0, 2): [("side", 1, 5), ("hop", 1, 0, 6), ("hop", 3, 0, 6)],
    (1, 1, 0): [("side", 3, 5), ("sum", 1, 1)],
    (1, 1, 1): [("side", 0, 6), ("home", 0)],
    (1, 1, 2): [("swap", 0, 3), ("swap", 1, 3), ("swap", 2, 3), ("side", 0, 7), ("hop", 1, 0, 7), ("swap", 3, 3)],
    (1, 2, 0): [("hop", 3, 0, 7)],
    (1, 2, 1): [("side", 2, 5), ("hop", 2, 0, 6)],
    (1, 2, 2): [("cross", 0), ("sum", 3, 1)],
    (2, 0, 0): [("hop", 1, 1, 6), ("hop", 3, 1, 6), ("sum", 2, 2)],
    (2, 0, 1): [("hop", 1, 1, 7), ("hop", 3, 1, 7)],
    (2, 0, 2): [("hop", 2, 0, 7), ("sum", 1, 2)],
    (2, 1, 0): [("home", 1)],
    (2, 1, 1): [("hop", 2, 1, 6), ("sum", 2, 3), ("sum", 1, 3)],
    (2, 1, 2): [("swap", 0, 5), ("swap", 1, 5), ("swap", 2, 5), ("swap", 3, 5), ("sum", 3, 2)],
    (2, 2, 0): [("hop", 2, 1, 7), ("ship", 0), ("cross", 1), ("sum", 2, 4)],
    (2, 2, 2): [("sum", 3, 3), ("sum", 1, 4)],
    (3, 0, 0): [("home", 2), ("sum", 1, 5)],
    (3, 0, 1): [("sum", 2, 5)],
    (3, 0, 2): [("home", 3), ("sum", 3, 4)],
    (3, 1, 2): [("ship", 1), ("cross", 2), ("sum", 3, 5), ("sum", 2, 6)],
    (3, 2, 0): [("home", 4), ("sum", 1, 6)],
    (3, 2, 1): [("ship", 3), ("sum", 2, 7)],
    (3, 2, 2): [("home", 5), ("sum", 1, 7)],
}


def split(values):
    high = values.astype(BF16)
    return high, (values - high.astype(F32)).astype(BF16)


def step_rows(step, slot, part, c):
    return pl.ds(step * STEP_ROWS + (slot * 2 + part) * PIECE + (c % 2) * PART, PART)


def main_kernel(
    lists_ref, orbitals_ref, occ_ref, vir_ref, held_ref,
    other,
    ints_mine, ints_all, vir_mine, vir_all, ints,
    high, low, total, stack, travel, amp, sums, landed,
    side_send, side_land, home, row_part, column_part,
    near_land, near_back, swapped, came, flags,
    note_sem, sent_sem, local_sem, swap_sem, box_sem, fetch_recv, side_recv, side_more,
    hop_recv, sum_recv, cross_recv, out_recv, own_sem, near_recv, far_recv, trade_recv, clear_sem,
    *chunks,
):
    group = lax.axis_index("grp")
    block = lax.axis_index("blk")
    column = group // 2
    upper_side = lax.rem(group, 2)
    opposite = group + 1 - 2 * upper_side
    facing = {"grp": opposite}
    core = lax.rem(block, 2)
    level = lax.rem(block // 2, 4)
    side = block // 8
    twin_block = block + 1 - 2 * core
    twin = {"blk": twin_block}
    across = {"blk": lax.rem(block + 8, 16)}
    ring = (
        {"blk": side * 8 + lax.rem(level + 1, 4) * 2 + core},
        {"blk": side * 8 + lax.rem(level + 3, 4) * 2 + core},
    )
    got, box = chunks[:CHUNKS], chunks[CHUNKS:]

    barrier = pltpu.get_barrier_semaphore()
    for step in range(1, GROUPS):
        pl.semaphore_signal(barrier, 1, device_id={"grp": lax.rem(group + step, GROUPS)}, device_id_type=MESH)
    for step in range(1, BLOCKS):
        pl.semaphore_signal(barrier, 1, device_id={"blk": lax.rem(block + step, BLOCKS)}, device_id_type=MESH)

    keep = pltpu.make_async_copy(held_ref, other, local_sem.at[0])
    keep.start()
    lane = lax.broadcasted_iota(jnp.int32, (1, LANES), 1)
    row = jnp.zeros((1, LANES), jnp.int32)
    for j in range(SLOTS):
        row = jnp.where(lane == j, lists_ref[0, j], row)
    for j in range(OWN):
        row = jnp.where(lane == SLOTS + j, orbitals_ref[j], row)
    ints_mine[...] = row
    ints_all[group] = row
    vir = vir_ref[...]
    vir_row = jnp.concatenate([vir, vir], axis=1)
    vir_mine[...] = vir_row
    vir_all[block] = vir_row
    pl.semaphore_wait(barrier, GROUPS + BLOCKS - 2)

    def remote(src, dst, send, recv, peer):
        return pltpu.make_async_remote_copy(src, dst, send, recv, device_id=peer, device_id_type=MESH)

    swap = remote(held_ref, total.at[pl.ds(OWN, OWN)], swap_sem.at[0], swap_sem.at[1], twin)

    def drain(like, sem):
        pltpu.make_async_copy(like, like, sem).wait()

    def drain_rows(count, sem):
        if count < WIDTH:
            drain(total.at[0, pl.ds(0, count)], sem)
        else:
            drain(total.at[pl.ds(0, count // WIDTH)], sem)

    def to_group(step, slot):
        return remote(ints_mine, ints_all.at[slot], note_sem.at[0], note_sem.at[1],
                      {"grp": lax.rem(group + step, GROUPS)})

    def to_block(step, slot):
        return remote(vir_mine, vir_all.at[slot], note_sem.at[2], note_sem.at[3],
                      {"blk": lax.rem(block + step, BLOCKS)})

    for step in range(1, GROUPS):
        to_group(step, group).start()
    for step in range(1, BLOCKS):
        to_block(step, block).start()
    swap.start()
    keep.wait()
    few, most = ints_all.at[pl.ds(0, GROUPS - 1)], vir_all.at[pl.ds(0, BLOCKS - 1)]
    drain(few, note_sem.at[1])
    to_scalar = pltpu.make_async_copy(ints_all, ints, local_sem.at[1])
    to_scalar.start()
    to_scalar.wait()

    def held_by(step, turn):
        return lax.rem(column + step, 4) * 2 + lax.rem(upper_side + turn, 2)

    for x in range(4):
        for turn in range(2):
            peer = x * 2 + lax.rem(upper_side + turn, 2)
            place = jnp.int32(0)
            found = jnp.int32(0)
            for slot in range(SLOTS):
                listed = ints[peer, 0, slot]
                match = listed // OWN == group
                place = jnp.where(match, listed % OWN, place)
                found = jnp.where(match, 1, found)
            flags[0, x * 2 + turn] = place
            flags[1, x * 2 + turn] = found

    def fetch(step, c, x):
        return remote(box[c].at[pl.ds(step * 2, 2)], got[c].at[pl.ds(x * 2, 2)],
                      box_sem.at[c], fetch_recv.at[c], {"grp": held_by(step, 0)})

    def fetch_straight(step, turn, c):
        return remote(box[c].at[step * 2 + turn], got[c].at[column * 2 + turn],
                      box_sem.at[c], fetch_recv.at[c], {"grp": held_by(step, turn)})

    others = [(step, turn) for step in range(4) for turn in range(2) if step or turn]

    def fill(c):
        for step in range(4):
            for turn in range(2):
                values = other[flags[0, lax.rem(column + step, 4) * 2 + turn], pl.ds(c * PART, PART), :]
                if step == 0 and not (turn and c in STRAIGHT_IN):
                    got[c][column * 2 + turn] = values
                else:
                    box[c][step * 2 + turn] = values

    fill(0)
    for c in range(CHUNKS):
        if c + 1 < CHUNKS:
            fill(c + 1)
        if c in STRAIGHT_IN:
            for step, turn in others:
                fetch_straight(step, turn, c).start()
            continue
        for step in range(1, 4):
            fetch(step, c, column).start()

    def prepare(source, first):
        def tile(index, carry):
            rows = pl.ds(pl.multiple_of((first + index) * WIDTH, WIDTH), WIDTH)
            upper, lower = split(source[index + (first if source is total else 0)])
            high[rows, :] = upper
            low[rows, :] = lower
            total[first + index] = jnp.zeros((WIDTH, AUX), F32)
            return carry
        lax.fori_loop(0, OWN, tile, 0)

    prepare(other, 0)
    pl.semaphore_signal(clear_sem, 1, device_id=twin, device_id_type=MESH)

    mine = [ints[group, 0, slot] for slot in range(SLOTS)]
    theirs = [ints[opposite, 0, slot] for slot in range(SLOTS)]
    one, none = jnp.float32(1), jnp.float32(0)
    sources = [jnp.minimum(row // OWN, GROUPS - 1) for row in mine]
    columns = [source // 2 for source in sources]
    their_columns = [jnp.minimum(row // OWN, GROUPS - 1) // 2 for row in theirs]
    level_with = [jnp.where((row < GROUPS * OWN) & (lax.rem(row // OWN, 2) == upper_side), one, none) for row in mine]
    opposed = [jnp.where((row < GROUPS * OWN) & (lax.rem(row // OWN, 2) != upper_side), one, none) for row in mine]
    partner_energy = [
        occ_ref[ints[sources[slot], 0, SLOTS + mine[slot] % OWN]] for slot in range(SLOTS)
    ]
    drain(most, note_sem.at[3])
    square = (lax.broadcasted_iota(jnp.int32, (WIDTH, WIDTH), 0)
              == lax.broadcasted_iota(jnp.int32, (WIDTH, WIDTH), 1))
    for owner, place in ((block, 0), (twin_block, 1)):
        line = vir_all[owner][:, :WIDTH]
        upright = jnp.sum(jnp.where(square, line, 0.0), axis=1, keepdims=True)
        for i in range(OWN):
            energy = occ_ref[ints[group, 0, SLOTS + i]]
            row_part[pl.ds((place * OWN + i) * WIDTH, WIDTH), :] = energy - upright
    lines = []
    for step in range(4):
        for slot in range(SLOTS):
            for part in range(2):
                from_level = lax.rem(level + (4 - step if slot == 0 else step), 4)
                from_side = side + part - 2 * part * side
                lines.append(partner_energy[slot] - vir_all[from_side * 8 + from_level * 2 + core])
    for call in range(CALLS):
        pieces = [line[:, call * PIECE:(call + 1) * PIECE] for line in lines]
        column_part[call] = jnp.concatenate(pieces, axis=1)

    def side_came(step, c):
        return side_more.at[SWAPPED.index(c), step - 1] if step else side_recv.at[c]

    def beside(step, slot, c):
        came = side_came(step, c)
        return remote(stack.at[c // 2, step_rows(step, slot, 0, c)], stack.at[c // 2, step_rows(step, slot, 1, c)],
                      sent_sem.at[1], came, across)

    def hop(step, slot, part, c):
        source = 1 if step == 2 else 0
        return remote(stack.at[c // 2, step_rows(source, slot, part, c)],
                      stack.at[c // 2, step_rows(step, slot, part, c)],
                      sent_sem.at[0], hop_recv.at[step - 1, part, c], ring[1 - slot if step == 3 else slot])

    def landing(step, slot, part, c):
        return landed.at[c // 2, step_rows(step - 1, slot, part, c)]

    def sum_hop(step, slot, part, c):
        return remote(sums.at[c // 2, step_rows(step, slot, part, c)], landing(step, slot, part, c),
                      sent_sem.at[0], sum_recv.at[step - 1, part, c], ring[1 - slot if step == 1 else slot])

    def traded(step, slot, c):
        return swapped.at[SWAPPED.index(c), step, slot]

    def trade(step, slot, c):
        place = SWAPPED.index(c)
        return remote(sums.at[c // 2, step_rows(step, slot, 1, c)], traded(step, slot, c),
                      sent_sem.at[1], trade_recv.at[place, step], across)

    def side_rows(slot, c):
        return pl.ds(slot * WIDTH + c * PART, PART)

    def cross(slot, c):
        rows = side_rows(slot, c)
        return remote(side_send.at[rows], side_land.at[rows], sent_sem.at[1], cross_recv.at[c], across)

    def pass_on(c):
        return remote(box[c].at[pl.ds(0, 2)], near_land.at[c], box_sem.at[c], near_recv.at[c], facing)

    def pass_back(c):
        return remote(home.at[c], near_back.at[c], sent_sem.at[1], far_recv.at[c], facing)

    def ship(step, c, x):
        return remote(box[c].at[pl.ds(step * 2, 2)], came.at[c, pl.ds(x * 2, 2)],
                      sent_sem.at[1], out_recv.at[c], {"grp": held_by(step, 0)})

    def on_fetch(c):
        if c in STRAIGHT_IN:
            drain_rows(7 * PART, fetch_recv.at[c])
            spread(c)
            return
        drain_rows(6 * PART, fetch_recv.at[c])
        for slot in range(SLOTS):
            box[c][slot] = got[c][their_columns[slot] * 2 + 1]
        pass_on(c).start()

    def on_pass(c):
        drain_rows(2 * PART, near_recv.at[c])
        spread(c)

    def spread(c):
        for slot in range(SLOTS):
            near = got[c][columns[slot] * 2] * level_with[slot]
            if c in STRAIGHT_IN:
                near += got[c][columns[slot] * 2 + 1] * opposed[slot]
            else:
                near += near_land[c, slot] * opposed[slot]
            stack[c // 2, step_rows(0, slot, 0, c), :] = near
        for slot in range(SLOTS):
            beside(0, slot, c).start()
            hop(1, slot, 0, c).start()
            hop(3, slot, 0, c).start()

    def on_side(step, c):
        drain_rows(2 * PART, side_came(step, c))
        if c not in SWAPPED:
            for slot in range(SLOTS):
                hop(1, slot, 1, c).start()
                hop(3, slot, 1, c).start()

    def on_hop(step, part, c):
        drain_rows(2 * PART, hop_recv.at[step - 1, part, c])
        for slot in range(SLOTS):
            if step == 1:
                hop(2, slot, part, c).start()
            if c in SWAPPED:
                beside(step, slot, c).start()

    def on_swap(step, c):
        for slot in range(SLOTS):
            trade(step, slot, c).start()

    def parts_of(c):
        return (0,) if c in SWAPPED else (1, 0)

    def on_sum(step, c):
        if c in SWAPPED:
            drain_rows(2 * PART, trade_recv.at[SWAPPED.index(c), step])
        for part in parts_of(c):
            if step == 3:
                drain_rows(2 * PART, sum_recv.at[1, part, c])
            for slot in range(SLOTS):
                rows = step_rows(step, slot, part, c)
                if c in SWAPPED:
                    sums[c // 2, rows, :] += traded(step, slot, c)[...]
                if step == 3:
                    sums[c // 2, rows, :] += landing(2, slot, part, c)[...]
        for part in parts_of(c):
            for slot in range(SLOTS):
                sum_hop(step, slot, part, c).start()

    def on_home(c):
        if c in SWAPPED:
            drain_rows(2 * PART, trade_recv.at[SWAPPED.index(c), 0])
        for part in parts_of(c):
            drain_rows(2 * PART, sum_recv.at[0, part, c])
            drain_rows(2 * PART, sum_recv.at[2, part, c])
            for slot in range(SLOTS):
                value = sums[c // 2, step_rows(0, slot, part, c), :] + landing(1, slot, part, c)[...]
                value += landing(3, slot, part, c)[...]
                if part:
                    side_send[side_rows(slot, c), :] = value
                    continue
                if c in SWAPPED:
                    value += traded(0, slot, c)[...]
                home[c, slot] = value
            if part:
                for slot in range(SLOTS):
                    cross(slot, c).start()
        if c in SWAPPED:
            pass_back(c).start()

    def on_cross(c):
        drain_rows(2 * PART, cross_recv.at[c])
        for slot in range(SLOTS):
            home[c, slot] += side_land[side_rows(slot, c), :]
        if c not in STRAIGHT_OUT:
            pass_back(c).start()

    def ship_straight(step, turn, c):
        return remote(box[c].at[step * 2 + turn], came.at[c, column * 2 + turn],
                      sent_sem.at[2], out_recv.at[c], {"grp": held_by(step, turn)})

    def on_ship(c):
        drain_rows((7 if c in STRAIGHT_IN else 8) * PART, box_sem.at[c])

        def blend(rows, source, step, turn):
            picks = [jnp.where(row // OWN == held_by(step, turn), one, none) for row in rows]
            return picks[0] * source[c, 0] + picks[1] * source[c, 1]

        def place(step, turn, values):
            if step or (turn and c in STRAIGHT_OUT):
                box[c][step * 2 + turn] = values
            else:
                came[c, column * 2 + turn] = values

        if c in STRAIGHT_OUT:
            for step in range(4):
                for turn in range(2):
                    place(step, turn, blend(mine, home, step, turn))
            for step, turn in others:
                ship_straight(step, turn, c).start()
            return
        for step in range(4):
            place(step, 0, blend(mine, home, step, 0))
        drain_rows(2 * PART, far_recv.at[c])
        for step in range(4):
            place(step, 1, blend(theirs, near_back, step, 0))
        for step in range(1, 4):
            ship(step, c, column).start()

    def finish(c):
        drain_rows((7 if c in STRAIGHT_OUT else 6) * PART, out_recv.at[c])
        rows = pl.ds(c * PART, PART)

        def add(index, carry):
            value = total[index, rows, :] + other[index, rows, :]
            for peer in range(GROUPS):
                here = (flags[0, peer] == index) & (flags[1, peer] > 0)
                value += jnp.where(here, one, none) * came[c, peer]
            other[index, rows, :] = value
            return carry

        lax.fori_loop(0, OWN, add, 0)

    act = {"fetch": on_fetch, "pass": on_pass, "side": on_side, "hop": on_hop, "swap": on_swap,
           "sum": on_sum, "home": on_home, "cross": on_cross, "ship": on_ship}

    def play(actions):
        for name, *where in actions:
            act[name](*where)

    play(OPENING[0][:HEAD])
    swap.wait()
    prepare(total, OWN)
    play(OPENING[0][HEAD:])

    def run(call, loop, index):
        for (at_call, at_loop, at_index), actions in BETWEEN.items():
            if at_loop != loop:
                continue

            @pl.when((call == at_call) & (index == at_index))
            def _():
                play(actions)

    def one_call(call, carry):
        for at_call in range(1, CALLS):
            if OPENING.get(at_call):
                @pl.when(call == at_call)
                def _():
                    play(OPENING[at_call])

        def cut(index, carry):
            start = index * 64
            rows = pl.ds(pl.multiple_of(start, 64), 64)
            upper, lower = split(stack[call, rows, :])
            travel[rows, :] = upper
            travel[pl.ds(pl.multiple_of(STACK + start, 64), 64), :] = lower
            travel[pl.ds(pl.multiple_of(2 * STACK + start, 64), 64), :] = upper
            sums[call, rows, :] = jnp.zeros((64, AUX), F32)
            return carry

        lax.fori_loop(0, STACK // 64, cut, 0)

        def pair_tile(index, carry):
            rows = pl.ds(pl.multiple_of(index * TILE, TILE), TILE)
            upper = high[rows, :]
            near = travel[pl.ds(0, STACK), :]
            pair = lax.dot_general(upper, near, NT, preferred_element_type=F32)
            pair += lax.dot_general(upper, travel[pl.ds(STACK, STACK), :], NT, preferred_element_type=F32)
            pair += lax.dot_general(low[rows, :], near, NT, preferred_element_type=F32)
            big, small = split(pair / (row_part[rows, :] + column_part[call]))
            amp[rows, pl.ds(0, STACK)] = big
            amp[rows, pl.ds(STACK, STACK)] = big
            amp[rows, pl.ds(2 * STACK, STACK)] = small
            run(call, 0, index)
            return carry

        lax.fori_loop(0, TILES, pair_tile, 0)

        def back_tile(index, carry):
            rows = pl.ds(pl.multiple_of(index * TILE, TILE), TILE)
            upper = high[rows, :]
            big = amp[rows, pl.ds(0, STACK)]
            back = lax.dot_general(big, upper, TN, preferred_element_type=F32)
            back += lax.dot_general(big, low[rows, :], TN, preferred_element_type=F32)
            back += lax.dot_general(amp[rows, pl.ds(2 * STACK, STACK)], upper, TN, preferred_element_type=F32)
            sums[call] += back
            run(call, 1, index)
            return carry

        lax.fori_loop(0, TILES, back_tile, 0)

        def own_tile(index, carry):
            rows = pl.ds(pl.multiple_of(index * TILE, TILE), TILE)
            held = pl.ds(index * (TILE // WIDTH), TILE // WIDTH)
            forward = jnp.dot(amp[rows, :], travel[...], preferred_element_type=F32)
            total[held] += forward.reshape(TILE // WIDTH, WIDTH, AUX)
            run(call, 2, index)
            return carry

        lax.fori_loop(0, TILES, own_tile, 0)
        return carry

    lax.fori_loop(0, CALLS, one_call, 0)

    give = remote(total.at[pl.ds(OWN, OWN)], other, own_sem.at[0], own_sem.at[1], twin)
    pl.semaphore_wait(clear_sem, 1)
    give.start()
    play(OPENING[4])
    give.wait()

    order = [place for name, place in [event[:2] for event in OPENING[4]] if name == "ship"]
    order = [c for c in range(CHUNKS) if c not in order] + order
    for c in order:
        finish(c)
    swaps = len(SWAPPED)
    ring_rows = 2 * 3 * SLOTS * PART * (2 * CHUNKS - swaps)
    other_rows = SLOTS * PART * (
        CHUNKS + 7 * swaps + (CHUNKS - swaps) + 4 * (CHUNKS - len(STRAIGHT_OUT)))
    drain(few, note_sem.at[0])
    drain(most, note_sem.at[2])
    drain_rows(ring_rows, sent_sem.at[0])
    drain_rows(other_rows, sent_sem.at[1])
    drain(total.at[pl.ds(0, 7 * len(STRAIGHT_OUT)), pl.ds(0, PART)], sent_sem.at[2])


def run_main(lists, orbitals, occ, vir, held):
    smem = pl.BlockSpec(memory_space=pltpu.SMEM)
    vmem = pl.BlockSpec(memory_space=pltpu.VMEM)
    hbm = pl.BlockSpec(memory_space=pl.ANY)
    dma = pltpu.SemaphoreType.DMA
    chunk = pltpu.VMEM((GROUPS, PART, AUX), F32)
    return pl.pallas_call(
        main_kernel,
        out_shape=pltpu.VMEM((OWN, WIDTH, AUX), F32),
        in_specs=[smem, smem, smem, vmem, hbm],
        out_specs=vmem,
        scratch_shapes=[
            pltpu.VMEM((1, LANES), jnp.int32),
            pltpu.VMEM((GROUPS, 1, LANES), jnp.int32),
            pltpu.VMEM((1, LANES), F32),
            pltpu.VMEM((BLOCKS, 1, LANES), F32),
            pltpu.SMEM((GROUPS, 1, LANES), jnp.int32),
            pltpu.VMEM((ALL, AUX), BF16),
            pltpu.VMEM((ALL, AUX), BF16),
            pltpu.VMEM((2 * OWN, WIDTH, AUX), F32),
            pltpu.VMEM((CALLS, STACK, AUX), F32),
            pltpu.VMEM((3 * STACK, AUX), BF16),
            pltpu.VMEM((ALL, 3 * STACK), BF16),
            pltpu.VMEM((CALLS, STACK, AUX), F32),
            pltpu.VMEM((CALLS, 3 * STEP_ROWS, AUX), F32),
            pltpu.VMEM((SLOTS * WIDTH, AUX), F32),
            pltpu.VMEM((SLOTS * WIDTH, AUX), F32),
            pltpu.VMEM((CHUNKS, SLOTS, PART, AUX), F32),
            pltpu.VMEM((ALL, 1), F32),
            pltpu.VMEM((4, 1, STACK), F32),
            pltpu.VMEM((CHUNKS, SLOTS, PART, AUX), F32),
            pltpu.VMEM((CHUNKS, SLOTS, PART, AUX), F32),
            pltpu.VMEM((len(SWAPPED), 4, SLOTS, PART, AUX), F32),
            pltpu.VMEM((CHUNKS, GROUPS, PART, AUX), F32),
            pltpu.SMEM((2, GROUPS), jnp.int32),
            dma((4,)),
            dma((3,)),
            dma((2,)),
            dma((2,)),
            dma((CHUNKS,)),
            dma((CHUNKS,)),
            dma((CHUNKS,)),
            dma((len(SWAPPED), 3)),
            dma((3, 2, CHUNKS)),
            dma((3, 2, CHUNKS)),
            dma((CHUNKS,)),
            dma((CHUNKS,)),
            dma((2,)),
            dma((CHUNKS,)),
            dma((CHUNKS,)),
            dma((len(SWAPPED), 4)),
            pltpu.SemaphoreType.REGULAR,
        ] + [chunk] * (2 * CHUNKS),
        compiler_params=pltpu.CompilerParams(
            collective_id=0, has_side_effects=True, vmem_limit_bytes=62_000_000),
        name="main",
    )(lists, orbitals, occ, vir, held)


def body(integrals, pair_lists, row_orbital, occ_energy, vir_energy):
    return run_main(pair_lists, row_orbital, occ_energy, vir_energy.reshape(1, WIDTH), integrals)


def solution(mesh):
    in_specs = (P("grp", "blk", None), P("grp", None), P("grp"), P(), P("blk"))
    out_specs = P("grp", "blk", None)
    return jax.shard_map(body, mesh=mesh, in_specs=in_specs, out_specs=out_specs, check_vma=False)
```
